256 devices in a mesh: mass: 32 (over x, z), sub: 8 (over y, core).
Axes of the slice: x: 4, y: 4, z: 8, core: 2. Of those that a mesh axis runs over, the one named last changes fastest.
Arguments:
- spectra: bfloat16 [32768, 4096], P(('mass', 'sub')), may hold values from -6 to 6
- w_in: bfloat16 [4096, 2048], P(None, 'sub'), may hold values from -0.09375 to 0.09375
- w_out: bfloat16 [2048, 512], P('sub'), may hold values from -0.125 to 0.125
- partner_rows: int32 [32, 8, 32, 8], P('mass', 'sub'), may hold values from 0 to 127
- pair_counts: int32 [32, 8, 32], P('mass', 'sub'), may hold values from 0 to 8, as said below
- pair_labels: int32 [32, 8, 32, 8], P('mass', 'sub'), may hold values from 0 to 1, as said below
Outputs:
- grad_in: float32 [4096, 2048], P('mass', 'sub')
- grad_out_t: float32 [512, 2048], P('mass', 'sub')
The draws below stay inside these ranges and needn't reach their ends.
Inputs may be any that keep to these rules, and one draw needn't show every extreme that they name: pair_counts[m, s, q] equals pair_counts[q, s, m], is 0 for q = m, and at most 8; some count equals 8. pair_labels[m, s, q, c] equals pair_labels[q, s, m, c] for q != m.
All inputs are finite; a program needn't handle non-finite values.
Results may differ from the reference program's by a relative error of at most 0.0053.
Values may be sent and summed in bfloat16 or wider, within the bound.
A program may use at most 64 MiB of HBM per device.

```python
import jax
import jax.numpy as jnp
from jax import lax

BINS = 4096
HID = 2048
EMB = 512
SPEC_DEV = 128
CAP = 8
SPECTRA = 32768
N_MASS = 32
N_SUB = 8


def mirrored(base, extra_dims):
    left = jnp.arange(N_MASS, dtype=jnp.int32)
    upper = left[:, None] < left[None, :]
    upper = upper.reshape((N_MASS, 1, N_MASS) + (1,) * extra_dims)
    return jnp.where(upper, base, jnp.swapaxes(base, 0, 2))


def draw_pair_counts(key, part):
    key_busy, key_low, key_extra = jax.random.split(jax.random.fold_in(key, 11), 3)
    busy = (jax.random.randint(key_busy, (N_MASS,), 0, 4) == 0).astype(jnp.int32)
    level = busy[:, None] + busy[None, :]
    low = jax.random.randint(key_low, (N_MASS, N_SUB, N_MASS), 0, CAP // 2 + 1)
    extra = jax.random.randint(key_extra, (N_MASS, N_SUB, N_MASS), CAP // 4, CAP // 2 + 1)
    base = jnp.minimum(CAP, low + level[:, None, :] * extra)
    both = mirrored(base, 0)
    left = jnp.arange(N_MASS, dtype=jnp.int32)
    same = (left[:, None] == left[None, :])[:, None, :]
    both = jnp.where(same, 0, both)
    both = both.at[0, :, 1].set(CAP)
    both = both.at[1, :, 0].set(CAP)
    return both.astype(jnp.int32)


def draw_pair_labels(key, part):
    base = jax.random.randint(jax.random.fold_in(key, 23), (N_MASS, N_SUB, N_MASS, CAP), 0, 2)
    return mirrored(base, 1).astype(jnp.int32)


def place_ends(drawn, stream_key, least, largest):
    longest = drawn.shape.index(max(drawn.shape))
    spots = []
    for shift in (0, 1):
        where = [jax.random.randint(jax.random.fold_in(stream_key, axis), (), 0, length) for axis, length in enumerate(drawn.shape)]
        where[longest] = (where[longest] + shift) % drawn.shape[longest]
        spots.append(tuple(where))
    return drawn.at[spots[0]].set(least).at[spots[1]].set(largest)


def steps_of(own_key, shape, cuts, smallest, top_value):
    loudness = 1.0
    for position, parts in cuts:
        heights = jax.random.uniform(jax.random.fold_in(jax.random.fold_in(own_key, 6), position), (parts,), jnp.float32, smallest / len(cuts), top_value / len(cuts))
        loudness = loudness * jnp.repeat(jnp.exp(heights), shape[position] // parts).reshape((-1,) + (1,) * (len(shape) - 1 - position))
    return loudness


def noise(own_key, dims, width, most, shards=(), kind=jnp.bfloat16):
    array = jax.random.normal(own_key, dims, jnp.float32) * width
    if len(shards) > 0:
        array = steps_of(own_key, dims, shards, -0.22, 0.18) * array
    return jnp.clip(array, min=-most, max=most).astype(kind)


def setup_inputs(seed: int = 0) -> dict:
    keys = jax.random.split(jax.random.key(seed), 7)
    return {
        "spectra": noise(keys[0], (SPECTRA, BINS), 1.0, 6.0, ((0, 256),)),
        "w_in": noise(keys[1], (BINS, HID), BINS ** -0.5, 0.09375, ((1, 8),)),
        "w_out": noise(keys[2], (HID, EMB), HID ** -0.5, 0.125, ((0, 8),)),
        "partner_rows": place_ends(jax.random.randint(keys[3], (N_MASS, N_SUB, N_MASS, CAP), 0, SPEC_DEV), jax.random.fold_in(keys[3], 1), 0, SPEC_DEV - 1).astype(jnp.int32),
        "pair_counts": draw_pair_counts(jax.random.fold_in(keys[6], 71), 0),
        "pair_labels": draw_pair_labels(jax.random.fold_in(keys[6], 71), 0),
    }


def reference(spectra, w_in, w_out, partner_rows, pair_counts, pair_labels):
    pre = jnp.dot(spectra, w_in, preferred_element_type=jnp.float32)
    hidden = jax.nn.silu(pre).astype(jnp.bfloat16)
    embed = jnp.dot(hidden, w_out, preferred_element_type=jnp.float32)
    norm = jnp.sqrt(lax.optimization_barrier(jnp.sum(embed * embed, axis=-1, keepdims=True)) + 1e-06)
    unit = embed / norm
    unit_b = unit.astype(jnp.bfloat16)
    cube = unit_b.reshape(N_MASS, N_SUB, SPEC_DEV, EMB)
    flat_rows = partner_rows.reshape(N_MASS, N_SUB, N_MASS * CAP, 1).astype(jnp.int32)
    mine = jnp.take_along_axis(cube, flat_rows, axis=2).reshape(N_MASS, N_SUB, N_MASS, CAP, EMB)
    theirs = jnp.swapaxes(mine, 0, 2)
    sim = lax.optimization_barrier(jnp.sum(mine.astype(jnp.float32) * theirs.astype(jnp.float32), axis=-1))
    valid = jnp.arange(CAP, dtype=jnp.int32)[None, None, None, :] < pair_counts[..., None]
    coef = jnp.where(valid, 2.0 * (sim - pair_labels.astype(jnp.float32)), jnp.float32(0.0))
    weighted = (coef[..., None] * theirs.astype(jnp.float32)).reshape(N_MASS, N_SUB, N_MASS * CAP, EMB)
    selector = (partner_rows.reshape(N_MASS, N_SUB, N_MASS * CAP, 1) == jnp.arange(SPEC_DEV, dtype=jnp.int32)[None, None, None, :]).astype(jnp.float32)
    grad_unit = jnp.einsum('abkr,abke->abre', selector, weighted, precision=lax.Precision.HIGHEST).reshape(SPECTRA, EMB)
    along = lax.optimization_barrier(jnp.sum(unit * grad_unit, axis=-1, keepdims=True))
    grad_embed = ((grad_unit - unit * along) / norm).astype(jnp.bfloat16)
    back = lax.dot_general(grad_embed, w_out, (((1,), (1,)), ((), ())), preferred_element_type=jnp.float32)
    gate = jax.nn.sigmoid(pre)
    grad_pre = (back * gate * (1.0 + pre * (1.0 - gate))).astype(jnp.bfloat16)
    grad_out_t = lax.dot_general(grad_embed, hidden, (((0,), (0,)), ((), ())), preferred_element_type=jnp.float32)
    grad_in = lax.dot_general(spectra, grad_pre, (((0,), (0,)), ((), ())), preferred_element_type=jnp.float32)
    return (grad_in, grad_out_t)
```

```python
import jax
import jax.numpy as jnp
from jax import lax
from jax.sharding import PartitionSpec as P


def per_device(spectra, w_in, w_out, partner_rows, pair_counts, pair_labels):
    own_rows = spectra.shape[0]
    peers = partner_rows.shape[2]
    slots = partner_rows.shape[3]
    shard_rows = lax.all_gather(spectra, "sub", axis=0, tiled=True)
    pre = jnp.dot(shard_rows, w_in, preferred_element_type=jnp.float32)
    hidden = jax.nn.silu(pre).astype(jnp.bfloat16)
    embed = lax.psum_scatter(
        jnp.dot(hidden, w_out, preferred_element_type=jnp.float32),
        "sub",
        scatter_dimension=0,
        tiled=True,
    )
    norm = jnp.sqrt(jnp.sum(embed * embed, axis=-1, keepdims=True) + 1e-06)
    unit = embed / norm
    unit_b = unit.astype(jnp.bfloat16)
    flat_rows = partner_rows.reshape(peers * slots)
    selector = flat_rows[:, None] == jnp.arange(own_rows, dtype=jnp.int32)[None, :]
    mine = jnp.dot(
        selector.astype(jnp.bfloat16), unit_b, preferred_element_type=jnp.float32
    ).astype(jnp.bfloat16)
    outgoing = mine.reshape(peers, slots, mine.shape[1])
    incoming = lax.all_to_all(outgoing, "mass", split_axis=0, concat_axis=0, tiled=True)
    theirs = incoming.astype(jnp.float32)
    sim = jnp.sum(outgoing.astype(jnp.float32) * theirs, axis=-1)
    valid = jnp.arange(slots, dtype=jnp.int32)[None, :] < pair_counts.reshape(peers)[:, None]
    labels = pair_labels.reshape(peers, slots).astype(jnp.float32)
    coef = jnp.where(valid, 2.0 * (sim - labels), jnp.float32(0.0))
    weighted = (coef[..., None] * theirs).reshape(peers * slots, theirs.shape[2])
    grad_unit = lax.dot_general(
        selector.astype(jnp.float32),
        weighted,
        (((0,), (0,)), ((), ())),
        precision=lax.Precision.HIGHEST,
    )
    along = jnp.sum(unit * grad_unit, axis=-1, keepdims=True)
    grad_embed = ((grad_unit - unit * along) / norm).astype(jnp.bfloat16)
    grad_rows = lax.all_gather(grad_embed, "sub", axis=0, tiled=True)
    back = lax.dot_general(
        grad_rows, w_out, (((1,), (1,)), ((), ())), preferred_element_type=jnp.float32
    )
    gate = jax.nn.sigmoid(pre)
    grad_pre = (back * gate * (1.0 + pre * (1.0 - gate))).astype(jnp.bfloat16)
    out_part = lax.dot_general(
        grad_rows, hidden, (((0,), (0,)), ((), ())), preferred_element_type=jnp.float32
    )
    in_part = lax.dot_general(
        shard_rows, grad_pre, (((0,), (0,)), ((), ())), preferred_element_type=jnp.float32
    )
    n_mass = peers
    in_rows = in_part.shape[0] // n_mass
    out_rows = out_part.shape[0] // n_mass
    partial = jnp.concatenate(
        [
            in_part.reshape(n_mass, in_rows, in_part.shape[1]),
            out_part.reshape(n_mass, out_rows, out_part.shape[1]),
        ],
        axis=1,
    ).astype(jnp.bfloat16)
    summed = jnp.sum(
        lax.all_to_all(partial, "mass", split_axis=0, concat_axis=0, tiled=True).astype(
            jnp.float32
        ),
        axis=0,
    )
    grad_in, grad_out_t = summed[:in_rows], summed[in_rows:]
    return (grad_in, grad_out_t)


def solution(mesh):
    placed = (
        P(("mass", "sub"), None),
        P(None, "sub"),
        P("sub", None),
        P("mass", "sub", None, None),
        P("mass", "sub", None),
        P("mass", "sub", None, None),
    )
    return jax.shard_map(
        per_device,
        mesh=mesh,
        in_specs=placed,
        out_specs=(P("mass", "sub"), P("mass", "sub")),
        check_vma=False,
    )
```

```python
import functools

import jax
import jax.numpy as jnp
from jax import lax
from jax.experimental import pallas as pl
from jax.experimental.pallas import tpu as pltpu
from jax.sharding import PartitionSpec as P

MESH = pl.DeviceIdType.MESH


def _exchange_kernel(n, x_ref, o_ref, got, send_sems, recv_sems):
    me = lax.axis_index("mass")
    barrier = pltpu.get_barrier_semaphore()
    for k in range(1, n):
        pl.semaphore_signal(
            barrier, inc=1, device_id={"mass": lax.rem(me + k, n)}, device_id_type=MESH
        )
    pl.semaphore_wait(barrier, n - 1)
    sends = []
    for k in range(1, n):
        peer = lax.rem(me + k, n)
        copy = pltpu.make_async_remote_copy(
            src_ref=x_ref.at[peer],
            dst_ref=got.at[me],
            send_sem=send_sems.at[k],
            recv_sem=recv_sems.at[k],
            device_id={"mass": peer},
            device_id_type=MESH,
        )
        copy.start()
        sends.append(copy)
    o_ref[me] = x_ref[me]
    for k in range(1, n):
        sends[k - 1].wait_send()
        source = lax.rem(me + n - k, n)
        pltpu.make_async_remote_copy(
            src_ref=x_ref.at[source],
            dst_ref=got.at[source],
            send_sem=send_sems.at[k],
            recv_sem=recv_sems.at[k],
            device_id={"mass": source},
            device_id_type=MESH,
        ).wait_recv()
        o_ref[source] = got[source]


def mass_exchange(x, collective_id):
    n = x.shape[0]
    return pl.pallas_call(
        functools.partial(_exchange_kernel, n),
        out_shape=jax.ShapeDtypeStruct(x.shape, x.dtype),
        in_specs=[pl.BlockSpec(memory_space=pltpu.VMEM)],
        out_specs=pl.BlockSpec(memory_space=pltpu.VMEM),
        scratch_shapes=[
            pltpu.VMEM(x.shape, x.dtype),
            pltpu.SemaphoreType.DMA((n,)),
            pltpu.SemaphoreType.DMA((n,)),
        ],
        compiler_params=pltpu.CompilerParams(collective_id=collective_id, has_side_effects=True),
    )(x)


def per_device(spectra, w_in, w_out, partner_rows, pair_counts, pair_labels):
    own_rows = spectra.shape[0]
    peers = partner_rows.shape[2]
    slots = partner_rows.shape[3]
    shard_rows = lax.all_gather(spectra, "sub", axis=0, tiled=True)
    pre = jnp.dot(shard_rows, w_in, preferred_element_type=jnp.float32)
    hidden = jax.nn.silu(pre).astype(jnp.bfloat16)
    embed = lax.psum_scatter(
        jnp.dot(hidden, w_out, preferred_element_type=jnp.float32),
        "sub",
        scatter_dimension=0,
        tiled=True,
    )
    norm = jnp.sqrt(jnp.sum(embed * embed, axis=-1, keepdims=True) + 1e-06)
    unit = embed / norm
    unit_b = unit.astype(jnp.bfloat16)
    flat_rows = partner_rows.reshape(peers * slots)
    selector = flat_rows[:, None] == jnp.arange(own_rows, dtype=jnp.int32)[None, :]
    mine = jnp.dot(
        selector.astype(jnp.bfloat16), unit_b, preferred_element_type=jnp.float32
    ).astype(jnp.bfloat16)
    outgoing = mine.reshape(peers, slots, mine.shape[1])
    incoming = mass_exchange(outgoing, 0)
    theirs = incoming.astype(jnp.float32)
    sim = jnp.sum(outgoing.astype(jnp.float32) * theirs, axis=-1)
    valid = jnp.arange(slots, dtype=jnp.int32)[None, :] < pair_counts.reshape(peers)[:, None]
    labels = pair_labels.reshape(peers, slots).astype(jnp.float32)
    coef = jnp.where(valid, 2.0 * (sim - labels), jnp.float32(0.0))
    weighted = (coef[..., None] * theirs).reshape(peers * slots, theirs.shape[2])
    grad_unit = lax.dot_general(
        selector.astype(jnp.float32),
        weighted,
        (((0,), (0,)), ((), ())),
        precision=lax.Precision.HIGHEST,
    )
    along = jnp.sum(unit * grad_unit, axis=-1, keepdims=True)
    grad_embed = ((grad_unit - unit * along) / norm).astype(jnp.bfloat16)
    grad_rows = lax.all_gather(grad_embed, "sub", axis=0, tiled=True)
    back = lax.dot_general(
        grad_rows, w_out, (((1,), (1,)), ((), ())), preferred_element_type=jnp.float32
    )
    gate = jax.nn.sigmoid(pre)
    grad_pre = (back * gate * (1.0 + pre * (1.0 - gate))).astype(jnp.bfloat16)
    out_part = lax.dot_general(
        grad_rows, hidden, (((0,), (0,)), ((), ())), preferred_element_type=jnp.float32
    )
    in_part = lax.dot_general(
        shard_rows, grad_pre, (((0,), (0,)), ((), ())), preferred_element_type=jnp.float32
    )
    n_mass = peers
    in_rows = in_part.shape[0] // n_mass
    out_rows = out_part.shape[0] // n_mass
    partial = jnp.concatenate(
        [
            in_part.reshape(n_mass, in_rows, in_part.shape[1]),
            out_part.reshape(n_mass, out_rows, out_part.shape[1]),
        ],
        axis=1,
    ).astype(jnp.bfloat16)
    summed = jnp.sum(
        mass_exchange(partial, 1).astype(
            jnp.float32
        ),
        axis=0,
    )
    grad_in, grad_out_t = summed[:in_rows], summed[in_rows:]
    return (grad_in, grad_out_t)


def solution(mesh):
    placed = (
        P(("mass", "sub"), None),
        P(None, "sub"),
        P("sub", None),
        P("mass", "sub", None, None),
        P("mass", "sub", None),
        P("mass", "sub", None, None),
    )
    return jax.shard_map(
        per_device,
        mesh=mesh,
        in_specs=placed,
        out_specs=(P("mass", "sub"), P("mass", "sub")),
        check_vma=False,
    )
```

```python
import functools

import jax
import jax.numpy as jnp
from jax import lax
from jax.experimental import pallas as pl
from jax.experimental.pallas import tpu as pltpu
from jax.sharding import PartitionSpec as P

MESH = pl.DeviceIdType.MESH


def _exchange_kernel(n, axis, gather, x_ref, o_ref, got, send_sems, recv_sems):
    me = lax.axis_index(axis)
    barrier = pltpu.get_barrier_semaphore()
    for k in range(1, n):
        pl.semaphore_signal(
            barrier, inc=1, device_id={axis: lax.rem(me + k, n)}, device_id_type=MESH
        )
    pl.semaphore_wait(barrier, n - 1)
    sends = []
    for k in range(1, n):
        peer = lax.rem(me + k, n)
        copy = pltpu.make_async_remote_copy(
            src_ref=x_ref if gather else x_ref.at[peer],
            dst_ref=got.at[me],
            send_sem=send_sems.at[k],
            recv_sem=recv_sems.at[k],
            device_id={axis: peer},
            device_id_type=MESH,
        )
        copy.start()
        sends.append(copy)
    o_ref[me] = x_ref[...] if gather else x_ref[me]
    for k in range(1, n):
        sends[k - 1].wait_send()
        source = lax.rem(me + n - k, n)
        pltpu.make_async_remote_copy(
            src_ref=x_ref if gather else x_ref.at[source],
            dst_ref=got.at[source],
            send_sem=send_sems.at[k],
            recv_sem=recv_sems.at[k],
            device_id={axis: source},
            device_id_type=MESH,
        ).wait_recv()
        o_ref[source] = got[source]


def exchange(x, axis, n, collective_id, gather=False):
    shape = (n,) + x.shape if gather else x.shape
    return pl.pallas_call(
        functools.partial(_exchange_kernel, n, axis, gather),
        out_shape=jax.ShapeDtypeStruct(shape, x.dtype),
        in_specs=[pl.BlockSpec(memory_space=pltpu.VMEM)],
        out_specs=pl.BlockSpec(memory_space=pltpu.VMEM),
        scratch_shapes=[
            pltpu.VMEM(shape, x.dtype),
            pltpu.SemaphoreType.DMA((n,)),
            pltpu.SemaphoreType.DMA((n,)),
        ],
        compiler_params=pltpu.CompilerParams(collective_id=collective_id, has_side_effects=True),
    )(x)


def per_device(spectra, w_in, w_out, partner_rows, pair_counts, pair_labels):
    own_rows = spectra.shape[0]
    peers = partner_rows.shape[2]
    slots = partner_rows.shape[3]
    shard_rows = lax.all_gather(spectra, "sub", axis=0, tiled=True)
    pre = jnp.dot(shard_rows, w_in, preferred_element_type=jnp.float32)
    hidden = jax.nn.silu(pre).astype(jnp.bfloat16)
    n_sub = shard_rows.shape[0] // own_rows
    embed_part = jnp.dot(hidden, w_out, preferred_element_type=jnp.float32)
    embed = jnp.sum(
        exchange(embed_part.reshape(n_sub, own_rows, embed_part.shape[1]), "sub", n_sub, 2),
        axis=0,
    )
    norm = jnp.sqrt(jnp.sum(embed * embed, axis=-1, keepdims=True) + 1e-06)
    unit = embed / norm
    unit_b = unit.astype(jnp.bfloat16)
    flat_rows = partner_rows.reshape(peers * slots)
    selector = flat_rows[:, None] == jnp.arange(own_rows, dtype=jnp.int32)[None, :]
    mine = jnp.dot(
        selector.astype(jnp.bfloat16), unit_b, preferred_element_type=jnp.float32
    ).astype(jnp.bfloat16)
    outgoing = mine.reshape(peers, slots, mine.shape[1])
    incoming = exchange(outgoing, "mass", peers, 0)
    theirs = incoming.astype(jnp.float32)
    sim = jnp.sum(outgoing.astype(jnp.float32) * theirs, axis=-1)
    valid = jnp.arange(slots, dtype=jnp.int32)[None, :] < pair_counts.reshape(peers)[:, None]
    labels = pair_labels.reshape(peers, slots).astype(jnp.float32)
    coef = jnp.where(valid, 2.0 * (sim - labels), jnp.float32(0.0))
    weighted = (coef[..., None] * theirs).reshape(peers * slots, theirs.shape[2])
    grad_unit = lax.dot_general(
        selector.astype(jnp.float32),
        weighted,
        (((0,), (0,)), ((), ())),
        precision=lax.Precision.HIGHEST,
    )
    along = jnp.sum(unit * grad_unit, axis=-1, keepdims=True)
    grad_embed = ((grad_unit - unit * along) / norm).astype(jnp.bfloat16)
    grad_rows = exchange(grad_embed, "sub", n_sub, 3, gather=True).reshape(
        n_sub * own_rows, grad_embed.shape[1]
    )
    back = lax.dot_general(
        grad_rows, w_out, (((1,), (1,)), ((), ())), preferred_element_type=jnp.float32
    )
    gate = jax.nn.sigmoid(pre)
    grad_pre = (back * gate * (1.0 + pre * (1.0 - gate))).astype(jnp.bfloat16)
    out_part = lax.dot_general(
        grad_rows, hidden, (((0,), (0,)), ((), ())), preferred_element_type=jnp.float32
    )
    in_part = lax.dot_general(
        shard_rows, grad_pre, (((0,), (0,)), ((), ())), preferred_element_type=jnp.float32
    )
    n_mass = peers
    in_rows = in_part.shape[0] // n_mass
    out_rows = out_part.shape[0] // n_mass
    partial = jnp.concatenate(
        [
            in_part.reshape(n_mass, in_rows, in_part.shape[1]),
            out_part.reshape(n_mass, out_rows, out_part.shape[1]),
        ],
        axis=1,
    ).astype(jnp.bfloat16)
    summed = jnp.sum(
        exchange(partial, "mass", peers, 1).astype(
            jnp.float32
        ),
        axis=0,
    )
    grad_in, grad_out_t = summed[:in_rows], summed[in_rows:]
    return (grad_in, grad_out_t)


def solution(mesh):
    placed = (
        P(("mass", "sub"), None),
        P(None, "sub"),
        P("sub", None),
        P("mass", "sub", None, None),
        P("mass", "sub", None),
        P("mass", "sub", None, None),
    )
    return jax.shard_map(
        per_device,
        mesh=mesh,
        in_specs=placed,
        out_specs=(P("mass", "sub"), P("mass", "sub")),
        check_vma=False,
    )
```

```python
import functools

import jax
import jax.numpy as jnp
from jax import lax
from jax.experimental import pallas as pl
from jax.experimental.pallas import tpu as pltpu
from jax.sharding import PartitionSpec as P

MESH = pl.DeviceIdType.MESH


def _exchange_kernel(n, stride, axis, gather, x_ref, o_ref, got, send_sems, recv_sems):
    me = lax.axis_index(axis)
    mine = lax.rem(lax.div(me, stride), n)
    base = me - mine * stride

    def member(j):
        return base + j * stride

    barrier = pltpu.get_barrier_semaphore()
    for k in range(1, n):
        pl.semaphore_signal(
            barrier, inc=1, device_id={axis: member(lax.rem(mine + k, n))}, device_id_type=MESH
        )
    pl.semaphore_wait(barrier, n - 1)
    sends = []
    for k in range(1, n):
        peer = lax.rem(mine + k, n)
        copy = pltpu.make_async_remote_copy(
            src_ref=x_ref if gather else x_ref.at[peer],
            dst_ref=got.at[mine],
            send_sem=send_sems.at[k],
            recv_sem=recv_sems.at[k],
            device_id={axis: member(peer)},
            device_id_type=MESH,
        )
        copy.start()
        sends.append(copy)
    o_ref[mine] = x_ref[...] if gather else x_ref[mine]
    for k in range(1, n):
        sends[k - 1].wait_send()
        source = lax.rem(mine + n - k, n)
        pltpu.make_async_remote_copy(
            src_ref=x_ref if gather else x_ref.at[source],
            dst_ref=got.at[source],
            send_sem=send_sems.at[k],
            recv_sem=recv_sems.at[k],
            device_id={axis: member(source)},
            device_id_type=MESH,
        ).wait_recv()
        o_ref[source] = got[source]


def exchange(x, axis, n, collective_id, gather=False, stride=1):
    shape = (n,) + x.shape if gather else x.shape
    return pl.pallas_call(
        functools.partial(_exchange_kernel, n, stride, axis, gather),
        out_shape=jax.ShapeDtypeStruct(shape, x.dtype),
        in_specs=[pl.BlockSpec(memory_space=pltpu.VMEM)],
        out_specs=pl.BlockSpec(memory_space=pltpu.VMEM),
        scratch_shapes=[
            pltpu.VMEM(shape, x.dtype),
            pltpu.SemaphoreType.DMA((n,)),
            pltpu.SemaphoreType.DMA((n,)),
        ],
        compiler_params=pltpu.CompilerParams(collective_id=collective_id, has_side_effects=True),
    )(x)


def reduce_scatter(x, axis, inner, first_inner, first_id):
    outer = x.shape[0] // inner
    blocks = x.reshape((outer, inner) + x.shape[1:])
    phases = [(outer, inner), (inner, 1)]
    if first_inner:
        blocks = jnp.swapaxes(blocks, 0, 1)
        phases.reverse()
    for number, (size, stride) in enumerate(phases):
        if size == 1:
            blocks = blocks[0].astype(jnp.float32)
            continue
        got = exchange(blocks.astype(x.dtype), axis, size, first_id + number, stride=stride)
        blocks = jnp.sum(got.astype(jnp.float32), axis=0)
    return blocks


def inner_size(devices):
    coords = [tuple(getattr(d, "coords", ())) for d in devices]
    if len(coords) < 2 or not coords[0]:
        return len(coords)
    varying = [c for c in range(len(coords[0])) if len({p[c] for p in coords}) > 1]
    slow = [c for c in varying if coords[1][c] == coords[0][c]]
    if not slow:
        return 1
    run = 0
    while run < len(coords) and coords[run][slow[0]] == coords[0][slow[0]]:
        run += 1
    return run


def per_device(mass_inner, sub_inner, spectra, w_in, w_out, partner_rows, pair_counts, pair_labels):
    own_rows = spectra.shape[0]
    peers = partner_rows.shape[2]
    slots = partner_rows.shape[3]
    shard_rows = lax.all_gather(spectra, "sub", axis=0, tiled=True)
    pre = jnp.dot(shard_rows, w_in, preferred_element_type=jnp.float32)
    hidden = jax.nn.silu(pre).astype(jnp.bfloat16)
    n_sub = shard_rows.shape[0] // own_rows
    embed_part = jnp.dot(hidden, w_out, preferred_element_type=jnp.float32)
    embed = reduce_scatter(
        embed_part.reshape(n_sub, own_rows, embed_part.shape[1]), "sub", sub_inner, True, 2
    )
    norm = jnp.sqrt(jnp.sum(embed * embed, axis=-1, keepdims=True) + 1e-06)
    unit = embed / norm
    unit_b = unit.astype(jnp.bfloat16)
    flat_rows = partner_rows.reshape(peers * slots)
    selector = flat_rows[:, None] == jnp.arange(own_rows, dtype=jnp.int32)[None, :]
    mine = jnp.dot(
        selector.astype(jnp.bfloat16), unit_b, preferred_element_type=jnp.float32
    ).astype(jnp.bfloat16)
    outgoing = mine.reshape(peers, slots, mine.shape[1])
    incoming = exchange(outgoing, "mass", peers, 1)
    theirs = incoming.astype(jnp.float32)
    sim = jnp.sum(outgoing.astype(jnp.float32) * theirs, axis=-1)
    valid = jnp.arange(slots, dtype=jnp.int32)[None, :] < pair_counts.reshape(peers)[:, None]
    labels = pair_labels.reshape(peers, slots).astype(jnp.float32)
    coef = jnp.where(valid, 2.0 * (sim - labels), jnp.float32(0.0))
    weighted = (coef[..., None] * theirs).reshape(peers * slots, theirs.shape[2])
    grad_unit = lax.dot_general(
        selector.astype(jnp.float32),
        weighted,
        (((0,), (0,)), ((), ())),
        precision=lax.Precision.HIGHEST,
    )
    along = jnp.sum(unit * grad_unit, axis=-1, keepdims=True)
    grad_embed = ((grad_unit - unit * along) / norm).astype(jnp.bfloat16)
    grad_rows = exchange(grad_embed, "sub", n_sub, 4, gather=True).reshape(
        n_sub * own_rows, grad_embed.shape[1]
    )
    back = lax.dot_general(
        grad_rows, w_out, (((1,), (1,)), ((), ())), preferred_element_type=jnp.float32
    )
    gate = jax.nn.sigmoid(pre)
    grad_pre = (back * gate * (1.0 + pre * (1.0 - gate))).astype(jnp.bfloat16)
    out_part = lax.dot_general(
        grad_rows, hidden, (((0,), (0,)), ((), ())), preferred_element_type=jnp.float32
    )
    in_part = lax.dot_general(
        shard_rows, grad_pre, (((0,), (0,)), ((), ())), preferred_element_type=jnp.float32
    )
    n_mass = peers
    in_rows = in_part.shape[0] // n_mass
    out_rows = out_part.shape[0] // n_mass
    partial = jnp.concatenate(
        [
            in_part.reshape(n_mass, in_rows, in_part.shape[1]),
            out_part.reshape(n_mass, out_rows, out_part.shape[1]),
        ],
        axis=1,
    ).astype(jnp.bfloat16)
    summed = reduce_scatter(partial, "mass", mass_inner, False, 5)
    grad_in, grad_out_t = summed[:in_rows], summed[in_rows:]
    return (grad_in, grad_out_t)


def solution(mesh):
    placed = (
        P(("mass", "sub"), None),
        P(None, "sub"),
        P("sub", None),
        P("mass", "sub", None, None),
        P("mass", "sub", None),
        P("mass", "sub", None, None),
    )
    mass_inner = inner_size(list(mesh.devices[:, 0]))
    sub_inner = inner_size(list(mesh.devices[0, :]))
    return jax.shard_map(
        functools.partial(per_device, mass_inner, sub_inner),
        mesh=mesh,
        in_specs=placed,
        out_specs=(P("mass", "sub"), P("mass", "sub")),
        check_vma=False,
    )
```

```python
import functools
import math

import jax
import jax.numpy as jnp
from jax import lax
from jax.experimental import pallas as pl
from jax.experimental.pallas import tpu as pltpu
from jax.sharding import PartitionSpec as P

MESH = pl.DeviceIdType.MESH


def _exchange_kernel(n, stride, axis, gather, x_ref, o_ref, got, send_sems, recv_sems):
    me = lax.axis_index(axis)
    mine = lax.rem(lax.div(me, stride), n)
    base = me - mine * stride

    def member(j):
        return base + j * stride

    barrier = pltpu.get_barrier_semaphore()
    for k in range(1, n):
        pl.semaphore_signal(
            barrier, inc=1, device_id={axis: member(lax.rem(mine + k, n))}, device_id_type=MESH
        )
    pl.semaphore_wait(barrier, n - 1)
    sends = []
    for k in range(1, n):
        peer = lax.rem(mine + k, n)
        copy = pltpu.make_async_remote_copy(
            src_ref=x_ref if gather else x_ref.at[peer],
            dst_ref=got.at[mine],
            send_sem=send_sems.at[k],
            recv_sem=recv_sems.at[k],
            device_id={axis: member(peer)},
            device_id_type=MESH,
        )
        copy.start()
        sends.append(copy)
    o_ref[mine] = x_ref[...] if gather else x_ref[mine]
    for k in range(1, n):
        sends[k - 1].wait_send()
        source = lax.rem(mine + n - k, n)
        pltpu.make_async_remote_copy(
            src_ref=x_ref if gather else x_ref.at[source],
            dst_ref=got.at[source],
            send_sem=send_sems.at[k],
            recv_sem=recv_sems.at[k],
            device_id={axis: member(source)},
            device_id_type=MESH,
        ).wait_recv()
        o_ref[source] = got[source]


def exchange(x, axis, n, collective_id, gather=False, stride=1):
    shape = (n,) + x.shape if gather else x.shape
    return pl.pallas_call(
        functools.partial(_exchange_kernel, n, stride, axis, gather),
        out_shape=jax.ShapeDtypeStruct(shape, x.dtype),
        in_specs=[pl.BlockSpec(memory_space=pltpu.VMEM)],
        out_specs=pl.BlockSpec(memory_space=pltpu.VMEM),
        scratch_shapes=[
            pltpu.VMEM(shape, x.dtype),
            pltpu.SemaphoreType.DMA((n,)),
            pltpu.SemaphoreType.DMA((n,)),
        ],
        compiler_params=pltpu.CompilerParams(
            collective_id=collective_id,
            has_side_effects=True,
            vmem_limit_bytes=min(3 * x.dtype.itemsize * math.prod(shape) + (8 << 20), 60 << 20),
        ),
    )(x)


def reduce_scatter(x, axis, inner, first_inner, first_id):
    outer = x.shape[0] // inner
    if first_inner:
        blocks = x.reshape((inner, outer) + x.shape[1:])
        phases = [(inner, 1), (outer, inner)]
    else:
        blocks = x.reshape((outer, inner) + x.shape[1:])
        phases = [(outer, inner), (inner, 1)]
    for number, (size, stride) in enumerate(phases):
        if size == 1:
            blocks = blocks[0].astype(jnp.float32)
            continue
        got = exchange(blocks.astype(x.dtype), axis, size, first_id + number, stride=stride)
        blocks = jnp.sum(got.astype(jnp.float32), axis=0)
    return blocks


def all_gather(x, axis, n, inner, first_id):
    outer = n // inner
    got = x[None]
    if outer > 1:
        got = exchange(x, axis, outer, first_id, gather=True, stride=inner)
    got = got[None]
    if inner > 1:
        got = exchange(got[0], axis, inner, first_id + 1, gather=True)
    return got.reshape((n * x.shape[0],) + x.shape[1:])


def inner_size(devices):
    coords = [tuple(getattr(d, "coords", ())) for d in devices]
    if len(coords) < 2 or not coords[0]:
        return len(coords)
    varying = [c for c in range(len(coords[0])) if len({p[c] for p in coords}) > 1]
    slow = [c for c in varying if coords[1][c] == coords[0][c]]
    if not slow:
        return 1
    run = 0
    while run < len(coords) and coords[run][slow[0]] == coords[0][slow[0]]:
        run += 1
    return run


def per_device(n_sub, mass_inner, sub_inner, spectra, w_in, w_out, partner_rows, pair_counts, pair_labels):
    own_rows = spectra.shape[0]
    peers = partner_rows.shape[2]
    slots = partner_rows.shape[3]
    shard_rows = all_gather(spectra, "sub", n_sub, sub_inner, 2)
    pre = jnp.dot(shard_rows, w_in, preferred_element_type=jnp.float32)
    hidden = jax.nn.silu(pre).astype(jnp.bfloat16)
    embed_part = jnp.dot(hidden, w_out, preferred_element_type=jnp.float32)
    embed = reduce_scatter(
        embed_part.reshape(n_sub, own_rows, embed_part.shape[1]), "sub", sub_inner, True, 4
    )
    norm = jnp.sqrt(jnp.sum(embed * embed, axis=-1, keepdims=True) + 1e-06)
    unit = embed / norm
    unit_b = unit.astype(jnp.bfloat16)
    flat_rows = partner_rows.reshape(peers * slots)
    selector = flat_rows[:, None] == jnp.arange(own_rows, dtype=jnp.int32)[None, :]
    mine = jnp.dot(
        selector.astype(jnp.bfloat16), unit_b, preferred_element_type=jnp.float32
    ).astype(jnp.bfloat16)
    outgoing = mine.reshape(peers, slots, mine.shape[1])
    incoming = exchange(outgoing, "mass", peers, 1)
    theirs = incoming.astype(jnp.float32)
    sim = jnp.sum(outgoing.astype(jnp.float32) * theirs, axis=-1)
    valid = jnp.arange(slots, dtype=jnp.int32)[None, :] < pair_counts.reshape(peers)[:, None]
    labels = pair_labels.reshape(peers, slots).astype(jnp.float32)
    coef = jnp.where(valid, 2.0 * (sim - labels), jnp.float32(0.0))
    weighted = (coef[..., None] * theirs).reshape(peers * slots, theirs.shape[2])
    grad_unit = lax.dot_general(
        selector.astype(jnp.float32),
        weighted,
        (((0,), (0,)), ((), ())),
        precision=lax.Precision.HIGHEST,
    )
    along = jnp.sum(unit * grad_unit, axis=-1, keepdims=True)
    grad_embed = ((grad_unit - unit * along) / norm).astype(jnp.bfloat16)
    grad_rows = all_gather(grad_embed, "sub", n_sub, sub_inner, 6)
    back = lax.dot_general(
        grad_rows, w_out, (((1,), (1,)), ((), ())), preferred_element_type=jnp.float32
    )
    gate = jax.nn.sigmoid(pre)
    grad_pre = (back * gate * (1.0 + pre * (1.0 - gate))).astype(jnp.bfloat16)
    out_part = lax.dot_general(
        grad_rows, hidden, (((0,), (0,)), ((), ())), preferred_element_type=jnp.float32
    )
    in_part = lax.dot_general(
        shard_rows, grad_pre, (((0,), (0,)), ((), ())), preferred_element_type=jnp.float32
    )
    n_mass = peers
    in_rows = in_part.shape[0] // n_mass
    out_rows = out_part.shape[0] // n_mass
    partial = jnp.concatenate(
        [
            in_part.reshape(n_mass, in_rows, in_part.shape[1]),
            out_part.reshape(n_mass, out_rows, out_part.shape[1]),
        ],
        axis=1,
    ).astype(jnp.bfloat16)
    summed = reduce_scatter(partial, "mass", mass_inner, False, 8)
    grad_in, grad_out_t = summed[:in_rows], summed[in_rows:]
    return (grad_in, grad_out_t)


def solution(mesh):
    placed = (
        P(("mass", "sub"), None),
        P(None, "sub"),
        P("sub", None),
        P("mass", "sub", None, None),
        P("mass", "sub", None),
        P("mass", "sub", None, None),
    )
    mass_inner = inner_size(list(mesh.devices[:, 0]))
    sub_inner = inner_size(list(mesh.devices[0, :]))
    return jax.shard_map(
        functools.partial(per_device, mesh.shape["sub"], mass_inner, sub_inner),
        mesh=mesh,
        in_specs=placed,
        out_specs=(P("mass", "sub"), P("mass", "sub")),
        check_vma=False,
    )
```

```python
import functools
import math

import jax
import jax.numpy as jnp
from jax import lax
from jax.experimental import pallas as pl
from jax.experimental.pallas import tpu as pltpu
from jax.sharding import PartitionSpec as P

MESH = pl.DeviceIdType.MESH


def _exchange_kernel(n, stride, axis, gather, x_ref, o_ref, got, send_sems, recv_sems):
    me = lax.axis_index(axis)
    mine = lax.rem(lax.div(me, stride), n)
    base = me - mine * stride

    def member(j):
        return base + j * stride

    barrier = pltpu.get_barrier_semaphore()
    for k in range(1, n):
        pl.semaphore_signal(
            barrier, inc=1, device_id={axis: member(lax.rem(mine + k, n))}, device_id_type=MESH
        )
    pl.semaphore_wait(barrier, n - 1)
    sends = []
    for k in range(1, n):
        peer = lax.rem(mine + k, n)
        copy = pltpu.make_async_remote_copy(
            src_ref=x_ref if gather else x_ref.at[peer],
            dst_ref=got.at[mine],
            send_sem=send_sems.at[k],
            recv_sem=recv_sems.at[k],
            device_id={axis: member(peer)},
            device_id_type=MESH,
        )
        copy.start()
        sends.append(copy)
    o_ref[mine] = x_ref[...] if gather else x_ref[mine]
    for k in range(1, n):
        sends[k - 1].wait_send()
        source = lax.rem(mine + n - k, n)
        pltpu.make_async_remote_copy(
            src_ref=x_ref if gather else x_ref.at[source],
            dst_ref=got.at[source],
            send_sem=send_sems.at[k],
            recv_sem=recv_sems.at[k],
            device_id={axis: member(source)},
            device_id_type=MESH,
        ).wait_recv()
        o_ref[source] = got[source]


def exchange(x, axis, n, collective_id, gather=False, stride=1):
    shape = (n,) + x.shape if gather else x.shape
    return pl.pallas_call(
        functools.partial(_exchange_kernel, n, stride, axis, gather),
        out_shape=jax.ShapeDtypeStruct(shape, x.dtype),
        in_specs=[pl.BlockSpec(memory_space=pltpu.VMEM)],
        out_specs=pl.BlockSpec(memory_space=pltpu.VMEM),
        scratch_shapes=[
            pltpu.VMEM(shape, x.dtype),
            pltpu.SemaphoreType.DMA((n,)),
            pltpu.SemaphoreType.DMA((n,)),
        ],
        compiler_params=pltpu.CompilerParams(
            collective_id=collective_id,
            has_side_effects=True,
            vmem_limit_bytes=min(3 * x.dtype.itemsize * math.prod(shape) + (8 << 20), 60 << 20),
        ),
    )(x)


def reduce_scatter(x, axis, inner, first_inner, first_id):
    outer = x.shape[0] // inner
    if first_inner:
        blocks = x.reshape((inner, outer) + x.shape[1:])
        phases = [(inner, 1), (outer, inner)]
    else:
        blocks = x.reshape((outer, inner) + x.shape[1:])
        phases = [(outer, inner), (inner, 1)]
    for number, (size, stride) in enumerate(phases):
        if size == 1:
            blocks = blocks[0].astype(jnp.float32)
            continue
        got = exchange(blocks.astype(x.dtype), axis, size, first_id + number, stride=stride)
        blocks = jnp.sum(got.astype(jnp.float32), axis=0)
    return blocks


def all_gather(x, axis, n, inner, first_id):
    outer = n // inner
    got = x[None]
    if outer > 1:
        got = exchange(x, axis, outer, first_id, gather=True, stride=inner)
    got = got[None]
    if inner > 1:
        got = exchange(got[0], axis, inner, first_id + 1, gather=True)
    return got.reshape((n * x.shape[0],) + x.shape[1:])


def inner_size(devices):
    coords = [tuple(getattr(d, "coords", ())) for d in devices]
    if len(coords) < 2 or not coords[0]:
        return len(coords)
    varying = [c for c in range(len(coords[0])) if len({p[c] for p in coords}) > 1]
    slow = [c for c in varying if coords[1][c] == coords[0][c]]
    if not slow:
        return 1
    run = 0
    while run < len(coords) and coords[run][slow[0]] == coords[0][slow[0]]:
        run += 1
    return run


def per_device(n_sub, mass_inner, sub_inner, spectra, w_in, w_out, partner_rows, pair_counts, pair_labels):
    own_rows = spectra.shape[0]
    peers = partner_rows.shape[2]
    slots = partner_rows.shape[3]
    shard_rows = all_gather(spectra, "sub", n_sub, sub_inner, 2)
    pre = jnp.dot(shard_rows, w_in, preferred_element_type=jnp.float32)
    hidden = jax.nn.silu(pre).astype(jnp.bfloat16)
    embed_part = jnp.dot(hidden, w_out, preferred_element_type=jnp.float32)
    embed = reduce_scatter(
        embed_part.reshape(n_sub, own_rows, embed_part.shape[1]), "sub", sub_inner, True, 4
    )
    norm = jnp.sqrt(jnp.sum(embed * embed, axis=-1, keepdims=True) + 1e-06)
    unit = embed / norm
    unit_b = unit.astype(jnp.bfloat16)
    flat_rows = partner_rows.reshape(peers * slots)
    selector = flat_rows[:, None] == jnp.arange(own_rows, dtype=jnp.int32)[None, :]
    mine = jnp.dot(
        selector.astype(jnp.bfloat16), unit_b, preferred_element_type=jnp.float32
    ).astype(jnp.bfloat16)
    outgoing = mine.reshape(peers, slots, mine.shape[1])
    incoming = exchange(outgoing, "mass", peers, 1)
    theirs = incoming.astype(jnp.float32)
    sim = jnp.sum(outgoing.astype(jnp.float32) * theirs, axis=-1)
    valid = jnp.arange(slots, dtype=jnp.int32)[None, :] < pair_counts.reshape(peers)[:, None]
    labels = pair_labels.reshape(peers, slots).astype(jnp.float32)
    coef = jnp.where(valid, 2.0 * (sim - labels), jnp.float32(0.0))
    weighted = (coef[..., None] * theirs).reshape(peers * slots, theirs.shape[2])
    grad_unit = lax.dot_general(
        selector.astype(jnp.float32),
        weighted,
        (((0,), (0,)), ((), ())),
        precision=lax.Precision.HIGHEST,
    )
    along = jnp.sum(unit * grad_unit, axis=-1, keepdims=True)
    grad_embed = ((grad_unit - unit * along) / norm).astype(jnp.bfloat16)
    grad_rows = all_gather(grad_embed, "sub", n_sub, sub_inner, 6)
    back = lax.dot_general(
        grad_rows, w_out, (((1,), (1,)), ((), ())), preferred_element_type=jnp.float32
    )
    gate = jax.nn.sigmoid(pre)
    grad_pre = (back * gate * (1.0 + pre * (1.0 - gate))).astype(jnp.bfloat16)
    out_part = lax.dot_general(
        grad_rows, hidden, (((0,), (0,)), ((), ())), preferred_element_type=jnp.float32
    )
    in_part_t = lax.dot_general(
        grad_pre, shard_rows, (((0,), (0,)), ((), ())), preferred_element_type=jnp.float32
    )
    n_mass = peers
    hid = in_part_t.shape[0]
    in_cols = in_part_t.shape[1] // n_mass
    out_rows = out_part.shape[0] // n_mass
    lanes = in_cols
    partial = jnp.concatenate(
        [
            jnp.swapaxes(in_part_t.astype(jnp.bfloat16).reshape(hid, n_mass, in_cols), 0, 1),
            out_part.astype(jnp.bfloat16).reshape(n_mass, out_rows * hid // lanes, lanes),
        ],
        axis=1,
    )
    summed = reduce_scatter(partial, "mass", mass_inner, False, 8)
    grad_in = summed[:hid].T
    grad_out_t = summed[hid:].reshape(out_rows, hid)
    return (grad_in, grad_out_t)


def solution(mesh):
    placed = (
        P(("mass", "sub"), None),
        P(None, "sub"),
        P("sub", None),
        P("mass", "sub", None, None),
        P("mass", "sub", None),
        P("mass", "sub", None, None),
    )
    mass_inner = inner_size(list(mesh.devices[:, 0]))
    sub_inner = inner_size(list(mesh.devices[0, :]))
    return jax.shard_map(
        functools.partial(per_device, mesh.shape["sub"], mass_inner, sub_inner),
        mesh=mesh,
        in_specs=placed,
        out_specs=(P("mass", "sub"), P("mass", "sub")),
        check_vma=False,
    )
```

```python
import functools
import math

import jax
import jax.numpy as jnp
from jax import lax
from jax.experimental import pallas as pl
from jax.experimental.pallas import tpu as pltpu
from jax.sharding import PartitionSpec as P

MESH = pl.DeviceIdType.MESH


def _exchange_kernel(n, stride, axis, gather, x_ref, o_ref, got, send_sems, recv_sems):
    me = lax.axis_index(axis)
    mine = lax.rem(lax.div(me, stride), n)
    base = me - mine * stride

    def member(j):
        return base + j * stride

    barrier = pltpu.get_barrier_semaphore()
    for k in range(1, n):
        pl.semaphore_signal(
            barrier, inc=1, device_id={axis: member(lax.rem(mine + k, n))}, device_id_type=MESH
        )
    pl.semaphore_wait(barrier, n - 1)
    sends = []
    for k in range(1, n):
        peer = lax.rem(mine + k, n)
        copy = pltpu.make_async_remote_copy(
            src_ref=x_ref if gather else x_ref.at[peer],
            dst_ref=got.at[mine],
            send_sem=send_sems.at[k],
            recv_sem=recv_sems.at[k],
            device_id={axis: member(peer)},
            device_id_type=MESH,
        )
        copy.start()
        sends.append(copy)
    o_ref[mine] = x_ref[...] if gather else x_ref[mine]
    for k in range(1, n):
        sends[k - 1].wait_send()
        source = lax.rem(mine + n - k, n)
        pltpu.make_async_remote_copy(
            src_ref=x_ref if gather else x_ref.at[source],
            dst_ref=got.at[source],
            send_sem=send_sems.at[k],
            recv_sem=recv_sems.at[k],
            device_id={axis: member(source)},
            device_id_type=MESH,
        ).wait_recv()
        o_ref[source] = got[source]


def exchange(x, axis, n, collective_id, gather=False, stride=1):
    shape = (n,) + x.shape if gather else x.shape
    return pl.pallas_call(
        functools.partial(_exchange_kernel, n, stride, axis, gather),
        out_shape=jax.ShapeDtypeStruct(shape, x.dtype),
        in_specs=[pl.BlockSpec(memory_space=pltpu.VMEM)],
        out_specs=pl.BlockSpec(memory_space=pltpu.VMEM),
        scratch_shapes=[
            pltpu.VMEM(shape, x.dtype),
            pltpu.SemaphoreType.DMA((n,)),
            pltpu.SemaphoreType.DMA((n,)),
        ],
        compiler_params=pltpu.CompilerParams(
            collective_id=collective_id,
            has_side_effects=True,
            vmem_limit_bytes=min(3 * x.dtype.itemsize * math.prod(shape) + (8 << 20), 60 << 20),
        ),
    )(x)


def reduce_scatter(x, axis, inner, first_inner, first_id):
    outer = x.shape[0] // inner
    if first_inner:
        blocks = x.reshape((inner, outer) + x.shape[1:])
        phases = [(inner, 1), (outer, inner)]
    else:
        blocks = x.reshape((outer, inner) + x.shape[1:])
        phases = [(outer, inner), (inner, 1)]
    for number, (size, stride) in enumerate(phases):
        if size == 1:
            blocks = blocks[0].astype(jnp.float32)
            continue
        got = exchange(blocks.astype(x.dtype), axis, size, first_id + number, stride=stride)
        blocks = jnp.sum(got.astype(jnp.float32), axis=0)
    return blocks


def all_gather(x, axis, n, inner, first_id):
    outer = n // inner
    got = x[None]
    if outer > 1:
        got = exchange(x, axis, outer, first_id, gather=True, stride=inner)
    got = got[None]
    if inner > 1:
        got = exchange(got[0], axis, inner, first_id + 1, gather=True)
    return got.reshape((n * x.shape[0],) + x.shape[1:])


def inner_size(devices):
    coords = [tuple(getattr(d, "coords", ())) for d in devices]
    if len(coords) < 2 or not coords[0]:
        return len(coords)
    varying = [c for c in range(len(coords[0])) if len({p[c] for p in coords}) > 1]
    slow = [c for c in varying if coords[1][c] == coords[0][c]]
    if not slow:
        return 1
    run = 0
    while run < len(coords) and coords[run][slow[0]] == coords[0][slow[0]]:
        run += 1
    return run


def per_device(n_sub, mass_inner, sub_inner, spectra, w_in, w_out, partner_rows, pair_counts, pair_labels):
    own_rows = spectra.shape[0]
    peers = partner_rows.shape[2]
    slots = partner_rows.shape[3]
    shard_rows = all_gather(spectra, "sub", n_sub, sub_inner, 2)
    pre = jnp.dot(shard_rows, w_in, preferred_element_type=jnp.float32)
    hidden = jax.nn.silu(pre).astype(jnp.bfloat16)
    embed_part = jnp.dot(hidden, w_out, preferred_element_type=jnp.float32)
    embed = reduce_scatter(
        embed_part.reshape(n_sub, own_rows, embed_part.shape[1]), "sub", sub_inner, True, 4
    )
    norm = jnp.sqrt(jnp.sum(embed * embed, axis=-1, keepdims=True) + 1e-06)
    unit = embed / norm
    unit_b = unit.astype(jnp.bfloat16)
    flat_rows = partner_rows.reshape(peers * slots)
    selector = flat_rows[:, None] == jnp.arange(own_rows, dtype=jnp.int32)[None, :]
    mine = jnp.dot(
        selector.astype(jnp.bfloat16), unit_b, preferred_element_type=jnp.float32
    ).astype(jnp.bfloat16)
    outgoing = mine.reshape(peers, slots, mine.shape[1])
    incoming = exchange(outgoing, "mass", peers, 1)
    theirs = incoming.astype(jnp.float32)
    sim = jnp.sum(outgoing.astype(jnp.float32) * theirs, axis=-1)
    valid = jnp.arange(slots, dtype=jnp.int32)[None, :] < pair_counts.reshape(peers)[:, None]
    labels = pair_labels.reshape(peers, slots).astype(jnp.float32)
    coef = jnp.where(valid, 2.0 * (sim - labels), jnp.float32(0.0))
    weighted = (coef[..., None] * theirs).reshape(peers * slots, theirs.shape[2])
    grad_unit = lax.dot_general(
        selector.astype(jnp.float32),
        weighted,
        (((0,), (0,)), ((), ())),
        precision=lax.Precision.HIGHEST,
    )
    along = jnp.sum(unit * grad_unit, axis=-1, keepdims=True)
    grad_embed = ((grad_unit - unit * along) / norm).astype(jnp.bfloat16)
    grad_rows = all_gather(grad_embed, "sub", n_sub, sub_inner, 6)
    back = lax.dot_general(
        grad_rows, w_out, (((1,), (1,)), ((), ())), preferred_element_type=jnp.float32
    )
    gate = jax.nn.sigmoid(pre)
    grad_pre = lax.optimization_barrier(
        (back * gate * (1.0 + pre * (1.0 - gate))).astype(jnp.bfloat16)
    )
    out_part = lax.dot_general(
        grad_rows, hidden, (((0,), (0,)), ((), ())), preferred_element_type=jnp.float32
    )
    in_part_t = lax.dot_general(
        grad_pre, shard_rows, (((0,), (0,)), ((), ())), preferred_element_type=jnp.float32
    )
    n_mass = peers
    hid = in_part_t.shape[0]
    in_cols = in_part_t.shape[1] // n_mass
    out_rows = out_part.shape[0] // n_mass
    lanes = in_cols
    partial = jnp.concatenate(
        [
            jnp.swapaxes(in_part_t.astype(jnp.bfloat16).reshape(hid, n_mass, in_cols), 0, 1),
            out_part.astype(jnp.bfloat16).reshape(n_mass, out_rows * hid // lanes, lanes),
        ],
        axis=1,
    )
    summed = reduce_scatter(partial, "mass", mass_inner, False, 8)
    grad_in = summed[:hid].T
    grad_out_t = summed[hid:].reshape(out_rows, hid)
    return (grad_in, grad_out_t)


def solution(mesh):
    placed = (
        P(("mass", "sub"), None),
        P(None, "sub"),
        P("sub", None),
        P("mass", "sub", None, None),
        P("mass", "sub", None),
        P("mass", "sub", None, None),
    )
    mass_inner = inner_size(list(mesh.devices[:, 0]))
    sub_inner = inner_size(list(mesh.devices[0, :]))
    return jax.shard_map(
        functools.partial(per_device, mesh.shape["sub"], mass_inner, sub_inner),
        mesh=mesh,
        in_specs=placed,
        out_specs=(P("mass", "sub"), P("mass", "sub")),
        check_vma=False,
    )
```

```python
import functools
import math

import jax
import jax.numpy as jnp
from jax import lax
from jax.experimental import pallas as pl
from jax.experimental.pallas import tpu as pltpu
from jax.sharding import PartitionSpec as P

MESH = pl.DeviceIdType.MESH


def _exchange_kernel(n, stride, axis, gather, x_ref, o_ref, got, send_sems, recv_sems):
    me = lax.axis_index(axis)
    mine = lax.rem(lax.div(me, stride), n)
    base = me - mine * stride

    def member(j):
        return base + j * stride

    barrier = pltpu.get_barrier_semaphore()
    for k in range(1, n):
        pl.semaphore_signal(
            barrier, inc=1, device_id={axis: member(lax.rem(mine + k, n))}, device_id_type=MESH
        )
    pl.semaphore_wait(barrier, n - 1)
    sends = []
    for k in range(1, n):
        peer = lax.rem(mine + k, n)
        copy = pltpu.make_async_remote_copy(
            src_ref=x_ref if gather else x_ref.at[peer],
            dst_ref=got.at[mine],
            send_sem=send_sems.at[k],
            recv_sem=recv_sems.at[k],
            device_id={axis: member(peer)},
            device_id_type=MESH,
        )
        copy.start()
        sends.append(copy)
    o_ref[mine] = x_ref[...] if gather else x_ref[mine]
    for k in range(1, n):
        sends[k - 1].wait_send()
        source = lax.rem(mine + n - k, n)
        pltpu.make_async_remote_copy(
            src_ref=x_ref if gather else x_ref.at[source],
            dst_ref=got.at[source],
            send_sem=send_sems.at[k],
            recv_sem=recv_sems.at[k],
            device_id={axis: member(source)},
            device_id_type=MESH,
        ).wait_recv()
        o_ref[source] = got[source]


def exchange(x, axis, n, collective_id, gather=False, stride=1):
    shape = (n,) + x.shape if gather else x.shape
    return pl.pallas_call(
        functools.partial(_exchange_kernel, n, stride, axis, gather),
        out_shape=jax.ShapeDtypeStruct(shape, x.dtype),
        in_specs=[pl.BlockSpec(memory_space=pltpu.VMEM)],
        out_specs=pl.BlockSpec(memory_space=pltpu.VMEM),
        scratch_shapes=[
            pltpu.VMEM(shape, x.dtype),
            pltpu.SemaphoreType.DMA((n,)),
            pltpu.SemaphoreType.DMA((n,)),
        ],
        compiler_params=pltpu.CompilerParams(
            collective_id=collective_id,
            has_side_effects=True,
            vmem_limit_bytes=min(3 * x.dtype.itemsize * math.prod(shape) + (8 << 20), 60 << 20),
        ),
    )(x)


def reduce_scatter(x, axis, inner, first_inner, first_id):
    outer = x.shape[0] // inner
    if first_inner:
        blocks = x.reshape((inner, outer) + x.shape[1:])
        phases = [(inner, 1), (outer, inner)]
    else:
        blocks = x.reshape((outer, inner) + x.shape[1:])
        phases = [(outer, inner), (inner, 1)]
    for number, (size, stride) in enumerate(phases):
        if size == 1:
            blocks = blocks[0].astype(jnp.float32)
            continue
        got = exchange(blocks.astype(x.dtype), axis, size, first_id + number, stride=stride)
        blocks = jnp.sum(got.astype(jnp.float32), axis=0)
    return blocks


def _gather_kernel(n_outer, n_inner, axis, x_ref, o_ref, got, send_sems, recv_sems):
    me = lax.axis_index(axis)
    ci = lax.rem(me, n_inner)
    yo = lax.div(me, n_inner)

    def device(c, y):
        return {axis: y * n_inner + c}

    def slot(c, y):
        return c * n_outer + y

    outer_peers = [lax.rem(yo + k, n_outer) for k in range(1, n_outer)]
    inner_peers = [lax.rem(ci + j, n_inner) for j in range(1, n_inner)]
    barrier = pltpu.get_barrier_semaphore()
    for y in outer_peers:
        pl.semaphore_signal(barrier, inc=1, device_id=device(ci, y), device_id_type=MESH)
    for c in inner_peers:
        pl.semaphore_signal(barrier, inc=1, device_id=device(c, yo), device_id_type=MESH)
    pl.semaphore_wait(barrier, len(outer_peers) + len(inner_peers))

    sends = []

    def send(src, c, y, to):
        copy = pltpu.make_async_remote_copy(
            src_ref=src,
            dst_ref=got.at[c, y],
            send_sem=send_sems.at[len(sends)],
            recv_sem=recv_sems.at[slot(c, y)],
            device_id=to,
            device_id_type=MESH,
        )
        copy.start()
        sends.append(copy)

    def receive(c, y):
        pltpu.make_async_remote_copy(
            src_ref=x_ref,
            dst_ref=got.at[c, y],
            send_sem=send_sems.at[0],
            recv_sem=recv_sems.at[slot(c, y)],
            device_id=device(c, y),
            device_id_type=MESH,
        ).wait_recv()

    for y in outer_peers:
        send(x_ref, ci, yo, device(ci, y))
    for c in inner_peers:
        send(x_ref, ci, yo, device(c, yo))
    o_ref[ci, yo] = x_ref[...]
    for k in range(1, n_outer):
        y = lax.rem(yo + n_outer - k, n_outer)
        receive(ci, y)
        for c in inner_peers:
            send(got.at[ci, y], ci, y, device(c, yo))
        o_ref[ci, y] = got[ci, y]
    for j in range(1, n_inner):
        c = lax.rem(ci + n_inner - j, n_inner)
        for k in range(n_outer):
            y = lax.rem(yo + k, n_outer)
            receive(c, y)
            o_ref[c, y] = got[c, y]
    for copy in sends:
        copy.wait_send()


def all_gather(x, axis, n, inner, collective_id):
    outer = n // inner
    shape = (inner, outer) + x.shape
    got = pl.pallas_call(
        functools.partial(_gather_kernel, outer, inner, axis),
        out_shape=jax.ShapeDtypeStruct(shape, x.dtype),
        in_specs=[pl.BlockSpec(memory_space=pltpu.VMEM)],
        out_specs=pl.BlockSpec(memory_space=pltpu.VMEM),
        scratch_shapes=[
            pltpu.VMEM(shape, x.dtype),
            pltpu.SemaphoreType.DMA((n,)),
            pltpu.SemaphoreType.DMA((n,)),
        ],
        compiler_params=pltpu.CompilerParams(
            collective_id=collective_id,
            has_side_effects=True,
            vmem_limit_bytes=min(3 * x.dtype.itemsize * math.prod(shape) + (8 << 20), 60 << 20),
        ),
    )(x)
    return got.reshape((n * x.shape[0],) + x.shape[1:])


def inner_size(devices):
    coords = [tuple(getattr(d, "coords", ())) for d in devices]
    if len(coords) < 2 or not coords[0]:
        return len(coords)
    varying = [c for c in range(len(coords[0])) if len({p[c] for p in coords}) > 1]
    slow = [c for c in varying if coords[1][c] == coords[0][c]]
    if not slow:
        return 1
    run = 0
    while run < len(coords) and coords[run][slow[0]] == coords[0][slow[0]]:
        run += 1
    return run


def per_device(n_sub, mass_inner, sub_inner, spectra, w_in, w_out, partner_rows, pair_counts, pair_labels):
    own_rows = spectra.shape[0]
    peers = partner_rows.shape[2]
    slots = partner_rows.shape[3]
    shard_rows = all_gather(spectra, "sub", n_sub, sub_inner, 2)
    pre = jnp.dot(shard_rows, w_in, preferred_element_type=jnp.float32)
    hidden = jax.nn.silu(pre).astype(jnp.bfloat16)
    embed_part = jnp.dot(hidden, w_out, preferred_element_type=jnp.float32)
    embed = reduce_scatter(
        embed_part.reshape(n_sub, own_rows, embed_part.shape[1]), "sub", sub_inner, True, 4
    )
    norm = jnp.sqrt(jnp.sum(embed * embed, axis=-1, keepdims=True) + 1e-06)
    unit = embed / norm
    unit_b = unit.astype(jnp.bfloat16)
    flat_rows = partner_rows.reshape(peers * slots)
    selector = flat_rows[:, None] == jnp.arange(own_rows, dtype=jnp.int32)[None, :]
    mine = jnp.dot(
        selector.astype(jnp.bfloat16), unit_b, preferred_element_type=jnp.float32
    ).astype(jnp.bfloat16)
    outgoing = mine.reshape(peers, slots, mine.shape[1])
    incoming = exchange(outgoing, "mass", peers, 1)
    theirs = incoming.astype(jnp.float32)
    sim = jnp.sum(outgoing.astype(jnp.float32) * theirs, axis=-1)
    valid = jnp.arange(slots, dtype=jnp.int32)[None, :] < pair_counts.reshape(peers)[:, None]
    labels = pair_labels.reshape(peers, slots).astype(jnp.float32)
    coef = jnp.where(valid, 2.0 * (sim - labels), jnp.float32(0.0))
    weighted = (coef[..., None] * theirs).reshape(peers * slots, theirs.shape[2])
    grad_unit = lax.dot_general(
        selector.astype(jnp.float32),
        weighted,
        (((0,), (0,)), ((), ())),
        precision=lax.Precision.HIGHEST,
    )
    along = jnp.sum(unit * grad_unit, axis=-1, keepdims=True)
    grad_embed = ((grad_unit - unit * along) / norm).astype(jnp.bfloat16)
    grad_rows = all_gather(grad_embed, "sub", n_sub, sub_inner, 6)
    back = lax.dot_general(
        grad_rows, w_out, (((1,), (1,)), ((), ())), preferred_element_type=jnp.float32
    )
    gate = jax.nn.sigmoid(pre)
    grad_pre = lax.optimization_barrier(
        (back * gate * (1.0 + pre * (1.0 - gate))).astype(jnp.bfloat16)
    )
    out_part = lax.dot_general(
        grad_rows, hidden, (((0,), (0,)), ((), ())), preferred_element_type=jnp.float32
    )
    in_part_t = lax.dot_general(
        grad_pre, shard_rows, (((0,), (0,)), ((), ())), preferred_element_type=jnp.float32
    )
    n_mass = peers
    hid = in_part_t.shape[0]
    in_cols = in_part_t.shape[1] // n_mass
    out_rows = out_part.shape[0] // n_mass
    lanes = in_cols
    partial = jnp.concatenate(
        [
            jnp.swapaxes(in_part_t.astype(jnp.bfloat16).reshape(hid, n_mass, in_cols), 0, 1),
            out_part.astype(jnp.bfloat16).reshape(n_mass, out_rows * hid // lanes, lanes),
        ],
        axis=1,
    )
    summed = reduce_scatter(partial, "mass", mass_inner, False, 8)
    grad_in = summed[:hid].T
    grad_out_t = summed[hid:].reshape(out_rows, hid)
    return (grad_in, grad_out_t)


def solution(mesh):
    placed = (
        P(("mass", "sub"), None),
        P(None, "sub"),
        P("sub", None),
        P("mass", "sub", None, None),
        P("mass", "sub", None),
        P("mass", "sub", None, None),
    )
    mass_inner = inner_size(list(mesh.devices[:, 0]))
    sub_inner = inner_size(list(mesh.devices[0, :]))
    return jax.shard_map(
        functools.partial(per_device, mesh.shape["sub"], mass_inner, sub_inner),
        mesh=mesh,
        in_specs=placed,
        out_specs=(P("mass", "sub"), P("mass", "sub")),
        check_vma=False,
    )
```

```python
import functools
import math

import jax
import jax.numpy as jnp
from jax import lax
from jax.experimental import pallas as pl
from jax.experimental.pallas import tpu as pltpu
from jax.sharding import PartitionSpec as P

MESH = pl.DeviceIdType.MESH


def _exchange_kernel(n, stride, axis, gather, x_ref, o_ref, got, send_sems, recv_sems):
    me = lax.axis_index(axis)
    mine = lax.rem(lax.div(me, stride), n)
    base = me - mine * stride

    def member(j):
        return base + j * stride

    barrier = pltpu.get_barrier_semaphore()
    for k in range(1, n):
        pl.semaphore_signal(
            barrier, inc=1, device_id={axis: member(lax.rem(mine + k, n))}, device_id_type=MESH
        )
    pl.semaphore_wait(barrier, n - 1)
    sends = []
    for k in range(1, n):
        peer = lax.rem(mine + k, n)
        copy = pltpu.make_async_remote_copy(
            src_ref=x_ref if gather else x_ref.at[peer],
            dst_ref=got.at[mine],
            send_sem=send_sems.at[k],
            recv_sem=recv_sems.at[k],
            device_id={axis: member(peer)},
            device_id_type=MESH,
        )
        copy.start()
        sends.append(copy)
    o_ref[mine] = x_ref[...] if gather else x_ref[mine]
    for k in range(1, n):
        sends[k - 1].wait_send()
        source = lax.rem(mine + n - k, n)
        pltpu.make_async_remote_copy(
            src_ref=x_ref if gather else x_ref.at[source],
            dst_ref=got.at[source],
            send_sem=send_sems.at[k],
            recv_sem=recv_sems.at[k],
            device_id={axis: member(source)},
            device_id_type=MESH,
        ).wait_recv()
        o_ref[source] = got[source]


def exchange(x, axis, n, collective_id, gather=False, stride=1):
    shape = (n,) + x.shape if gather else x.shape
    return pl.pallas_call(
        functools.partial(_exchange_kernel, n, stride, axis, gather),
        out_shape=jax.ShapeDtypeStruct(shape, x.dtype),
        in_specs=[pl.BlockSpec(memory_space=pltpu.VMEM)],
        out_specs=pl.BlockSpec(memory_space=pltpu.VMEM),
        scratch_shapes=[
            pltpu.VMEM(shape, x.dtype),
            pltpu.SemaphoreType.DMA((n,)),
            pltpu.SemaphoreType.DMA((n,)),
        ],
        compiler_params=pltpu.CompilerParams(
            collective_id=collective_id,
            has_side_effects=True,
            vmem_limit_bytes=min(3 * x.dtype.itemsize * math.prod(shape) + (8 << 20), 60 << 20),
        ),
    )(x)


def reduce_scatter(x, axis, inner, first_inner, first_id):
    outer = x.shape[0] // inner
    if first_inner:
        blocks = x.reshape((inner, outer) + x.shape[1:])
        phases = [(inner, 1), (outer, inner)]
    else:
        blocks = x.reshape((outer, inner) + x.shape[1:])
        phases = [(outer, inner), (inner, 1)]
    for number, (size, stride) in enumerate(phases):
        if size == 1:
            blocks = blocks[0].astype(jnp.float32)
            continue
        got = exchange(blocks.astype(x.dtype), axis, size, first_id + number, stride=stride)
        blocks = jnp.sum(got.astype(jnp.float32), axis=0)
    return blocks


def _gather_kernel(n_outer, n_inner, axis, x_ref, o_ref, got, send_sems, recv_sems):
    me = lax.axis_index(axis)
    ci = lax.rem(me, n_inner)
    yo = lax.div(me, n_inner)

    def device(c, y):
        return {axis: y * n_inner + c}

    def slot(c, y):
        return c * n_outer + y

    outer_peers = [lax.rem(yo + k, n_outer) for k in range(1, n_outer)]
    inner_peers = [lax.rem(ci + j, n_inner) for j in range(1, n_inner)]
    barrier = pltpu.get_barrier_semaphore()
    for y in outer_peers:
        pl.semaphore_signal(barrier, inc=1, device_id=device(ci, y), device_id_type=MESH)
    for c in inner_peers:
        pl.semaphore_signal(barrier, inc=1, device_id=device(c, yo), device_id_type=MESH)
    pl.semaphore_wait(barrier, len(outer_peers) + len(inner_peers))

    sends = []

    def send(src, c, y, to):
        copy = pltpu.make_async_remote_copy(
            src_ref=src,
            dst_ref=got.at[c, y],
            send_sem=send_sems.at[len(sends)],
            recv_sem=recv_sems.at[slot(c, y)],
            device_id=to,
            device_id_type=MESH,
        )
        copy.start()
        sends.append(copy)

    def receive(c, y):
        pltpu.make_async_remote_copy(
            src_ref=x_ref,
            dst_ref=got.at[c, y],
            send_sem=send_sems.at[0],
            recv_sem=recv_sems.at[slot(c, y)],
            device_id=device(c, y),
            device_id_type=MESH,
        ).wait_recv()

    for y in outer_peers:
        send(x_ref, ci, yo, device(ci, y))
    for c in inner_peers:
        send(x_ref, ci, yo, device(c, yo))
    o_ref[ci, yo] = x_ref[...]
    for k in range(1, n_outer):
        y = lax.rem(yo + n_outer - k, n_outer)
        receive(ci, y)
        for c in inner_peers:
            send(got.at[ci, y], ci, y, device(c, yo))
        o_ref[ci, y] = got[ci, y]
    for j in range(1, n_inner):
        c = lax.rem(ci + n_inner - j, n_inner)
        for k in range(n_outer):
            y = lax.rem(yo + k, n_outer)
            receive(c, y)
            o_ref[c, y] = got[c, y]
    for copy in sends:
        copy.wait_send()


def all_gather(x, axis, n, inner, collective_id):
    outer = n // inner
    shape = (inner, outer) + x.shape
    got = pl.pallas_call(
        functools.partial(_gather_kernel, outer, inner, axis),
        out_shape=jax.ShapeDtypeStruct(shape, x.dtype),
        in_specs=[pl.BlockSpec(memory_space=pltpu.VMEM)],
        out_specs=pl.BlockSpec(memory_space=pltpu.VMEM),
        scratch_shapes=[
            pltpu.VMEM(shape, x.dtype),
            pltpu.SemaphoreType.DMA((n,)),
            pltpu.SemaphoreType.DMA((n,)),
        ],
        compiler_params=pltpu.CompilerParams(
            collective_id=collective_id,
            has_side_effects=True,
            vmem_limit_bytes=min(3 * x.dtype.itemsize * math.prod(shape) + (8 << 20), 60 << 20),
        ),
    )(x)
    return got.reshape((n * x.shape[0],) + x.shape[1:])


def _reduce_kernel(n_o, n_i, chunks, axis, p_ref, o_ref, g1, b_ref, g2, s1, r1, s2, r2):
    me = lax.axis_index(axis)
    zi = lax.rem(me, n_i)
    xo = lax.div(me, n_i)
    zc = n_i // chunks

    def device(x, z):
        return {axis: x * n_i + z}

    barrier = pltpu.get_barrier_semaphore()
    for k in range(1, n_o):
        pl.semaphore_signal(
            barrier, inc=1, device_id=device(lax.rem(xo + k, n_o), zi), device_id_type=MESH
        )
    for k in range(1, n_i):
        pl.semaphore_signal(
            barrier, inc=1, device_id=device(xo, lax.rem(zi + k, n_i)), device_id_type=MESH
        )
    pl.semaphore_wait(barrier, n_o + n_i - 2)

    def along_x(k, c, to, dst_x):
        blocks = pl.ds(c * zc, zc)
        return pltpu.make_async_remote_copy(
            src_ref=p_ref.at[to, blocks],
            dst_ref=g1.at[dst_x, blocks],
            send_sem=s1.at[k, c],
            recv_sem=r1.at[k, c],
            device_id=device(to, zi),
            device_id_type=MESH,
        )

    def along_z(k, z):
        return pltpu.make_async_remote_copy(
            src_ref=b_ref.at[z],
            dst_ref=g2.at[zi],
            send_sem=s2.at[k],
            recv_sem=r2.at[k],
            device_id=device(xo, z),
            device_id_type=MESH,
        )

    first = []
    for c in range(chunks):
        for k in range(1, n_o):
            copy = along_x(k, c, lax.rem(xo + k, n_o), xo)
            copy.start()
            first.append(copy)
    sources = [lax.rem(xo + n_o - k, n_o) for k in range(1, n_o)]
    for c in range(chunks):
        for k in range(1, n_o):
            pltpu.make_async_remote_copy(
                src_ref=p_ref.at[sources[k - 1], pl.ds(c * zc, zc)],
                dst_ref=g1.at[sources[k - 1], pl.ds(c * zc, zc)],
                send_sem=s1.at[k, c],
                recv_sem=r1.at[k, c],
                device_id=device(sources[k - 1], zi),
                device_id_type=MESH,
            ).wait_recv()
        for z in range(c * zc, (c + 1) * zc):
            total = p_ref[xo, z].astype(jnp.float32)
            for src in sources:
                total = total + g1[src, z].astype(jnp.float32)
            b_ref[z] = total.astype(b_ref.dtype)
            offset = lax.rem(z - zi + n_i, n_i)

            @pl.when(offset == 0)
            def _():
                o_ref[...] = total

            @pl.when(offset != 0)
            def _():
                along_z(offset, z).start()

    for k in range(1, n_i):
        src = lax.rem(zi + n_i - k, n_i)
        pltpu.make_async_remote_copy(
            src_ref=b_ref.at[src],
            dst_ref=g2.at[src],
            send_sem=s2.at[k],
            recv_sem=r2.at[k],
            device_id=device(xo, src),
            device_id_type=MESH,
        ).wait_recv()
        o_ref[...] = o_ref[...] + g2[src].astype(jnp.float32)
    for copy in first:
        copy.wait_send()
    for z in range(n_i):
        offset = lax.rem(z - zi + n_i, n_i)

        @pl.when(offset != 0)
        def _():
            along_z(offset, z).wait_send()


def reduce_scatter_2d(x, axis, inner):
    n = x.shape[0]
    outer = n // inner
    chunks = next(c for c in (4, 2, 1) if inner % c == 0)
    blocks = x.reshape((outer, inner) + x.shape[1:])
    return pl.pallas_call(
        functools.partial(_reduce_kernel, outer, inner, chunks, axis),
        out_shape=jax.ShapeDtypeStruct(x.shape[1:], jnp.float32),
        in_specs=[pl.BlockSpec(memory_space=pltpu.VMEM)],
        out_specs=pl.BlockSpec(memory_space=pltpu.VMEM),
        scratch_shapes=[
            pltpu.VMEM(blocks.shape, x.dtype),
            pltpu.VMEM((inner,) + x.shape[1:], x.dtype),
            pltpu.VMEM((inner,) + x.shape[1:], x.dtype),
            pltpu.SemaphoreType.DMA((outer, chunks)),
            pltpu.SemaphoreType.DMA((outer, chunks)),
            pltpu.SemaphoreType.DMA((inner,)),
            pltpu.SemaphoreType.DMA((inner,)),
        ],
        compiler_params=pltpu.CompilerParams(
            collective_id=8,
            has_side_effects=True,
            vmem_limit_bytes=min(4 * x.dtype.itemsize * x.size + (8 << 20), 60 << 20),
        ),
    )(blocks)


def inner_size(devices):
    coords = [tuple(getattr(d, "coords", ())) for d in devices]
    if len(coords) < 2 or not coords[0]:
        return len(coords)
    varying = [c for c in range(len(coords[0])) if len({p[c] for p in coords}) > 1]
    slow = [c for c in varying if coords[1][c] == coords[0][c]]
    if not slow:
        return 1
    run = 0
    while run < len(coords) and coords[run][slow[0]] == coords[0][slow[0]]:
        run += 1
    return run


def per_device(n_sub, mass_inner, sub_inner, spectra, w_in, w_out, partner_rows, pair_counts, pair_labels):
    own_rows = spectra.shape[0]
    peers = partner_rows.shape[2]
    slots = partner_rows.shape[3]
    shard_rows = all_gather(spectra, "sub", n_sub, sub_inner, 2)
    pre = jnp.dot(shard_rows, w_in, preferred_element_type=jnp.float32)
    hidden = jax.nn.silu(pre).astype(jnp.bfloat16)
    embed_part = jnp.dot(hidden, w_out, preferred_element_type=jnp.float32)
    embed = reduce_scatter(
        embed_part.reshape(n_sub, own_rows, embed_part.shape[1]), "sub", sub_inner, True, 4
    )
    norm = jnp.sqrt(jnp.sum(embed * embed, axis=-1, keepdims=True) + 1e-06)
    unit = embed / norm
    unit_b = unit.astype(jnp.bfloat16)
    flat_rows = partner_rows.reshape(peers * slots)
    selector = flat_rows[:, None] == jnp.arange(own_rows, dtype=jnp.int32)[None, :]
    mine = jnp.dot(
        selector.astype(jnp.bfloat16), unit_b, preferred_element_type=jnp.float32
    ).astype(jnp.bfloat16)
    outgoing = mine.reshape(peers, slots, mine.shape[1])
    incoming = exchange(outgoing, "mass", peers, 1)
    theirs = incoming.astype(jnp.float32)
    sim = jnp.sum(outgoing.astype(jnp.float32) * theirs, axis=-1)
    valid = jnp.arange(slots, dtype=jnp.int32)[None, :] < pair_counts.reshape(peers)[:, None]
    labels = pair_labels.reshape(peers, slots).astype(jnp.float32)
    coef = jnp.where(valid, 2.0 * (sim - labels), jnp.float32(0.0))
    weighted = (coef[..., None] * theirs).reshape(peers * slots, theirs.shape[2])
    grad_unit = lax.dot_general(
        selector.astype(jnp.float32),
        weighted,
        (((0,), (0,)), ((), ())),
        precision=lax.Precision.HIGHEST,
    )
    along = jnp.sum(unit * grad_unit, axis=-1, keepdims=True)
    grad_embed = ((grad_unit - unit * along) / norm).astype(jnp.bfloat16)
    grad_rows = all_gather(grad_embed, "sub", n_sub, sub_inner, 6)
    back = lax.dot_general(
        grad_rows, w_out, (((1,), (1,)), ((), ())), preferred_element_type=jnp.float32
    )
    gate = jax.nn.sigmoid(pre)
    grad_pre = lax.optimization_barrier(
        (back * gate * (1.0 + pre * (1.0 - gate))).astype(jnp.bfloat16)
    )
    out_part = lax.dot_general(
        grad_rows, hidden, (((0,), (0,)), ((), ())), preferred_element_type=jnp.float32
    )
    in_part_t = lax.dot_general(
        grad_pre, shard_rows, (((0,), (0,)), ((), ())), preferred_element_type=jnp.float32
    )
    n_mass = peers
    hid = in_part_t.shape[0]
    in_cols = in_part_t.shape[1] // n_mass
    out_rows = out_part.shape[0] // n_mass
    lanes = in_cols
    partial = jnp.concatenate(
        [
            jnp.swapaxes(in_part_t.astype(jnp.bfloat16).reshape(hid, n_mass, in_cols), 0, 1),
            out_part.astype(jnp.bfloat16).reshape(n_mass, out_rows * hid // lanes, lanes),
        ],
        axis=1,
    )
    summed = reduce_scatter_2d(partial, "mass", mass_inner)
    grad_in = summed[:hid].T
    grad_out_t = summed[hid:].reshape(out_rows, hid)
    return (grad_in, grad_out_t)


def solution(mesh):
    placed = (
        P(("mass", "sub"), None),
        P(None, "sub"),
        P("sub", None),
        P("mass", "sub", None, None),
        P("mass", "sub", None),
        P("mass", "sub", None, None),
    )
    mass_inner = inner_size(list(mesh.devices[:, 0]))
    sub_inner = inner_size(list(mesh.devices[0, :]))
    return jax.shard_map(
        functools.partial(per_device, mesh.shape["sub"], mass_inner, sub_inner),
        mesh=mesh,
        in_specs=placed,
        out_specs=(P("mass", "sub"), P("mass", "sub")),
        check_vma=False,
    )
```

```python
import functools
import math

import jax
import jax.numpy as jnp
from jax import lax
from jax.experimental import pallas as pl
from jax.experimental.pallas import tpu as pltpu
from jax.sharding import PartitionSpec as P

MESH = pl.DeviceIdType.MESH


def _exchange_kernel(n, stride, axis, gather, x_ref, o_ref, got, send_sems, recv_sems):
    me = lax.axis_index(axis)
    mine = lax.rem(lax.div(me, stride), n)
    base = me - mine * stride

    def member(j):
        return base + j * stride

    barrier = pltpu.get_barrier_semaphore()
    for k in range(1, n):
        pl.semaphore_signal(
            barrier, inc=1, device_id={axis: member(lax.rem(mine + k, n))}, device_id_type=MESH
        )
    pl.semaphore_wait(barrier, n - 1)
    sends = []
    for k in range(1, n):
        peer = lax.rem(mine + k, n)
        copy = pltpu.make_async_remote_copy(
            src_ref=x_ref if gather else x_ref.at[peer],
            dst_ref=got.at[mine],
            send_sem=send_sems.at[k],
            recv_sem=recv_sems.at[k],
            device_id={axis: member(peer)},
            device_id_type=MESH,
        )
        copy.start()
        sends.append(copy)
    o_ref[mine] = x_ref[...] if gather else x_ref[mine]
    for k in range(1, n):
        sends[k - 1].wait_send()
        source = lax.rem(mine + n - k, n)
        pltpu.make_async_remote_copy(
            src_ref=x_ref if gather else x_ref.at[source],
            dst_ref=got.at[source],
            send_sem=send_sems.at[k],
            recv_sem=recv_sems.at[k],
            device_id={axis: member(source)},
            device_id_type=MESH,
        ).wait_recv()
        o_ref[source] = got[source]


def exchange(x, axis, n, collective_id, gather=False, stride=1):
    shape = (n,) + x.shape if gather else x.shape
    return pl.pallas_call(
        functools.partial(_exchange_kernel, n, stride, axis, gather),
        out_shape=jax.ShapeDtypeStruct(shape, x.dtype),
        in_specs=[pl.BlockSpec(memory_space=pltpu.VMEM)],
        out_specs=pl.BlockSpec(memory_space=pltpu.VMEM),
        scratch_shapes=[
            pltpu.VMEM(shape, x.dtype),
            pltpu.SemaphoreType.DMA((n,)),
            pltpu.SemaphoreType.DMA((n,)),
        ],
        compiler_params=pltpu.CompilerParams(
            collective_id=collective_id,
            has_side_effects=True,
            vmem_limit_bytes=min(3 * x.dtype.itemsize * math.prod(shape) + (8 << 20), 60 << 20),
        ),
    )(x)


def reduce_scatter(x, axis, inner, first_inner, first_id, wire=(None, None)):
    outer = x.shape[0] // inner
    if first_inner:
        blocks = x.reshape((inner, outer) + x.shape[1:])
        phases = [(inner, 1), (outer, inner)]
    else:
        blocks = x.reshape((outer, inner) + x.shape[1:])
        phases = [(outer, inner), (inner, 1)]
    for number, (size, stride) in enumerate(phases):
        if size == 1:
            blocks = blocks[0].astype(jnp.float32)
            continue
        got = exchange(blocks.astype(wire[number] or x.dtype), axis, size, first_id + number, stride=stride)
        blocks = jnp.sum(got.astype(jnp.float32), axis=0)
    return blocks


def _gather_kernel(n_outer, n_inner, axis, x_ref, o_ref, got, send_sems, recv_sems):
    me = lax.axis_index(axis)
    ci = lax.rem(me, n_inner)
    yo = lax.div(me, n_inner)

    def device(c, y):
        return {axis: y * n_inner + c}

    def slot(c, y):
        return c * n_outer + y

    outer_peers = [lax.rem(yo + k, n_outer) for k in range(1, n_outer)]
    inner_peers = [lax.rem(ci + j, n_inner) for j in range(1, n_inner)]
    barrier = pltpu.get_barrier_semaphore()
    for y in outer_peers:
        pl.semaphore_signal(barrier, inc=1, device_id=device(ci, y), device_id_type=MESH)
    for c in inner_peers:
        pl.semaphore_signal(barrier, inc=1, device_id=device(c, yo), device_id_type=MESH)
    pl.semaphore_wait(barrier, len(outer_peers) + len(inner_peers))

    sends = []

    def send(src, c, y, to):
        copy = pltpu.make_async_remote_copy(
            src_ref=src,
            dst_ref=got.at[c, y],
            send_sem=send_sems.at[len(sends)],
            recv_sem=recv_sems.at[slot(c, y)],
            device_id=to,
            device_id_type=MESH,
        )
        copy.start()
        sends.append(copy)

    def receive(c, y):
        pltpu.make_async_remote_copy(
            src_ref=x_ref,
            dst_ref=got.at[c, y],
            send_sem=send_sems.at[0],
            recv_sem=recv_sems.at[slot(c, y)],
            device_id=device(c, y),
            device_id_type=MESH,
        ).wait_recv()

    for y in outer_peers:
        send(x_ref, ci, yo, device(ci, y))
    for c in inner_peers:
        send(x_ref, ci, yo, device(c, yo))
    o_ref[ci, yo] = x_ref[...]
    for k in range(1, n_outer):
        y = lax.rem(yo + n_outer - k, n_outer)
        receive(ci, y)
        for c in inner_peers:
            send(got.at[ci, y], ci, y, device(c, yo))
        o_ref[ci, y] = got[ci, y]
    for j in range(1, n_inner):
        c = lax.rem(ci + n_inner - j, n_inner)
        for k in range(n_outer):
            y = lax.rem(yo + k, n_outer)
            receive(c, y)
            o_ref[c, y] = got[c, y]
    for copy in sends:
        copy.wait_send()


def all_gather(x, axis, n, inner, collective_id):
    outer = n // inner
    shape = (inner, outer) + x.shape
    got = pl.pallas_call(
        functools.partial(_gather_kernel, outer, inner, axis),
        out_shape=jax.ShapeDtypeStruct(shape, x.dtype),
        in_specs=[pl.BlockSpec(memory_space=pltpu.VMEM)],
        out_specs=pl.BlockSpec(memory_space=pltpu.VMEM),
        scratch_shapes=[
            pltpu.VMEM(shape, x.dtype),
            pltpu.SemaphoreType.DMA((n,)),
            pltpu.SemaphoreType.DMA((n,)),
        ],
        compiler_params=pltpu.CompilerParams(
            collective_id=collective_id,
            has_side_effects=True,
            vmem_limit_bytes=min(3 * x.dtype.itemsize * math.prod(shape) + (8 << 20), 60 << 20),
        ),
    )(x)
    return got.reshape((n * x.shape[0],) + x.shape[1:])


def _reduce_kernel(n_o, n_i, chunks, axis, p_ref, o_ref, g1, b_ref, g2, s1, r1, s2, r2):
    me = lax.axis_index(axis)
    zi = lax.rem(me, n_i)
    xo = lax.div(me, n_i)
    zc = n_i // chunks

    def device(x, z):
        return {axis: x * n_i + z}

    barrier = pltpu.get_barrier_semaphore()
    for k in range(1, n_o):
        pl.semaphore_signal(
            barrier, inc=1, device_id=device(lax.rem(xo + k, n_o), zi), device_id_type=MESH
        )
    for k in range(1, n_i):
        pl.semaphore_signal(
            barrier, inc=1, device_id=device(xo, lax.rem(zi + k, n_i)), device_id_type=MESH
        )
    pl.semaphore_wait(barrier, n_o + n_i - 2)

    def along_x(k, c, to, dst_x):
        blocks = pl.ds(c * zc, zc)
        return pltpu.make_async_remote_copy(
            src_ref=p_ref.at[to, blocks],
            dst_ref=g1.at[dst_x, blocks],
            send_sem=s1.at[k, c],
            recv_sem=r1.at[k, c],
            device_id=device(to, zi),
            device_id_type=MESH,
        )

    def along_z(k, z):
        return pltpu.make_async_remote_copy(
            src_ref=b_ref.at[z],
            dst_ref=g2.at[zi],
            send_sem=s2.at[k],
            recv_sem=r2.at[k],
            device_id=device(xo, z),
            device_id_type=MESH,
        )

    first = []
    for c in range(chunks):
        for k in range(1, n_o):
            copy = along_x(k, c, lax.rem(xo + k, n_o), xo)
            copy.start()
            first.append(copy)
    sources = [lax.rem(xo + n_o - k, n_o) for k in range(1, n_o)]
    for c in range(chunks):
        for k in range(1, n_o):
            pltpu.make_async_remote_copy(
                src_ref=p_ref.at[sources[k - 1], pl.ds(c * zc, zc)],
                dst_ref=g1.at[sources[k - 1], pl.ds(c * zc, zc)],
                send_sem=s1.at[k, c],
                recv_sem=r1.at[k, c],
                device_id=device(sources[k - 1], zi),
                device_id_type=MESH,
            ).wait_recv()
        for z in range(c * zc, (c + 1) * zc):
            total = p_ref[xo, z].astype(jnp.float32)
            for src in sources:
                total = total + g1[src, z].astype(jnp.float32)
            b_ref[z] = total.astype(b_ref.dtype)
            offset = lax.rem(z - zi + n_i, n_i)

            @pl.when(offset == 0)
            def _():
                o_ref[...] = total

            @pl.when(offset != 0)
            def _():
                along_z(offset, z).start()

    for k in range(1, n_i):
        src = lax.rem(zi + n_i - k, n_i)
        pltpu.make_async_remote_copy(
            src_ref=b_ref.at[src],
            dst_ref=g2.at[src],
            send_sem=s2.at[k],
            recv_sem=r2.at[k],
            device_id=device(xo, src),
            device_id_type=MESH,
        ).wait_recv()
        o_ref[...] = o_ref[...] + g2[src].astype(jnp.float32)
    for copy in first:
        copy.wait_send()
    for z in range(n_i):
        offset = lax.rem(z - zi + n_i, n_i)

        @pl.when(offset != 0)
        def _():
            along_z(offset, z).wait_send()


def reduce_scatter_2d(x, axis, inner):
    n = x.shape[0]
    outer = n // inner
    chunks = next(c for c in (4, 2, 1) if inner % c == 0)
    blocks = x.reshape((outer, inner) + x.shape[1:])
    return pl.pallas_call(
        functools.partial(_reduce_kernel, outer, inner, chunks, axis),
        out_shape=jax.ShapeDtypeStruct(x.shape[1:], jnp.float32),
        in_specs=[pl.BlockSpec(memory_space=pltpu.VMEM)],
        out_specs=pl.BlockSpec(memory_space=pltpu.VMEM),
        scratch_shapes=[
            pltpu.VMEM(blocks.shape, x.dtype),
            pltpu.VMEM((inner,) + x.shape[1:], x.dtype),
            pltpu.VMEM((inner,) + x.shape[1:], x.dtype),
            pltpu.SemaphoreType.DMA((outer, chunks)),
            pltpu.SemaphoreType.DMA((outer, chunks)),
            pltpu.SemaphoreType.DMA((inner,)),
            pltpu.SemaphoreType.DMA((inner,)),
        ],
        compiler_params=pltpu.CompilerParams(
            collective_id=8,
            has_side_effects=True,
            vmem_limit_bytes=min(4 * x.dtype.itemsize * x.size + (8 << 20), 60 << 20),
        ),
    )(blocks)


def inner_size(devices):
    coords = [tuple(getattr(d, "coords", ())) for d in devices]
    if len(coords) < 2 or not coords[0]:
        return len(coords)
    varying = [c for c in range(len(coords[0])) if len({p[c] for p in coords}) > 1]
    slow = [c for c in varying if coords[1][c] == coords[0][c]]
    if not slow:
        return 1
    run = 0
    while run < len(coords) and coords[run][slow[0]] == coords[0][slow[0]]:
        run += 1
    return run


def per_device(n_sub, mass_inner, sub_inner, spectra, w_in, w_out, partner_rows, pair_counts, pair_labels):
    own_rows = spectra.shape[0]
    peers = partner_rows.shape[2]
    slots = partner_rows.shape[3]
    shard_rows = all_gather(spectra, "sub", n_sub, sub_inner, 2)
    pre = jnp.dot(shard_rows, w_in, preferred_element_type=jnp.float32)
    hidden = jax.nn.silu(pre).astype(jnp.bfloat16)
    embed_part = jnp.dot(hidden, w_out, preferred_element_type=jnp.float32)
    embed = reduce_scatter(
        embed_part.reshape(n_sub, own_rows, embed_part.shape[1]), "sub", sub_inner, True, 4,
        wire=(jnp.float32, jnp.bfloat16),
    )
    norm = jnp.sqrt(jnp.sum(embed * embed, axis=-1, keepdims=True) + 1e-06)
    unit = embed / norm
    unit_b = unit.astype(jnp.bfloat16)
    flat_rows = partner_rows.reshape(peers * slots)
    selector = flat_rows[:, None] == jnp.arange(own_rows, dtype=jnp.int32)[None, :]
    mine = jnp.dot(
        selector.astype(jnp.bfloat16), unit_b, preferred_element_type=jnp.float32
    ).astype(jnp.bfloat16)
    outgoing = mine.reshape(peers, slots, mine.shape[1])
    incoming = exchange(outgoing, "mass", peers, 1)
    theirs = incoming.astype(jnp.float32)
    sim = jnp.sum(outgoing.astype(jnp.float32) * theirs, axis=-1)
    valid = jnp.arange(slots, dtype=jnp.int32)[None, :] < pair_counts.reshape(peers)[:, None]
    labels = pair_labels.reshape(peers, slots).astype(jnp.float32)
    coef = jnp.where(valid, 2.0 * (sim - labels), jnp.float32(0.0))
    weighted = (coef[..., None] * theirs).reshape(peers * slots, theirs.shape[2])
    grad_unit = lax.dot_general(
        selector.astype(jnp.float32),
        weighted,
        (((0,), (0,)), ((), ())),
        precision=lax.Precision.HIGHEST,
    )
    along = jnp.sum(unit * grad_unit, axis=-1, keepdims=True)
    grad_embed = ((grad_unit - unit * along) / norm).astype(jnp.bfloat16)
    grad_rows = all_gather(grad_embed, "sub", n_sub, sub_inner, 6)
    back = lax.dot_general(
        grad_rows, w_out, (((1,), (1,)), ((), ())), preferred_element_type=jnp.float32
    )
    gate = jax.nn.sigmoid(pre)
    grad_pre = lax.optimization_barrier(
        (back * gate * (1.0 + pre * (1.0 - gate))).astype(jnp.bfloat16)
    )
    out_part = lax.dot_general(
        grad_rows, hidden, (((0,), (0,)), ((), ())), preferred_element_type=jnp.float32
    )
    in_part_t = lax.dot_general(
        grad_pre, shard_rows, (((0,), (0,)), ((), ())), preferred_element_type=jnp.float32
    )
    n_mass = peers
    hid = in_part_t.shape[0]
    in_cols = in_part_t.shape[1] // n_mass
    out_rows = out_part.shape[0] // n_mass
    lanes = in_cols
    partial = jnp.concatenate(
        [
            jnp.swapaxes(in_part_t.astype(jnp.bfloat16).reshape(hid, n_mass, in_cols), 0, 1),
            out_part.astype(jnp.bfloat16).reshape(n_mass, out_rows * hid // lanes, lanes),
        ],
        axis=1,
    )
    summed = reduce_scatter_2d(partial, "mass", mass_inner)
    grad_in = summed[:hid].T
    grad_out_t = summed[hid:].reshape(out_rows, hid)
    return (grad_in, grad_out_t)


def solution(mesh):
    placed = (
        P(("mass", "sub"), None),
        P(None, "sub"),
        P("sub", None),
        P("mass", "sub", None, None),
        P("mass", "sub", None),
        P("mass", "sub", None, None),
    )
    mass_inner = inner_size(list(mesh.devices[:, 0]))
    sub_inner = inner_size(list(mesh.devices[0, :]))
    return jax.shard_map(
        functools.partial(per_device, mesh.shape["sub"], mass_inner, sub_inner),
        mesh=mesh,
        in_specs=placed,
        out_specs=(P("mass", "sub"), P("mass", "sub")),
        check_vma=False,
    )
```

```python
import functools
import math

import jax
import jax.numpy as jnp
from jax import lax
from jax.experimental import pallas as pl
from jax.experimental.pallas import tpu as pltpu
from jax.sharding import PartitionSpec as P

MESH = pl.DeviceIdType.MESH


def _exchange_kernel(n, stride, axis, gather, x_ref, o_ref, got, send_sems, recv_sems):
    me = lax.axis_index(axis)
    mine = lax.rem(lax.div(me, stride), n)
    base = me - mine * stride

    def member(j):
        return base + j * stride

    barrier = pltpu.get_barrier_semaphore()
    for k in range(1, n):
        pl.semaphore_signal(
            barrier, inc=1, device_id={axis: member(lax.rem(mine + k, n))}, device_id_type=MESH
        )
    pl.semaphore_wait(barrier, n - 1)
    sends = []
    for k in range(1, n):
        peer = lax.rem(mine + k, n)
        copy = pltpu.make_async_remote_copy(
            src_ref=x_ref if gather else x_ref.at[peer],
            dst_ref=got.at[mine],
            send_sem=send_sems.at[k],
            recv_sem=recv_sems.at[k],
            device_id={axis: member(peer)},
            device_id_type=MESH,
        )
        copy.start()
        sends.append(copy)
    o_ref[mine] = x_ref[...] if gather else x_ref[mine]
    for k in range(1, n):
        sends[k - 1].wait_send()
        source = lax.rem(mine + n - k, n)
        pltpu.make_async_remote_copy(
            src_ref=x_ref if gather else x_ref.at[source],
            dst_ref=got.at[source],
            send_sem=send_sems.at[k],
            recv_sem=recv_sems.at[k],
            device_id={axis: member(source)},
            device_id_type=MESH,
        ).wait_recv()
        o_ref[source] = got[source]


def exchange(x, axis, n, collective_id, gather=False, stride=1):
    shape = (n,) + x.shape if gather else x.shape
    return pl.pallas_call(
        functools.partial(_exchange_kernel, n, stride, axis, gather),
        out_shape=jax.ShapeDtypeStruct(shape, x.dtype),
        in_specs=[pl.BlockSpec(memory_space=pltpu.VMEM)],
        out_specs=pl.BlockSpec(memory_space=pltpu.VMEM),
        scratch_shapes=[
            pltpu.VMEM(shape, x.dtype),
            pltpu.SemaphoreType.DMA((n,)),
            pltpu.SemaphoreType.DMA((n,)),
        ],
        compiler_params=pltpu.CompilerParams(
            collective_id=collective_id,
            has_side_effects=True,
            vmem_limit_bytes=min(3 * x.dtype.itemsize * math.prod(shape) + (8 << 20), 60 << 20),
        ),
    )(x)


def reduce_scatter(x, axis, inner, first_inner, first_id):
    outer = x.shape[0] // inner
    if first_inner:
        blocks = x.reshape((inner, outer) + x.shape[1:])
        phases = [(inner, 1), (outer, inner)]
    else:
        blocks = x.reshape((outer, inner) + x.shape[1:])
        phases = [(outer, inner), (inner, 1)]
    for number, (size, stride) in enumerate(phases):
        if size == 1:
            blocks = blocks[0].astype(jnp.float32)
            continue
        got = exchange(blocks.astype(x.dtype), axis, size, first_id + number, stride=stride)
        blocks = jnp.sum(got.astype(jnp.float32), axis=0)
    return blocks


def _gather_kernel(n_outer, n_inner, axis, x_ref, o_ref, got, send_sems, recv_sems):
    me = lax.axis_index(axis)
    ci = lax.rem(me, n_inner)
    yo = lax.div(me, n_inner)

    def device(c, y):
        return {axis: y * n_inner + c}

    def slot(c, y):
        return c * n_outer + y

    outer_peers = [lax.rem(yo + k, n_outer) for k in range(1, n_outer)]
    inner_peers = [lax.rem(ci + j, n_inner) for j in range(1, n_inner)]
    barrier = pltpu.get_barrier_semaphore()
    for y in outer_peers:
        pl.semaphore_signal(barrier, inc=1, device_id=device(ci, y), device_id_type=MESH)
    for c in inner_peers:
        pl.semaphore_signal(barrier, inc=1, device_id=device(c, yo), device_id_type=MESH)
    pl.semaphore_wait(barrier, len(outer_peers) + len(inner_peers))

    sends = []

    def send(src, c, y, to):
        copy = pltpu.make_async_remote_copy(
            src_ref=src,
            dst_ref=got.at[c, y],
            send_sem=send_sems.at[len(sends)],
            recv_sem=recv_sems.at[slot(c, y)],
            device_id=to,
            device_id_type=MESH,
        )
        copy.start()
        sends.append(copy)

    def receive(c, y):
        pltpu.make_async_remote_copy(
            src_ref=x_ref,
            dst_ref=got.at[c, y],
            send_sem=send_sems.at[0],
            recv_sem=recv_sems.at[slot(c, y)],
            device_id=device(c, y),
            device_id_type=MESH,
        ).wait_recv()

    for y in outer_peers:
        send(x_ref, ci, yo, device(ci, y))
    for c in inner_peers:
        send(x_ref, ci, yo, device(c, yo))
    o_ref[ci, yo] = x_ref[...]
    for k in range(1, n_outer):
        y = lax.rem(yo + n_outer - k, n_outer)
        receive(ci, y)
        for c in inner_peers:
            send(got.at[ci, y], ci, y, device(c, yo))
        o_ref[ci, y] = got[ci, y]
    for j in range(1, n_inner):
        c = lax.rem(ci + n_inner - j, n_inner)
        for k in range(n_outer):
            y = lax.rem(yo + k, n_outer)
            receive(c, y)
            o_ref[c, y] = got[c, y]
    for copy in sends:
        copy.wait_send()


def all_gather(x, axis, n, inner, collective_id):
    outer = n // inner
    shape = (inner, outer) + x.shape
    got = pl.pallas_call(
        functools.partial(_gather_kernel, outer, inner, axis),
        out_shape=jax.ShapeDtypeStruct(shape, x.dtype),
        in_specs=[pl.BlockSpec(memory_space=pltpu.VMEM)],
        out_specs=pl.BlockSpec(memory_space=pltpu.VMEM),
        scratch_shapes=[
            pltpu.VMEM(shape, x.dtype),
            pltpu.SemaphoreType.DMA((n,)),
            pltpu.SemaphoreType.DMA((n,)),
        ],
        compiler_params=pltpu.CompilerParams(
            collective_id=collective_id,
            has_side_effects=True,
            vmem_limit_bytes=min(3 * x.dtype.itemsize * math.prod(shape) + (8 << 20), 60 << 20),
        ),
    )(x)
    return got.reshape((n * x.shape[0],) + x.shape[1:])


def _reduce_kernel(n_o, n_i, chunks, axis, p_ref, o_ref, g1, b_ref, g2, s1, r1, s2, r2):
    me = lax.axis_index(axis)
    zi = lax.rem(me, n_i)
    xo = lax.div(me, n_i)
    zc = n_i // chunks

    def device(x, z):
        return {axis: x * n_i + z}

    barrier = pltpu.get_barrier_semaphore()
    for k in range(1, n_o):
        pl.semaphore_signal(
            barrier, inc=1, device_id=device(lax.rem(xo + k, n_o), zi), device_id_type=MESH
        )
    for k in range(1, n_i):
        pl.semaphore_signal(
            barrier, inc=1, device_id=device(xo, lax.rem(zi + k, n_i)), device_id_type=MESH
        )
    pl.semaphore_wait(barrier, n_o + n_i - 2)

    def along_x(k, c, to, dst_x):
        blocks = pl.ds(c * zc, zc)
        return pltpu.make_async_remote_copy(
            src_ref=p_ref.at[to, blocks],
            dst_ref=g1.at[dst_x, blocks],
            send_sem=s1.at[k, c],
            recv_sem=r1.at[k, c],
            device_id=device(to, zi),
            device_id_type=MESH,
        )

    def along_z(k, z):
        return pltpu.make_async_remote_copy(
            src_ref=b_ref.at[z],
            dst_ref=g2.at[zi],
            send_sem=s2.at[k],
            recv_sem=r2.at[k],
            device_id=device(xo, z),
            device_id_type=MESH,
        )

    first = []
    for c in range(chunks):
        for k in range(1, n_o):
            copy = along_x(k, c, lax.rem(xo + k, n_o), xo)
            copy.start()
            first.append(copy)
    sources = [lax.rem(xo + n_o - k, n_o) for k in range(1, n_o)]
    for c in range(chunks):
        for k in range(1, n_o):
            pltpu.make_async_remote_copy(
                src_ref=p_ref.at[sources[k - 1], pl.ds(c * zc, zc)],
                dst_ref=g1.at[sources[k - 1], pl.ds(c * zc, zc)],
                send_sem=s1.at[k, c],
                recv_sem=r1.at[k, c],
                device_id=device(sources[k - 1], zi),
                device_id_type=MESH,
            ).wait_recv()
        for z in range(c * zc, (c + 1) * zc):
            total = p_ref[xo, z].astype(jnp.float32)
            for src in sources:
                total = total + g1[src, z].astype(jnp.float32)
            b_ref[z] = total.astype(b_ref.dtype)
            offset = lax.rem(z - zi + n_i, n_i)

            @pl.when(offset == 0)
            def _():
                o_ref[...] = total

            @pl.when(offset != 0)
            def _():
                along_z(offset, z).start()

    for k in range(1, n_i):
        src = lax.rem(zi + n_i - k, n_i)
        pltpu.make_async_remote_copy(
            src_ref=b_ref.at[src],
            dst_ref=g2.at[src],
            send_sem=s2.at[k],
            recv_sem=r2.at[k],
            device_id=device(xo, src),
            device_id_type=MESH,
        ).wait_recv()
        o_ref[...] = o_ref[...] + g2[src].astype(jnp.float32)
    for copy in first:
        copy.wait_send()
    for z in range(n_i):
        offset = lax.rem(z - zi + n_i, n_i)

        @pl.when(offset != 0)
        def _():
            along_z(offset, z).wait_send()


def reduce_scatter_2d(x, axis, inner):
    n = x.shape[0]
    outer = n // inner
    chunks = next(c for c in (4, 2, 1) if inner % c == 0)
    blocks = x.reshape((outer, inner) + x.shape[1:])
    return pl.pallas_call(
        functools.partial(_reduce_kernel, outer, inner, chunks, axis),
        out_shape=jax.ShapeDtypeStruct(x.shape[1:], jnp.float32),
        in_specs=[pl.BlockSpec(memory_space=pltpu.VMEM)],
        out_specs=pl.BlockSpec(memory_space=pltpu.VMEM),
        scratch_shapes=[
            pltpu.VMEM(blocks.shape, x.dtype),
            pltpu.VMEM((inner,) + x.shape[1:], x.dtype),
            pltpu.VMEM((inner,) + x.shape[1:], x.dtype),
            pltpu.SemaphoreType.DMA((outer, chunks)),
            pltpu.SemaphoreType.DMA((outer, chunks)),
            pltpu.SemaphoreType.DMA((inner,)),
            pltpu.SemaphoreType.DMA((inner,)),
        ],
        compiler_params=pltpu.CompilerParams(
            collective_id=8,
            has_side_effects=True,
            vmem_limit_bytes=min(4 * x.dtype.itemsize * x.size + (8 << 20), 60 << 20),
        ),
    )(blocks)


def _relay_kernel(n_o, n_i, axis, x_ref, o_ref, g1, g2, s1, r1, s2, r2, own):
    me = lax.axis_index(axis)
    zi = lax.rem(me, n_i)
    xo = lax.div(me, n_i)

    def device(x, z):
        return {axis: x * n_i + z}

    barrier = pltpu.get_barrier_semaphore()
    for k in range(1, n_o):
        pl.semaphore_signal(
            barrier, inc=1, device_id=device(lax.rem(xo + k, n_o), zi), device_id_type=MESH
        )
    for k in range(1, n_i):
        pl.semaphore_signal(
            barrier, inc=1, device_id=device(xo, lax.rem(zi + k, n_i)), device_id_type=MESH
        )
    pl.semaphore_wait(barrier, n_o + n_i - 2)

    def along_x(k, x, src_x):
        return pltpu.make_async_remote_copy(
            src_ref=x_ref.at[x],
            dst_ref=g1.at[:, src_x],
            send_sem=s1.at[k],
            recv_sem=r1.at[k],
            device_id=device(x, zi),
            device_id_type=MESH,
        )

    def along_z(k, z, src_z):
        return pltpu.make_async_remote_copy(
            src_ref=g1.at[z],
            dst_ref=g2.at[src_z],
            send_sem=s2.at[k],
            recv_sem=r2.at[k],
            device_id=device(xo, z),
            device_id_type=MESH,
        )

    first = [along_x(k, lax.rem(xo + k, n_o), xo) for k in range(1, n_o)]
    for copy in first:
        copy.start()
    local = pltpu.make_async_copy(x_ref.at[xo], g1.at[:, xo], own)
    local.start()
    local.wait()
    for k in range(1, n_o):
        src = lax.rem(xo + n_o - k, n_o)
        along_x(k, src, src).wait_recv()
    second = [along_z(k, lax.rem(zi + k, n_i), zi) for k in range(1, n_i)]
    for copy in second:
        copy.start()
    for x in range(n_o):
        o_ref[x, zi] = g1[zi, x]
    for k in range(1, n_i):
        src = lax.rem(zi + n_i - k, n_i)
        along_z(k, src, src).wait_recv()
        for x in range(n_o):
            o_ref[x, src] = g2[src, x]
    for copy in first + second:
        copy.wait_send()


def all_to_all_2d(x, axis, inner, collective_id):
    n = x.shape[0]
    outer = n // inner
    blocks = x.reshape((outer, inner) + x.shape[1:])
    turned = (inner, outer) + x.shape[1:]
    got = pl.pallas_call(
        functools.partial(_relay_kernel, outer, inner, axis),
        out_shape=jax.ShapeDtypeStruct(blocks.shape, x.dtype),
        in_specs=[pl.BlockSpec(memory_space=pltpu.VMEM)],
        out_specs=pl.BlockSpec(memory_space=pltpu.VMEM),
        scratch_shapes=[
            pltpu.VMEM(turned, x.dtype),
            pltpu.VMEM(turned, x.dtype),
            pltpu.SemaphoreType.DMA((outer,)),
            pltpu.SemaphoreType.DMA((outer,)),
            pltpu.SemaphoreType.DMA((inner,)),
            pltpu.SemaphoreType.DMA((inner,)),
            pltpu.SemaphoreType.DMA(()),
        ],
        compiler_params=pltpu.CompilerParams(collective_id=collective_id, has_side_effects=True),
    )(blocks)
    return got.reshape(x.shape)


def inner_size(devices):
    coords = [tuple(getattr(d, "coords", ())) for d in devices]
    if len(coords) < 2 or not coords[0]:
        return len(coords)
    varying = [c for c in range(len(coords[0])) if len({p[c] for p in coords}) > 1]
    slow = [c for c in varying if coords[1][c] == coords[0][c]]
    if not slow:
        return 1
    run = 0
    while run < len(coords) and coords[run][slow[0]] == coords[0][slow[0]]:
        run += 1
    return run


def per_device(n_sub, mass_inner, sub_inner, spectra, w_in, w_out, partner_rows, pair_counts, pair_labels):
    own_rows = spectra.shape[0]
    peers = partner_rows.shape[2]
    slots = partner_rows.shape[3]
    shard_rows = all_gather(spectra, "sub", n_sub, sub_inner, 2)
    pre = jnp.dot(shard_rows, w_in, preferred_element_type=jnp.float32)
    hidden = jax.nn.silu(pre).astype(jnp.bfloat16)
    embed_part = jnp.dot(hidden, w_out, preferred_element_type=jnp.float32)
    embed = reduce_scatter(
        embed_part.reshape(n_sub, own_rows, embed_part.shape[1]), "sub", sub_inner, True, 4
    )
    norm = jnp.sqrt(jnp.sum(embed * embed, axis=-1, keepdims=True) + 1e-06)
    unit = embed / norm
    unit_b = unit.astype(jnp.bfloat16)
    flat_rows = partner_rows.reshape(peers * slots)
    selector = flat_rows[:, None] == jnp.arange(own_rows, dtype=jnp.int32)[None, :]
    mine = jnp.dot(
        selector.astype(jnp.bfloat16), unit_b, preferred_element_type=jnp.float32
    ).astype(jnp.bfloat16)
    outgoing = mine.reshape(peers, slots, mine.shape[1])
    incoming = all_to_all_2d(outgoing, "mass", mass_inner, 1)
    theirs = incoming.astype(jnp.float32)
    sim = jnp.sum(outgoing.astype(jnp.float32) * theirs, axis=-1)
    valid = jnp.arange(slots, dtype=jnp.int32)[None, :] < pair_counts.reshape(peers)[:, None]
    labels = pair_labels.reshape(peers, slots).astype(jnp.float32)
    coef = jnp.where(valid, 2.0 * (sim - labels), jnp.float32(0.0))
    weighted = (coef[..., None] * theirs).reshape(peers * slots, theirs.shape[2])
    grad_unit = lax.dot_general(
        selector.astype(jnp.float32),
        weighted,
        (((0,), (0,)), ((), ())),
        precision=lax.Precision.HIGHEST,
    )
    along = jnp.sum(unit * grad_unit, axis=-1, keepdims=True)
    grad_embed = ((grad_unit - unit * along) / norm).astype(jnp.bfloat16)
    grad_rows = all_gather(grad_embed, "sub", n_sub, sub_inner, 6)
    back = lax.dot_general(
        grad_rows, w_out, (((1,), (1,)), ((), ())), preferred_element_type=jnp.float32
    )
    gate = jax.nn.sigmoid(pre)
    grad_pre = lax.optimization_barrier(
        (back * gate * (1.0 + pre * (1.0 - gate))).astype(jnp.bfloat16)
    )
    out_part = lax.dot_general(
        grad_rows, hidden, (((0,), (0,)), ((), ())), preferred_element_type=jnp.float32
    )
    in_part_t = lax.dot_general(
        grad_pre, shard_rows, (((0,), (0,)), ((), ())), preferred_element_type=jnp.float32
    )
    n_mass = peers
    hid = in_part_t.shape[0]
    in_cols = in_part_t.shape[1] // n_mass
    out_rows = out_part.shape[0] // n_mass
    lanes = in_cols
    partial = jnp.concatenate(
        [
            jnp.swapaxes(in_part_t.astype(jnp.bfloat16).reshape(hid, n_mass, in_cols), 0, 1),
            out_part.astype(jnp.bfloat16).reshape(n_mass, out_rows * hid // lanes, lanes),
        ],
        axis=1,
    )
    summed = reduce_scatter_2d(partial, "mass", mass_inner)
    grad_in = summed[:hid].T
    grad_out_t = summed[hid:].reshape(out_rows, hid)
    return (grad_in, grad_out_t)


def solution(mesh):
    placed = (
        P(("mass", "sub"), None),
        P(None, "sub"),
        P("sub", None),
        P("mass", "sub", None, None),
        P("mass", "sub", None),
        P("mass", "sub", None, None),
    )
    mass_inner = inner_size(list(mesh.devices[:, 0]))
    sub_inner = inner_size(list(mesh.devices[0, :]))
    return jax.shard_map(
        functools.partial(per_device, mesh.shape["sub"], mass_inner, sub_inner),
        mesh=mesh,
        in_specs=placed,
        out_specs=(P("mass", "sub"), P("mass", "sub")),
        check_vma=False,
    )
```

```python
import functools
import math

import jax
import jax.numpy as jnp
from jax import lax
from jax.experimental import pallas as pl
from jax.experimental.pallas import tpu as pltpu
from jax.sharding import PartitionSpec as P

MESH = pl.DeviceIdType.MESH


def _exchange_kernel(n, stride, axis, gather, x_ref, o_ref, got, send_sems, recv_sems):
    me = lax.axis_index(axis)
    mine = lax.rem(lax.div(me, stride), n)
    base = me - mine * stride

    def member(j):
        return base + j * stride

    barrier = pltpu.get_barrier_semaphore()
    for k in range(1, n):
        pl.semaphore_signal(
            barrier, inc=1, device_id={axis: member(lax.rem(mine + k, n))}, device_id_type=MESH
        )
    pl.semaphore_wait(barrier, n - 1)
    sends = []
    for k in range(1, n):
        peer = lax.rem(mine + k, n)
        copy = pltpu.make_async_remote_copy(
            src_ref=x_ref if gather else x_ref.at[peer],
            dst_ref=got.at[mine],
            send_sem=send_sems.at[k],
            recv_sem=recv_sems.at[k],
            device_id={axis: member(peer)},
            device_id_type=MESH,
        )
        copy.start()
        sends.append(copy)
    o_ref[mine] = x_ref[...] if gather else x_ref[mine]
    for k in range(1, n):
        sends[k - 1].wait_send()
        source = lax.rem(mine + n - k, n)
        pltpu.make_async_remote_copy(
            src_ref=x_ref if gather else x_ref.at[source],
            dst_ref=got.at[source],
            send_sem=send_sems.at[k],
            recv_sem=recv_sems.at[k],
            device_id={axis: member(source)},
            device_id_type=MESH,
        ).wait_recv()
        o_ref[source] = got[source]


def exchange(x, axis, n, collective_id, gather=False, stride=1):
    shape = (n,) + x.shape if gather else x.shape
    return pl.pallas_call(
        functools.partial(_exchange_kernel, n, stride, axis, gather),
        out_shape=jax.ShapeDtypeStruct(shape, x.dtype),
        in_specs=[pl.BlockSpec(memory_space=pltpu.VMEM)],
        out_specs=pl.BlockSpec(memory_space=pltpu.VMEM),
        scratch_shapes=[
            pltpu.VMEM(shape, x.dtype),
            pltpu.SemaphoreType.DMA((n,)),
            pltpu.SemaphoreType.DMA((n,)),
        ],
        compiler_params=pltpu.CompilerParams(
            collective_id=collective_id,
            has_side_effects=True,
            vmem_limit_bytes=min(3 * x.dtype.itemsize * math.prod(shape) + (8 << 20), 60 << 20),
        ),
    )(x)


def reduce_scatter(x, axis, inner, first_inner, first_id):
    outer = x.shape[0] // inner
    if first_inner:
        blocks = x.reshape((inner, outer) + x.shape[1:])
        phases = [(inner, 1), (outer, inner)]
    else:
        blocks = x.reshape((outer, inner) + x.shape[1:])
        phases = [(outer, inner), (inner, 1)]
    for number, (size, stride) in enumerate(phases):
        if size == 1:
            blocks = blocks[0].astype(jnp.float32)
            continue
        got = exchange(blocks.astype(x.dtype), axis, size, first_id + number, stride=stride)
        blocks = jnp.sum(got.astype(jnp.float32), axis=0)
    return blocks


def _gather_kernel(n_outer, n_inner, axis, x_ref, o_ref, got, send_sems, recv_sems):
    me = lax.axis_index(axis)
    ci = lax.rem(me, n_inner)
    yo = lax.div(me, n_inner)

    def device(c, y):
        return {axis: y * n_inner + c}

    def slot(c, y):
        return c * n_outer + y

    outer_peers = [lax.rem(yo + k, n_outer) for k in range(1, n_outer)]
    inner_peers = [lax.rem(ci + j, n_inner) for j in range(1, n_inner)]
    barrier = pltpu.get_barrier_semaphore()
    for y in outer_peers:
        pl.semaphore_signal(barrier, inc=1, device_id=device(ci, y), device_id_type=MESH)
    for c in inner_peers:
        pl.semaphore_signal(barrier, inc=1, device_id=device(c, yo), device_id_type=MESH)
    pl.semaphore_wait(barrier, len(outer_peers) + len(inner_peers))

    sends = []

    def send(src, c, y, to):
        copy = pltpu.make_async_remote_copy(
            src_ref=src,
            dst_ref=got.at[c, y],
            send_sem=send_sems.at[len(sends)],
            recv_sem=recv_sems.at[slot(c, y)],
            device_id=to,
            device_id_type=MESH,
        )
        copy.start()
        sends.append(copy)

    def receive(c, y):
        pltpu.make_async_remote_copy(
            src_ref=x_ref,
            dst_ref=got.at[c, y],
            send_sem=send_sems.at[0],
            recv_sem=recv_sems.at[slot(c, y)],
            device_id=device(c, y),
            device_id_type=MESH,
        ).wait_recv()

    for y in outer_peers:
        send(x_ref, ci, yo, device(ci, y))
    for c in inner_peers:
        send(x_ref, ci, yo, device(c, yo))
    o_ref[ci, yo] = x_ref[...]
    for k in range(1, n_outer):
        y = lax.rem(yo + n_outer - k, n_outer)
        receive(ci, y)
        for c in inner_peers:
            send(got.at[ci, y], ci, y, device(c, yo))
        o_ref[ci, y] = got[ci, y]
    for j in range(1, n_inner):
        c = lax.rem(ci + n_inner - j, n_inner)
        for k in range(n_outer):
            y = lax.rem(yo + k, n_outer)
            receive(c, y)
            o_ref[c, y] = got[c, y]
    for copy in sends:
        copy.wait_send()


def all_gather(x, axis, n, inner, collective_id):
    outer = n // inner
    shape = (inner, outer) + x.shape
    got = pl.pallas_call(
        functools.partial(_gather_kernel, outer, inner, axis),
        out_shape=jax.ShapeDtypeStruct(shape, x.dtype),
        in_specs=[pl.BlockSpec(memory_space=pltpu.VMEM)],
        out_specs=pl.BlockSpec(memory_space=pltpu.VMEM),
        scratch_shapes=[
            pltpu.VMEM(shape, x.dtype),
            pltpu.SemaphoreType.DMA((n,)),
            pltpu.SemaphoreType.DMA((n,)),
        ],
        compiler_params=pltpu.CompilerParams(
            collective_id=collective_id,
            has_side_effects=True,
            vmem_limit_bytes=min(3 * x.dtype.itemsize * math.prod(shape) + (8 << 20), 60 << 20),
        ),
    )(x)
    return got.reshape((n * x.shape[0],) + x.shape[1:])


def _reduce_kernel(n_o, s_o, n_i, s_i, chunks, axis, p_ref, o_ref, g1, b_ref, g2, s1, r1, s2, r2):
    me = lax.axis_index(axis)
    zi = lax.rem(lax.div(me, s_i), n_i)
    xo = lax.rem(lax.div(me, s_o), n_o)
    zc = n_i // chunks

    def device(x, z):
        return {axis: me + (x - xo) * s_o + (z - zi) * s_i}

    barrier = pltpu.get_barrier_semaphore()
    for k in range(1, n_o):
        pl.semaphore_signal(
            barrier, inc=1, device_id=device(lax.rem(xo + k, n_o), zi), device_id_type=MESH
        )
    for k in range(1, n_i):
        pl.semaphore_signal(
            barrier, inc=1, device_id=device(xo, lax.rem(zi + k, n_i)), device_id_type=MESH
        )
    pl.semaphore_wait(barrier, n_o + n_i - 2)

    def along_x(k, c, to, dst_x):
        blocks = pl.ds(c * zc, zc)
        return pltpu.make_async_remote_copy(
            src_ref=p_ref.at[to, blocks],
            dst_ref=g1.at[dst_x, blocks],
            send_sem=s1.at[k, c],
            recv_sem=r1.at[k, c],
            device_id=device(to, zi),
            device_id_type=MESH,
        )

    def along_z(k, z):
        return pltpu.make_async_remote_copy(
            src_ref=b_ref.at[z],
            dst_ref=g2.at[zi],
            send_sem=s2.at[k],
            recv_sem=r2.at[k],
            device_id=device(xo, z),
            device_id_type=MESH,
        )

    first = []
    for c in range(chunks):
        for k in range(1, n_o):
            copy = along_x(k, c, lax.rem(xo + k, n_o), xo)
            copy.start()
            first.append(copy)
    sources = [lax.rem(xo + n_o - k, n_o) for k in range(1, n_o)]
    for c in range(chunks):
        for k in range(1, n_o):
            pltpu.make_async_remote_copy(
                src_ref=p_ref.at[sources[k - 1], pl.ds(c * zc, zc)],
                dst_ref=g1.at[sources[k - 1], pl.ds(c * zc, zc)],
                send_sem=s1.at[k, c],
                recv_sem=r1.at[k, c],
                device_id=device(sources[k - 1], zi),
                device_id_type=MESH,
            ).wait_recv()
        for z in range(c * zc, (c + 1) * zc):
            total = p_ref[xo, z].astype(jnp.float32)
            for src in sources:
                total = total + g1[src, z].astype(jnp.float32)
            b_ref[z] = total.astype(b_ref.dtype)
            offset = lax.rem(z - zi + n_i, n_i)

            @pl.when(offset == 0)
            def _():
                o_ref[...] = total

            @pl.when(offset != 0)
            def _():
                along_z(offset, z).start()

    for k in range(1, n_i):
        src = lax.rem(zi + n_i - k, n_i)
        pltpu.make_async_remote_copy(
            src_ref=b_ref.at[src],
            dst_ref=g2.at[src],
            send_sem=s2.at[k],
            recv_sem=r2.at[k],
            device_id=device(xo, src),
            device_id_type=MESH,
        ).wait_recv()
        o_ref[...] = o_ref[...] + g2[src].astype(jnp.float32)
    for copy in first:
        copy.wait_send()
    for z in range(n_i):
        offset = lax.rem(z - zi + n_i, n_i)

        @pl.when(offset != 0)
        def _():
            along_z(offset, z).wait_send()


def reduce_scatter_2d(x, axis, first, second, collective_id):
    (n_o, s_o), (n_i, s_i) = first, second
    chunks = next(c for c in (4, 2, 1) if n_i % c == 0)
    return pl.pallas_call(
        functools.partial(_reduce_kernel, n_o, s_o, n_i, s_i, chunks, axis),
        out_shape=jax.ShapeDtypeStruct(x.shape[2:], jnp.float32),
        in_specs=[pl.BlockSpec(memory_space=pltpu.VMEM)],
        out_specs=pl.BlockSpec(memory_space=pltpu.VMEM),
        scratch_shapes=[
            pltpu.VMEM(x.shape, x.dtype),
            pltpu.VMEM(x.shape[1:], x.dtype),
            pltpu.VMEM(x.shape[1:], x.dtype),
            pltpu.SemaphoreType.DMA((n_o, chunks)),
            pltpu.SemaphoreType.DMA((n_o, chunks)),
            pltpu.SemaphoreType.DMA((n_i,)),
            pltpu.SemaphoreType.DMA((n_i,)),
        ],
        compiler_params=pltpu.CompilerParams(
            collective_id=collective_id,
            has_side_effects=True,
            vmem_limit_bytes=min(4 * x.dtype.itemsize * x.size + (8 << 20), 60 << 20),
        ),
    )(x)


def inner_size(devices):
    coords = [tuple(getattr(d, "coords", ())) for d in devices]
    if len(coords) < 2 or not coords[0]:
        return len(coords)
    varying = [c for c in range(len(coords[0])) if len({p[c] for p in coords}) > 1]
    slow = [c for c in varying if coords[1][c] == coords[0][c]]
    if not slow:
        return 1
    run = 0
    while run < len(coords) and coords[run][slow[0]] == coords[0][slow[0]]:
        run += 1
    return run


def per_device(n_sub, mass_inner, sub_inner, spectra, w_in, w_out, partner_rows, pair_counts, pair_labels):
    own_rows = spectra.shape[0]
    peers = partner_rows.shape[2]
    slots = partner_rows.shape[3]
    shard_rows = all_gather(spectra, "sub", n_sub, sub_inner, 2)
    pre = jnp.dot(shard_rows, w_in, preferred_element_type=jnp.float32)
    hidden = jax.nn.silu(pre).astype(jnp.bfloat16)
    embed_part = jnp.dot(hidden, w_out, preferred_element_type=jnp.float32)
    sub_outer = n_sub // sub_inner
    embed = reduce_scatter_2d(
        embed_part.reshape(sub_inner, sub_outer, own_rows, embed_part.shape[1]),
        "sub",
        (sub_inner, 1),
        (sub_outer, sub_inner),
        4,
    )
    norm = jnp.sqrt(jnp.sum(embed * embed, axis=-1, keepdims=True) + 1e-06)
    unit = embed / norm
    unit_b = unit.astype(jnp.bfloat16)
    flat_rows = partner_rows.reshape(peers * slots)
    selector = flat_rows[:, None] == jnp.arange(own_rows, dtype=jnp.int32)[None, :]
    mine = jnp.dot(
        selector.astype(jnp.bfloat16), unit_b, preferred_element_type=jnp.float32
    ).astype(jnp.bfloat16)
    outgoing = mine.reshape(peers, slots, mine.shape[1])
    incoming = exchange(outgoing, "mass", peers, 1)
    theirs = incoming.astype(jnp.float32)
    sim = jnp.sum(outgoing.astype(jnp.float32) * theirs, axis=-1)
    valid = jnp.arange(slots, dtype=jnp.int32)[None, :] < pair_counts.reshape(peers)[:, None]
    labels = pair_labels.reshape(peers, slots).astype(jnp.float32)
    coef = jnp.where(valid, 2.0 * (sim - labels), jnp.float32(0.0))
    weighted = (coef[..., None] * theirs).reshape(peers * slots, theirs.shape[2])
    grad_unit = lax.dot_general(
        selector.astype(jnp.float32),
        weighted,
        (((0,), (0,)), ((), ())),
        precision=lax.Precision.HIGHEST,
    )
    along = jnp.sum(unit * grad_unit, axis=-1, keepdims=True)
    grad_embed = ((grad_unit - unit * along) / norm).astype(jnp.bfloat16)
    grad_rows = all_gather(grad_embed, "sub", n_sub, sub_inner, 6)
    back = lax.dot_general(
        grad_rows, w_out, (((1,), (1,)), ((), ())), preferred_element_type=jnp.float32
    )
    gate = jax.nn.sigmoid(pre)
    grad_pre = lax.optimization_barrier(
        (back * gate * (1.0 + pre * (1.0 - gate))).astype(jnp.bfloat16)
    )
    out_part = lax.dot_general(
        grad_rows, hidden, (((0,), (0,)), ((), ())), preferred_element_type=jnp.float32
    )
    in_part_t = lax.dot_general(
        grad_pre, shard_rows, (((0,), (0,)), ((), ())), preferred_element_type=jnp.float32
    )
    n_mass = peers
    hid = in_part_t.shape[0]
    in_cols = in_part_t.shape[1] // n_mass
    out_rows = out_part.shape[0] // n_mass
    lanes = in_cols
    partial = jnp.concatenate(
        [
            jnp.swapaxes(in_part_t.astype(jnp.bfloat16).reshape(hid, n_mass, in_cols), 0, 1),
            out_part.astype(jnp.bfloat16).reshape(n_mass, out_rows * hid // lanes, lanes),
        ],
        axis=1,
    )
    mass_outer = n_mass // mass_inner
    summed = reduce_scatter_2d(
        partial.reshape((mass_outer, mass_inner) + partial.shape[1:]),
        "mass",
        (mass_outer, mass_inner),
        (mass_inner, 1),
        8,
    )
    grad_in = summed[:hid].T
    grad_out_t = summed[hid:].reshape(out_rows, hid)
    return (grad_in, grad_out_t)


def solution(mesh):
    placed = (
        P(("mass", "sub"), None),
        P(None, "sub"),
        P("sub", None),
        P("mass", "sub", None, None),
        P("mass", "sub", None),
        P("mass", "sub", None, None),
    )
    mass_inner = inner_size(list(mesh.devices[:, 0]))
    sub_inner = inner_size(list(mesh.devices[0, :]))
    return jax.shard_map(
        functools.partial(per_device, mesh.shape["sub"], mass_inner, sub_inner),
        mesh=mesh,
        in_specs=placed,
        out_specs=(P("mass", "sub"), P("mass", "sub")),
        check_vma=False,
    )
```

```python
import functools
import math

import jax
import jax.numpy as jnp
from jax import lax
from jax.experimental import pallas as pl
from jax.experimental.pallas import tpu as pltpu
from jax.sharding import PartitionSpec as P

MESH = pl.DeviceIdType.MESH


def _exchange_kernel(n, stride, axis, gather, x_ref, o_ref, got, send_sems, recv_sems):
    me = lax.axis_index(axis)
    mine = lax.rem(lax.div(me, stride), n)
    base = me - mine * stride

    def member(j):
        return base + j * stride

    barrier = pltpu.get_barrier_semaphore()
    for k in range(1, n):
        pl.semaphore_signal(
            barrier, inc=1, device_id={axis: member(lax.rem(mine + k, n))}, device_id_type=MESH
        )
    pl.semaphore_wait(barrier, n - 1)
    sends = []
    for k in range(1, n):
        peer = lax.rem(mine + k, n)
        copy = pltpu.make_async_remote_copy(
            src_ref=x_ref if gather else x_ref.at[peer],
            dst_ref=got.at[mine],
            send_sem=send_sems.at[k],
            recv_sem=recv_sems.at[k],
            device_id={axis: member(peer)},
            device_id_type=MESH,
        )
        copy.start()
        sends.append(copy)
    o_ref[mine] = x_ref[...] if gather else x_ref[mine]
    for k in range(1, n):
        sends[k - 1].wait_send()
        source = lax.rem(mine + n - k, n)
        pltpu.make_async_remote_copy(
            src_ref=x_ref if gather else x_ref.at[source],
            dst_ref=got.at[source],
            send_sem=send_sems.at[k],
            recv_sem=recv_sems.at[k],
            device_id={axis: member(source)},
            device_id_type=MESH,
        ).wait_recv()
        o_ref[source] = got[source]


def exchange(x, axis, n, collective_id, gather=False, stride=1):
    shape = (n,) + x.shape if gather else x.shape
    return pl.pallas_call(
        functools.partial(_exchange_kernel, n, stride, axis, gather),
        out_shape=jax.ShapeDtypeStruct(shape, x.dtype),
        in_specs=[pl.BlockSpec(memory_space=pltpu.VMEM)],
        out_specs=pl.BlockSpec(memory_space=pltpu.VMEM),
        scratch_shapes=[
            pltpu.VMEM(shape, x.dtype),
            pltpu.SemaphoreType.DMA((n,)),
            pltpu.SemaphoreType.DMA((n,)),
        ],
        compiler_params=pltpu.CompilerParams(
            collective_id=collective_id,
            has_side_effects=True,
            vmem_limit_bytes=min(3 * x.dtype.itemsize * math.prod(shape) + (8 << 20), 60 << 20),
        ),
    )(x)


def reduce_scatter(x, axis, inner, first_inner, first_id):
    outer = x.shape[0] // inner
    if first_inner:
        blocks = x.reshape((inner, outer) + x.shape[1:])
        phases = [(inner, 1), (outer, inner)]
    else:
        blocks = x.reshape((outer, inner) + x.shape[1:])
        phases = [(outer, inner), (inner, 1)]
    for number, (size, stride) in enumerate(phases):
        if size == 1:
            blocks = blocks[0].astype(jnp.float32)
            continue
        got = exchange(blocks.astype(x.dtype), axis, size, first_id + number, stride=stride)
        blocks = jnp.sum(got.astype(jnp.float32), axis=0)
    return blocks


def _gather_kernel(n_outer, n_inner, axis, x_ref, o_ref, got, send_sems, recv_sems):
    me = lax.axis_index(axis)
    ci = lax.rem(me, n_inner)
    yo = lax.div(me, n_inner)

    def device(c, y):
        return {axis: y * n_inner + c}

    def slot(c, y):
        return c * n_outer + y

    outer_peers = [lax.rem(yo + k, n_outer) for k in range(1, n_outer)]
    inner_peers = [lax.rem(ci + j, n_inner) for j in range(1, n_inner)]
    barrier = pltpu.get_barrier_semaphore()
    for y in outer_peers:
        pl.semaphore_signal(barrier, inc=1, device_id=device(ci, y), device_id_type=MESH)
    for c in inner_peers:
        pl.semaphore_signal(barrier, inc=1, device_id=device(c, yo), device_id_type=MESH)
    pl.semaphore_wait(barrier, len(outer_peers) + len(inner_peers))

    sends = []

    def send(src, c, y, to):
        copy = pltpu.make_async_remote_copy(
            src_ref=src,
            dst_ref=got.at[c, y],
            send_sem=send_sems.at[len(sends)],
            recv_sem=recv_sems.at[slot(c, y)],
            device_id=to,
            device_id_type=MESH,
        )
        copy.start()
        sends.append(copy)

    def receive(c, y):
        pltpu.make_async_remote_copy(
            src_ref=x_ref,
            dst_ref=got.at[c, y],
            send_sem=send_sems.at[0],
            recv_sem=recv_sems.at[slot(c, y)],
            device_id=device(c, y),
            device_id_type=MESH,
        ).wait_recv()

    for y in outer_peers:
        send(x_ref, ci, yo, device(ci, y))
    for c in inner_peers:
        send(x_ref, ci, yo, device(c, yo))
    o_ref[ci, yo] = x_ref[...]
    for k in range(1, n_outer):
        y = lax.rem(yo + n_outer - k, n_outer)
        receive(ci, y)
        for c in inner_peers:
            send(got.at[ci, y], ci, y, device(c, yo))
        o_ref[ci, y] = got[ci, y]
    for j in range(1, n_inner):
        c = lax.rem(ci + n_inner - j, n_inner)
        for k in range(n_outer):
            y = lax.rem(yo + k, n_outer)
            receive(c, y)
            o_ref[c, y] = got[c, y]
    for copy in sends:
        copy.wait_send()


def all_gather(x, axis, n, inner, collective_id):
    outer = n // inner
    shape = (inner, outer) + x.shape
    got = pl.pallas_call(
        functools.partial(_gather_kernel, outer, inner, axis),
        out_shape=jax.ShapeDtypeStruct(shape, x.dtype),
        in_specs=[pl.BlockSpec(memory_space=pltpu.VMEM)],
        out_specs=pl.BlockSpec(memory_space=pltpu.VMEM),
        scratch_shapes=[
            pltpu.VMEM(shape, x.dtype),
            pltpu.SemaphoreType.DMA((n,)),
            pltpu.SemaphoreType.DMA((n,)),
        ],
        compiler_params=pltpu.CompilerParams(
            collective_id=collective_id,
            has_side_effects=True,
            vmem_limit_bytes=min(3 * x.dtype.itemsize * math.prod(shape) + (8 << 20), 60 << 20),
        ),
    )(x)
    return got.reshape((n * x.shape[0],) + x.shape[1:])


def _reduce_kernel(n_o, s_o, n_i, s_i, chunks, axis, p_ref, o_ref, g1, b_ref, g2, s1, r1, s2, r2):
    me = lax.axis_index(axis)
    zi = lax.rem(lax.div(me, s_i), n_i)
    xo = lax.rem(lax.div(me, s_o), n_o)
    zc = n_i // chunks

    def device(x, z):
        return {axis: me + (x - xo) * s_o + (z - zi) * s_i}

    barrier = pltpu.get_barrier_semaphore()
    for k in range(1, n_o):
        pl.semaphore_signal(
            barrier, inc=1, device_id=device(lax.rem(xo + k, n_o), zi), device_id_type=MESH
        )
    for k in range(1, n_i):
        pl.semaphore_signal(
            barrier, inc=1, device_id=device(xo, lax.rem(zi + k, n_i)), device_id_type=MESH
        )
    pl.semaphore_wait(barrier, n_o + n_i - 2)

    def along_x(k, c, to, dst_x):
        blocks = pl.ds(c * zc, zc)
        return pltpu.make_async_remote_copy(
            src_ref=p_ref.at[to, blocks],
            dst_ref=g1.at[dst_x, blocks],
            send_sem=s1.at[k, c],
            recv_sem=r1.at[k, c],
            device_id=device(to, zi),
            device_id_type=MESH,
        )

    def along_z(k, z):
        return pltpu.make_async_remote_copy(
            src_ref=b_ref.at[z],
            dst_ref=g2.at[zi],
            send_sem=s2.at[k],
            recv_sem=r2.at[k],
            device_id=device(xo, z),
            device_id_type=MESH,
        )

    first = []
    for c in range(chunks):
        for k in range(1, n_o):
            copy = along_x(k, c, lax.rem(xo + k, n_o), xo)
            copy.start()
            first.append(copy)
    sources = [lax.rem(xo + n_o - k, n_o) for k in range(1, n_o)]
    for c in range(chunks):
        for k in range(1, n_o):
            pltpu.make_async_remote_copy(
                src_ref=p_ref.at[sources[k - 1], pl.ds(c * zc, zc)],
                dst_ref=g1.at[sources[k - 1], pl.ds(c * zc, zc)],
                send_sem=s1.at[k, c],
                recv_sem=r1.at[k, c],
                device_id=device(sources[k - 1], zi),
                device_id_type=MESH,
            ).wait_recv()
        for z in range(c * zc, (c + 1) * zc):
            total = p_ref[xo, z].astype(jnp.float32)
            for src in sources:
                total = total + g1[src, z].astype(jnp.float32)
            b_ref[z] = total.astype(b_ref.dtype)
            offset = lax.rem(z - zi + n_i, n_i)

            @pl.when(offset == 0)
            def _():
                o_ref[...] = total

            @pl.when(offset != 0)
            def _():
                along_z(offset, z).start()

    for k in range(1, n_i):
        src = lax.rem(zi + n_i - k, n_i)
        pltpu.make_async_remote_copy(
            src_ref=b_ref.at[src],
            dst_ref=g2.at[src],
            send_sem=s2.at[k],
            recv_sem=r2.at[k],
            device_id=device(xo, src),
            device_id_type=MESH,
        ).wait_recv()
        o_ref[...] = o_ref[...] + g2[src].astype(jnp.float32)
    for copy in first:
        copy.wait_send()
    for z in range(n_i):
        offset = lax.rem(z - zi + n_i, n_i)

        @pl.when(offset != 0)
        def _():
            along_z(offset, z).wait_send()


def reduce_scatter_2d(x, axis, first, second, collective_id):
    (n_o, s_o), (n_i, s_i) = first, second
    chunks = next(c for c in (8, 4, 2, 1) if n_i % c == 0)
    return pl.pallas_call(
        functools.partial(_reduce_kernel, n_o, s_o, n_i, s_i, chunks, axis),
        out_shape=jax.ShapeDtypeStruct(x.shape[2:], jnp.float32),
        in_specs=[pl.BlockSpec(memory_space=pltpu.VMEM)],
        out_specs=pl.BlockSpec(memory_space=pltpu.VMEM),
        scratch_shapes=[
            pltpu.VMEM(x.shape, x.dtype),
            pltpu.VMEM(x.shape[1:], x.dtype),
            pltpu.VMEM(x.shape[1:], x.dtype),
            pltpu.SemaphoreType.DMA((n_o, chunks)),
            pltpu.SemaphoreType.DMA((n_o, chunks)),
            pltpu.SemaphoreType.DMA((n_i,)),
            pltpu.SemaphoreType.DMA((n_i,)),
        ],
        compiler_params=pltpu.CompilerParams(
            collective_id=collective_id,
            has_side_effects=True,
            vmem_limit_bytes=min(4 * x.dtype.itemsize * x.size + (8 << 20), 60 << 20),
        ),
    )(x)


def inner_size(devices):
    coords = [tuple(getattr(d, "coords", ())) for d in devices]
    if len(coords) < 2 or not coords[0]:
        return len(coords)
    varying = [c for c in range(len(coords[0])) if len({p[c] for p in coords}) > 1]
    slow = [c for c in varying if coords[1][c] == coords[0][c]]
    if not slow:
        return 1
    run = 0
    while run < len(coords) and coords[run][slow[0]] == coords[0][slow[0]]:
        run += 1
    return run


def per_device(n_sub, mass_inner, sub_inner, spectra, w_in, w_out, partner_rows, pair_counts, pair_labels):
    own_rows = spectra.shape[0]
    peers = partner_rows.shape[2]
    slots = partner_rows.shape[3]
    shard_rows = all_gather(spectra, "sub", n_sub, sub_inner, 2)
    pre = jnp.dot(shard_rows, w_in, preferred_element_type=jnp.float32)
    hidden = jax.nn.silu(pre).astype(jnp.bfloat16)
    embed_part = jnp.dot(hidden, w_out, preferred_element_type=jnp.float32)
    sub_outer = n_sub // sub_inner
    embed = reduce_scatter_2d(
        embed_part.reshape(sub_inner, sub_outer, own_rows, embed_part.shape[1]),
        "sub",
        (sub_inner, 1),
        (sub_outer, sub_inner),
        4,
    )
    norm = jnp.sqrt(jnp.sum(embed * embed, axis=-1, keepdims=True) + 1e-06)
    unit = embed / norm
    unit_b = unit.astype(jnp.bfloat16)
    flat_rows = partner_rows.reshape(peers * slots)
    selector = flat_rows[:, None] == jnp.arange(own_rows, dtype=jnp.int32)[None, :]
    mine = jnp.dot(
        selector.astype(jnp.bfloat16), unit_b, preferred_element_type=jnp.float32
    ).astype(jnp.bfloat16)
    outgoing = mine.reshape(peers, slots, mine.shape[1])
    incoming = exchange(outgoing, "mass", peers, 1)
    theirs = incoming.astype(jnp.float32)
    sim = jnp.sum(outgoing.astype(jnp.float32) * theirs, axis=-1)
    valid = jnp.arange(slots, dtype=jnp.int32)[None, :] < pair_counts.reshape(peers)[:, None]
    labels = pair_labels.reshape(peers, slots).astype(jnp.float32)
    coef = jnp.where(valid, 2.0 * (sim - labels), jnp.float32(0.0))
    weighted = (coef[..., None] * theirs).reshape(peers * slots, theirs.shape[2])
    grad_unit = lax.dot_general(
        selector.astype(jnp.float32),
        weighted,
        (((0,), (0,)), ((), ())),
        precision=lax.Precision.HIGHEST,
    )
    along = jnp.sum(unit * grad_unit, axis=-1, keepdims=True)
    grad_embed = ((grad_unit - unit * along) / norm).astype(jnp.bfloat16)
    grad_rows = all_gather(grad_embed, "sub", n_sub, sub_inner, 6)
    back = lax.dot_general(
        grad_rows, w_out, (((1,), (1,)), ((), ())), preferred_element_type=jnp.float32
    )
    gate = jax.nn.sigmoid(pre)
    grad_pre = lax.optimization_barrier(
        (back * gate * (1.0 + pre * (1.0 - gate))).astype(jnp.bfloat16)
    )
    out_part = lax.dot_general(
        grad_rows, hidden, (((0,), (0,)), ((), ())), preferred_element_type=jnp.float32
    )
    in_part_t = lax.dot_general(
        grad_pre, shard_rows, (((0,), (0,)), ((), ())), preferred_element_type=jnp.float32
    )
    n_mass = peers
    hid = in_part_t.shape[0]
    in_cols = in_part_t.shape[1] // n_mass
    out_rows = out_part.shape[0] // n_mass
    lanes = in_cols
    partial = jnp.concatenate(
        [
            jnp.swapaxes(in_part_t.astype(jnp.bfloat16).reshape(hid, n_mass, in_cols), 0, 1),
            out_part.astype(jnp.bfloat16).reshape(n_mass, out_rows * hid // lanes, lanes),
        ],
        axis=1,
    )
    mass_outer = n_mass // mass_inner
    summed = reduce_scatter_2d(
        partial.reshape((mass_outer, mass_inner) + partial.shape[1:]),
        "mass",
        (mass_outer, mass_inner),
        (mass_inner, 1),
        8,
    )
    grad_in = summed[:hid].T
    grad_out_t = summed[hid:].reshape(out_rows, hid)
    return (grad_in, grad_out_t)


def solution(mesh):
    placed = (
        P(("mass", "sub"), None),
        P(None, "sub"),
        P("sub", None),
        P("mass", "sub", None, None),
        P("mass", "sub", None),
        P("mass", "sub", None, None),
    )
    mass_inner = inner_size(list(mesh.devices[:, 0]))
    sub_inner = inner_size(list(mesh.devices[0, :]))
    return jax.shard_map(
        functools.partial(per_device, mesh.shape["sub"], mass_inner, sub_inner),
        mesh=mesh,
        in_specs=placed,
        out_specs=(P("mass", "sub"), P("mass", "sub")),
        check_vma=False,
    )
```

```python
import functools
import math

import jax
import jax.numpy as jnp
from jax import lax
from jax.experimental import pallas as pl
from jax.experimental.pallas import tpu as pltpu
from jax.sharding import PartitionSpec as P

MESH = pl.DeviceIdType.MESH


def _exchange_kernel(n, stride, axis, gather, x_ref, o_ref, got, send_sems, recv_sems):
    me = lax.axis_index(axis)
    mine = lax.rem(lax.div(me, stride), n)
    base = me - mine * stride

    def member(j):
        return base + j * stride

    barrier = pltpu.get_barrier_semaphore()
    for k in range(1, n):
        pl.semaphore_signal(
            barrier, inc=1, device_id={axis: member(lax.rem(mine + k, n))}, device_id_type=MESH
        )
    pl.semaphore_wait(barrier, n - 1)
    sends = []
    for k in range(1, n):
        peer = lax.rem(mine + k, n)
        copy = pltpu.make_async_remote_copy(
            src_ref=x_ref if gather else x_ref.at[peer],
            dst_ref=got.at[mine],
            send_sem=send_sems.at[k],
            recv_sem=recv_sems.at[k],
            device_id={axis: member(peer)},
            device_id_type=MESH,
        )
        copy.start()
        sends.append(copy)
    o_ref[mine] = x_ref[...] if gather else x_ref[mine]
    for k in range(1, n):
        sends[k - 1].wait_send()
        source = lax.rem(mine + n - k, n)
        pltpu.make_async_remote_copy(
            src_ref=x_ref if gather else x_ref.at[source],
            dst_ref=got.at[source],
            send_sem=send_sems.at[k],
            recv_sem=recv_sems.at[k],
            device_id={axis: member(source)},
            device_id_type=MESH,
        ).wait_recv()
        o_ref[source] = got[source]


def exchange(x, axis, n, collective_id, gather=False, stride=1):
    shape = (n,) + x.shape if gather else x.shape
    return pl.pallas_call(
        functools.partial(_exchange_kernel, n, stride, axis, gather),
        out_shape=jax.ShapeDtypeStruct(shape, x.dtype),
        in_specs=[pl.BlockSpec(memory_space=pltpu.VMEM)],
        out_specs=pl.BlockSpec(memory_space=pltpu.VMEM),
        scratch_shapes=[
            pltpu.VMEM(shape, x.dtype),
            pltpu.SemaphoreType.DMA((n,)),
            pltpu.SemaphoreType.DMA((n,)),
        ],
        compiler_params=pltpu.CompilerParams(
            collective_id=collective_id,
            has_side_effects=True,
            vmem_limit_bytes=min(3 * x.dtype.itemsize * math.prod(shape) + (8 << 20), 60 << 20),
        ),
    )(x)


def reduce_scatter(x, axis, inner, first_inner, first_id):
    outer = x.shape[0] // inner
    if first_inner:
        blocks = x.reshape((inner, outer) + x.shape[1:])
        phases = [(inner, 1), (outer, inner)]
    else:
        blocks = x.reshape((outer, inner) + x.shape[1:])
        phases = [(outer, inner), (inner, 1)]
    for number, (size, stride) in enumerate(phases):
        if size == 1:
            blocks = blocks[0].astype(jnp.float32)
            continue
        got = exchange(blocks.astype(x.dtype), axis, size, first_id + number, stride=stride)
        blocks = jnp.sum(got.astype(jnp.float32), axis=0)
    return blocks


def _gather_kernel(n_outer, n_inner, axis, x_ref, o_ref, got, send_sems, recv_sems, local_sems):
    me = lax.axis_index(axis)
    ci = lax.rem(me, n_inner)
    yo = lax.div(me, n_inner)

    def device(c, y):
        return {axis: y * n_inner + c}

    def slot(c, y):
        return c * n_outer + y

    outer_peers = [lax.rem(yo + k, n_outer) for k in range(1, n_outer)]
    inner_peers = [lax.rem(ci + j, n_inner) for j in range(1, n_inner)]
    barrier = pltpu.get_barrier_semaphore()
    for y in outer_peers:
        pl.semaphore_signal(barrier, inc=1, device_id=device(ci, y), device_id_type=MESH)
    for c in inner_peers:
        pl.semaphore_signal(barrier, inc=1, device_id=device(c, yo), device_id_type=MESH)
    pl.semaphore_wait(barrier, len(outer_peers) + len(inner_peers))

    sends = []

    def send(src, c, y, to):
        copy = pltpu.make_async_remote_copy(
            src_ref=src,
            dst_ref=got.at[c, y],
            send_sem=send_sems.at[len(sends)],
            recv_sem=recv_sems.at[slot(c, y)],
            device_id=to,
            device_id_type=MESH,
        )
        copy.start()
        sends.append(copy)

    def receive(c, y):
        pltpu.make_async_remote_copy(
            src_ref=x_ref,
            dst_ref=got.at[c, y],
            send_sem=send_sems.at[0],
            recv_sem=recv_sems.at[slot(c, y)],
            device_id=device(c, y),
            device_id_type=MESH,
        ).wait_recv()

    locals_ = []

    def keep(src, c, y):
        copy = pltpu.make_async_copy(src, o_ref.at[c, y], local_sems.at[slot(c, y)])
        copy.start()
        locals_.append(copy)

    for y in outer_peers:
        send(x_ref, ci, yo, device(ci, y))
    for c in inner_peers:
        send(x_ref, ci, yo, device(c, yo))
    keep(x_ref, ci, yo)
    for k in range(1, n_outer):
        y = lax.rem(yo + n_outer - k, n_outer)
        receive(ci, y)
        for c in inner_peers:
            send(got.at[ci, y], ci, y, device(c, yo))
        keep(got.at[ci, y], ci, y)
    for j in range(1, n_inner):
        c = lax.rem(ci + n_inner - j, n_inner)
        for k in range(n_outer):
            y = lax.rem(yo + k, n_outer)
            receive(c, y)
            keep(got.at[c, y], c, y)
    for copy in sends:
        copy.wait_send()
    for copy in locals_:
        copy.wait()


def all_gather(x, axis, n, inner, collective_id):
    outer = n // inner
    shape = (inner, outer) + x.shape
    got = pl.pallas_call(
        functools.partial(_gather_kernel, outer, inner, axis),
        out_shape=jax.ShapeDtypeStruct(shape, x.dtype),
        in_specs=[pl.BlockSpec(memory_space=pltpu.VMEM)],
        out_specs=pl.BlockSpec(memory_space=pltpu.VMEM),
        scratch_shapes=[
            pltpu.VMEM(shape, x.dtype),
            pltpu.SemaphoreType.DMA((n,)),
            pltpu.SemaphoreType.DMA((n,)),
            pltpu.SemaphoreType.DMA((n,)),
        ],
        compiler_params=pltpu.CompilerParams(
            collective_id=collective_id,
            has_side_effects=True,
            vmem_limit_bytes=min(3 * x.dtype.itemsize * math.prod(shape) + (8 << 20), 60 << 20),
        ),
    )(x)
    return got.reshape((n * x.shape[0],) + x.shape[1:])


def _reduce_kernel(n_o, s_o, n_i, s_i, chunks, axis, p_ref, o_ref, g1, b_ref, g2, s1, r1, s2, r2):
    me = lax.axis_index(axis)
    zi = lax.rem(lax.div(me, s_i), n_i)
    xo = lax.rem(lax.div(me, s_o), n_o)
    zc = n_i // chunks

    def device(x, z):
        return {axis: me + (x - xo) * s_o + (z - zi) * s_i}

    barrier = pltpu.get_barrier_semaphore()
    for k in range(1, n_o):
        pl.semaphore_signal(
            barrier, inc=1, device_id=device(lax.rem(xo + k, n_o), zi), device_id_type=MESH
        )
    for k in range(1, n_i):
        pl.semaphore_signal(
            barrier, inc=1, device_id=device(xo, lax.rem(zi + k, n_i)), device_id_type=MESH
        )
    pl.semaphore_wait(barrier, n_o + n_i - 2)

    def along_x(k, c, to, dst_x):
        blocks = pl.ds(c * zc, zc)
        return pltpu.make_async_remote_copy(
            src_ref=p_ref.at[to, blocks],
            dst_ref=g1.at[dst_x, blocks],
            send_sem=s1.at[k, c],
            recv_sem=r1.at[k, c],
            device_id=device(to, zi),
            device_id_type=MESH,
        )

    def along_z(k, z):
        return pltpu.make_async_remote_copy(
            src_ref=b_ref.at[z],
            dst_ref=g2.at[zi],
            send_sem=s2.at[k],
            recv_sem=r2.at[k],
            device_id=device(xo, z),
            device_id_type=MESH,
        )

    first = []
    for c in range(chunks):
        for k in range(1, n_o):
            copy = along_x(k, c, lax.rem(xo + k, n_o), xo)
            copy.start()
            first.append(copy)
    sources = [lax.rem(xo + n_o - k, n_o) for k in range(1, n_o)]
    for c in range(chunks):
        for k in range(1, n_o):
            pltpu.make_async_remote_copy(
                src_ref=p_ref.at[sources[k - 1], pl.ds(c * zc, zc)],
                dst_ref=g1.at[sources[k - 1], pl.ds(c * zc, zc)],
                send_sem=s1.at[k, c],
                recv_sem=r1.at[k, c],
                device_id=device(sources[k - 1], zi),
                device_id_type=MESH,
            ).wait_recv()
        for z in range(c * zc, (c + 1) * zc):
            total = p_ref[xo, z].astype(jnp.float32)
            for src in sources:
                total = total + g1[src, z].astype(jnp.float32)
            b_ref[z] = total.astype(b_ref.dtype)
            offset = lax.rem(z - zi + n_i, n_i)

            @pl.when(offset == 0)
            def _():
                o_ref[...] = total

            @pl.when(offset != 0)
            def _():
                along_z(offset, z).start()

    for k in range(1, n_i):
        src = lax.rem(zi + n_i - k, n_i)
        pltpu.make_async_remote_copy(
            src_ref=b_ref.at[src],
            dst_ref=g2.at[src],
            send_sem=s2.at[k],
            recv_sem=r2.at[k],
            device_id=device(xo, src),
            device_id_type=MESH,
        ).wait_recv()
        o_ref[...] = o_ref[...] + g2[src].astype(jnp.float32)
    for copy in first:
        copy.wait_send()
    for z in range(n_i):
        offset = lax.rem(z - zi + n_i, n_i)

        @pl.when(offset != 0)
        def _():
            along_z(offset, z).wait_send()


def reduce_scatter_2d(x, axis, first, second, collective_id):
    (n_o, s_o), (n_i, s_i) = first, second
    chunks = next(c for c in (8, 4, 2, 1) if n_i % c == 0)
    return pl.pallas_call(
        functools.partial(_reduce_kernel, n_o, s_o, n_i, s_i, chunks, axis),
        out_shape=jax.ShapeDtypeStruct(x.shape[2:], jnp.float32),
        in_specs=[pl.BlockSpec(memory_space=pltpu.VMEM)],
        out_specs=pl.BlockSpec(memory_space=pltpu.VMEM),
        scratch_shapes=[
            pltpu.VMEM(x.shape, x.dtype),
            pltpu.VMEM(x.shape[1:], x.dtype),
            pltpu.VMEM(x.shape[1:], x.dtype),
            pltpu.SemaphoreType.DMA((n_o, chunks)),
            pltpu.SemaphoreType.DMA((n_o, chunks)),
            pltpu.SemaphoreType.DMA((n_i,)),
            pltpu.SemaphoreType.DMA((n_i,)),
        ],
        compiler_params=pltpu.CompilerParams(
            collective_id=collective_id,
            has_side_effects=True,
            vmem_limit_bytes=min(4 * x.dtype.itemsize * x.size + (8 << 20), 60 << 20),
        ),
    )(x)


def inner_size(devices):
    coords = [tuple(getattr(d, "coords", ())) for d in devices]
    if len(coords) < 2 or not coords[0]:
        return len(coords)
    varying = [c for c in range(len(coords[0])) if len({p[c] for p in coords}) > 1]
    slow = [c for c in varying if coords[1][c] == coords[0][c]]
    if not slow:
        return 1
    run = 0
    while run < len(coords) and coords[run][slow[0]] == coords[0][slow[0]]:
        run += 1
    return run


def per_device(n_sub, mass_inner, sub_inner, spectra, w_in, w_out, partner_rows, pair_counts, pair_labels):
    own_rows = spectra.shape[0]
    peers = partner_rows.shape[2]
    slots = partner_rows.shape[3]
    shard_rows = all_gather(spectra, "sub", n_sub, sub_inner, 2)
    pre = jnp.dot(shard_rows, w_in, preferred_element_type=jnp.float32)
    hidden = jax.nn.silu(pre).astype(jnp.bfloat16)
    embed_part = jnp.dot(hidden, w_out, preferred_element_type=jnp.float32)
    sub_outer = n_sub // sub_inner
    embed = reduce_scatter_2d(
        embed_part.reshape(sub_inner, sub_outer, own_rows, embed_part.shape[1]),
        "sub",
        (sub_inner, 1),
        (sub_outer, sub_inner),
        4,
    )
    norm = jnp.sqrt(jnp.sum(embed * embed, axis=-1, keepdims=True) + 1e-06)
    unit = embed / norm
    unit_b = unit.astype(jnp.bfloat16)
    flat_rows = partner_rows.reshape(peers * slots)
    selector = flat_rows[:, None] == jnp.arange(own_rows, dtype=jnp.int32)[None, :]
    mine = jnp.dot(
        selector.astype(jnp.bfloat16), unit_b, preferred_element_type=jnp.float32
    ).astype(jnp.bfloat16)
    outgoing = mine.reshape(peers, slots, mine.shape[1])
    incoming = exchange(outgoing, "mass", peers, 1)
    theirs = incoming.astype(jnp.float32)
    sim = jnp.sum(outgoing.astype(jnp.float32) * theirs, axis=-1)
    valid = jnp.arange(slots, dtype=jnp.int32)[None, :] < pair_counts.reshape(peers)[:, None]
    labels = pair_labels.reshape(peers, slots).astype(jnp.float32)
    coef = jnp.where(valid, 2.0 * (sim - labels), jnp.float32(0.0))
    weighted = (coef[..., None] * theirs).reshape(peers * slots, theirs.shape[2])
    grad_unit = lax.dot_general(
        selector.astype(jnp.float32),
        weighted,
        (((0,), (0,)), ((), ())),
        precision=lax.Precision.HIGHEST,
    )
    along = jnp.sum(unit * grad_unit, axis=-1, keepdims=True)
    grad_embed = ((grad_unit - unit * along) / norm).astype(jnp.bfloat16)
    grad_rows = all_gather(grad_embed, "sub", n_sub, sub_inner, 6)
    back = lax.dot_general(
        grad_rows, w_out, (((1,), (1,)), ((), ())), preferred_element_type=jnp.float32
    )
    gate = jax.nn.sigmoid(pre)
    grad_pre = lax.optimization_barrier(
        (back * gate * (1.0 + pre * (1.0 - gate))).astype(jnp.bfloat16)
    )
    out_part = lax.dot_general(
        grad_rows, hidden, (((0,), (0,)), ((), ())), preferred_element_type=jnp.float32
    )
    in_part_t = lax.dot_general(
        grad_pre, shard_rows, (((0,), (0,)), ((), ())), preferred_element_type=jnp.float32
    )
    n_mass = peers
    hid = in_part_t.shape[0]
    in_cols = in_part_t.shape[1] // n_mass
    out_rows = out_part.shape[0] // n_mass
    lanes = in_cols
    partial = jnp.concatenate(
        [
            jnp.swapaxes(in_part_t.astype(jnp.bfloat16).reshape(hid, n_mass, in_cols), 0, 1),
            out_part.astype(jnp.bfloat16).reshape(n_mass, out_rows * hid // lanes, lanes),
        ],
        axis=1,
    )
    mass_outer = n_mass // mass_inner
    summed = reduce_scatter_2d(
        partial.reshape((mass_outer, mass_inner) + partial.shape[1:]),
        "mass",
        (mass_outer, mass_inner),
        (mass_inner, 1),
        8,
    )
    grad_in = summed[:hid].T
    grad_out_t = summed[hid:].reshape(out_rows, hid)
    return (grad_in, grad_out_t)


def solution(mesh):
    placed = (
        P(("mass", "sub"), None),
        P(None, "sub"),
        P("sub", None),
        P("mass", "sub", None, None),
        P("mass", "sub", None),
        P("mass", "sub", None, None),
    )
    mass_inner = inner_size(list(mesh.devices[:, 0]))
    sub_inner = inner_size(list(mesh.devices[0, :]))
    return jax.shard_map(
        functools.partial(per_device, mesh.shape["sub"], mass_inner, sub_inner),
        mesh=mesh,
        in_specs=placed,
        out_specs=(P("mass", "sub"), P("mass", "sub")),
        check_vma=False,
    )
```

```python
import functools
import math

import jax
import jax.numpy as jnp
from jax import lax
from jax.experimental import pallas as pl
from jax.experimental.pallas import tpu as pltpu
from jax.sharding import PartitionSpec as P

MESH = pl.DeviceIdType.MESH


def _exchange_kernel(n, stride, axis, gather, x_ref, o_ref, got, send_sems, recv_sems):
    me = lax.axis_index(axis)
    mine = lax.rem(lax.div(me, stride), n)
    base = me - mine * stride

    def member(j):
        return base + j * stride

    barrier = pltpu.get_barrier_semaphore()
    for k in range(1, n):
        pl.semaphore_signal(
            barrier, inc=1, device_id={axis: member(lax.rem(mine + k, n))}, device_id_type=MESH
        )
    pl.semaphore_wait(barrier, n - 1)
    sends = []
    for k in range(1, n):
        peer = lax.rem(mine + k, n)
        copy = pltpu.make_async_remote_copy(
            src_ref=x_ref if gather else x_ref.at[peer],
            dst_ref=got.at[mine],
            send_sem=send_sems.at[k],
            recv_sem=recv_sems.at[k],
            device_id={axis: member(peer)},
            device_id_type=MESH,
        )
        copy.start()
        sends.append(copy)
    o_ref[mine] = x_ref[...] if gather else x_ref[mine]
    for k in range(1, n):
        sends[k - 1].wait_send()
        source = lax.rem(mine + n - k, n)
        pltpu.make_async_remote_copy(
            src_ref=x_ref if gather else x_ref.at[source],
            dst_ref=got.at[source],
            send_sem=send_sems.at[k],
            recv_sem=recv_sems.at[k],
            device_id={axis: member(source)},
            device_id_type=MESH,
        ).wait_recv()
        o_ref[source] = got[source]


def exchange(x, axis, n, collective_id, gather=False, stride=1):
    shape = (n,) + x.shape if gather else x.shape
    return pl.pallas_call(
        functools.partial(_exchange_kernel, n, stride, axis, gather),
        out_shape=jax.ShapeDtypeStruct(shape, x.dtype),
        in_specs=[pl.BlockSpec(memory_space=pltpu.VMEM)],
        out_specs=pl.BlockSpec(memory_space=pltpu.VMEM),
        scratch_shapes=[
            pltpu.VMEM(shape, x.dtype),
            pltpu.SemaphoreType.DMA((n,)),
            pltpu.SemaphoreType.DMA((n,)),
        ],
        compiler_params=pltpu.CompilerParams(
            collective_id=collective_id,
            has_side_effects=True,
            vmem_limit_bytes=min(3 * x.dtype.itemsize * math.prod(shape) + (8 << 20), 60 << 20),
        ),
    )(x)


def reduce_scatter(x, axis, inner, first_inner, first_id):
    outer = x.shape[0] // inner
    if first_inner:
        blocks = x.reshape((inner, outer) + x.shape[1:])
        phases = [(inner, 1), (outer, inner)]
    else:
        blocks = x.reshape((outer, inner) + x.shape[1:])
        phases = [(outer, inner), (inner, 1)]
    for number, (size, stride) in enumerate(phases):
        if size == 1:
            blocks = blocks[0].astype(jnp.float32)
            continue
        got = exchange(blocks.astype(x.dtype), axis, size, first_id + number, stride=stride)
        blocks = jnp.sum(got.astype(jnp.float32), axis=0)
    return blocks


def _gather_kernel(n_outer, n_inner, axis, x_ref, o_ref, got, send_sems, recv_sems, own):
    me = lax.axis_index(axis)
    ci = lax.rem(me, n_inner)
    yo = lax.div(me, n_inner)

    def device(c, y):
        return {axis: y * n_inner + c}

    def slot(c, y):
        return c * n_outer + y

    outer_peers = [lax.rem(yo + k, n_outer) for k in range(1, n_outer)]
    inner_peers = [lax.rem(ci + j, n_inner) for j in range(1, n_inner)]
    barrier = pltpu.get_barrier_semaphore()
    for y in outer_peers:
        pl.semaphore_signal(barrier, inc=1, device_id=device(ci, y), device_id_type=MESH)
    for c in inner_peers:
        pl.semaphore_signal(barrier, inc=1, device_id=device(c, yo), device_id_type=MESH)
    pl.semaphore_wait(barrier, len(outer_peers) + len(inner_peers))

    sends = []

    def send(src, c, y, to):
        copy = pltpu.make_async_remote_copy(
            src_ref=src,
            dst_ref=got.at[c, y],
            send_sem=send_sems.at[len(sends)],
            recv_sem=recv_sems.at[slot(c, y)],
            device_id=to,
            device_id_type=MESH,
        )
        copy.start()
        sends.append(copy)

    def receive(c, y):
        pltpu.make_async_remote_copy(
            src_ref=x_ref,
            dst_ref=got.at[c, y],
            send_sem=send_sems.at[0],
            recv_sem=recv_sems.at[slot(c, y)],
            device_id=device(c, y),
            device_id_type=MESH,
        ).wait_recv()

    for y in outer_peers:
        send(x_ref, ci, yo, device(ci, y))
    for c in inner_peers:
        send(x_ref, ci, yo, device(c, yo))
    mine = pltpu.make_async_copy(x_ref, o_ref.at[ci, yo], own)
    mine.start()
    for k in range(1, n_outer):
        y = lax.rem(yo + n_outer - k, n_outer)
        receive(ci, y)
        for c in inner_peers:
            send(got.at[ci, y], ci, y, device(c, yo))
        o_ref[ci, y] = got[ci, y]
    for j in range(1, n_inner):
        c = lax.rem(ci + n_inner - j, n_inner)
        for k in range(n_outer):
            y = lax.rem(yo + k, n_outer)
            receive(c, y)
            o_ref[c, y] = got[c, y]
    for copy in sends:
        copy.wait_send()
    mine.wait()


def all_gather(x, axis, n, inner, collective_id):
    outer = n // inner
    shape = (inner, outer) + x.shape
    got = pl.pallas_call(
        functools.partial(_gather_kernel, outer, inner, axis),
        out_shape=jax.ShapeDtypeStruct(shape, x.dtype),
        in_specs=[pl.BlockSpec(memory_space=pl.ANY)],
        out_specs=pl.BlockSpec(memory_space=pltpu.VMEM),
        scratch_shapes=[
            pltpu.VMEM(shape, x.dtype),
            pltpu.SemaphoreType.DMA((n,)),
            pltpu.SemaphoreType.DMA((n,)),
            pltpu.SemaphoreType.DMA(()),
        ],
        compiler_params=pltpu.CompilerParams(
            collective_id=collective_id,
            has_side_effects=True,
            vmem_limit_bytes=min(3 * x.dtype.itemsize * math.prod(shape) + (8 << 20), 60 << 20),
        ),
    )(x)
    return got.reshape((n * x.shape[0],) + x.shape[1:])


def _reduce_kernel(n_o, s_o, n_i, s_i, chunks, axis, p_ref, o_ref, g1, b_ref, g2, s1, r1, s2, r2):
    me = lax.axis_index(axis)
    zi = lax.rem(lax.div(me, s_i), n_i)
    xo = lax.rem(lax.div(me, s_o), n_o)
    zc = n_i // chunks

    def device(x, z):
        return {axis: me + (x - xo) * s_o + (z - zi) * s_i}

    barrier = pltpu.get_barrier_semaphore()
    for k in range(1, n_o):
        pl.semaphore_signal(
            barrier, inc=1, device_id=device(lax.rem(xo + k, n_o), zi), device_id_type=MESH
        )
    for k in range(1, n_i):
        pl.semaphore_signal(
            barrier, inc=1, device_id=device(xo, lax.rem(zi + k, n_i)), device_id_type=MESH
        )
    pl.semaphore_wait(barrier, n_o + n_i - 2)

    def along_x(k, c, to, dst_x):
        blocks = pl.ds(c * zc, zc)
        return pltpu.make_async_remote_copy(
            src_ref=p_ref.at[to, blocks],
            dst_ref=g1.at[dst_x, blocks],
            send_sem=s1.at[k, c],
            recv_sem=r1.at[k, c],
            device_id=device(to, zi),
            device_id_type=MESH,
        )

    def along_z(k, z):
        return pltpu.make_async_remote_copy(
            src_ref=b_ref.at[z],
            dst_ref=g2.at[zi],
            send_sem=s2.at[k],
            recv_sem=r2.at[k],
            device_id=device(xo, z),
            device_id_type=MESH,
        )

    first = []
    for c in range(chunks):
        for k in range(1, n_o):
            copy = along_x(k, c, lax.rem(xo + k, n_o), xo)
            copy.start()
            first.append(copy)
    sources = [lax.rem(xo + n_o - k, n_o) for k in range(1, n_o)]
    for c in range(chunks):
        for k in range(1, n_o):
            pltpu.make_async_remote_copy(
                src_ref=p_ref.at[sources[k - 1], pl.ds(c * zc, zc)],
                dst_ref=g1.at[sources[k - 1], pl.ds(c * zc, zc)],
                send_sem=s1.at[k, c],
                recv_sem=r1.at[k, c],
                device_id=device(sources[k - 1], zi),
                device_id_type=MESH,
            ).wait_recv()
        for z in range(c * zc, (c + 1) * zc):
            total = p_ref[xo, z].astype(jnp.float32)
            for src in sources:
                total = total + g1[src, z].astype(jnp.float32)
            b_ref[z] = total.astype(b_ref.dtype)
            offset = lax.rem(z - zi + n_i, n_i)

            @pl.when(offset == 0)
            def _():
                o_ref[...] = total

            @pl.when(offset != 0)
            def _():
                along_z(offset, z).start()

    for k in range(1, n_i):
        src = lax.rem(zi + n_i - k, n_i)
        pltpu.make_async_remote_copy(
            src_ref=b_ref.at[src],
            dst_ref=g2.at[src],
            send_sem=s2.at[k],
            recv_sem=r2.at[k],
            device_id=device(xo, src),
            device_id_type=MESH,
        ).wait_recv()
        o_ref[...] = o_ref[...] + g2[src].astype(jnp.float32)
    for copy in first:
        copy.wait_send()
    for z in range(n_i):
        offset = lax.rem(z - zi + n_i, n_i)

        @pl.when(offset != 0)
        def _():
            along_z(offset, z).wait_send()


def reduce_scatter_2d(x, axis, first, second, collective_id):
    (n_o, s_o), (n_i, s_i) = first, second
    chunks = next(c for c in (8, 4, 2, 1) if n_i % c == 0)
    return pl.pallas_call(
        functools.partial(_reduce_kernel, n_o, s_o, n_i, s_i, chunks, axis),
        out_shape=jax.ShapeDtypeStruct(x.shape[2:], jnp.float32),
        in_specs=[pl.BlockSpec(memory_space=pltpu.VMEM)],
        out_specs=pl.BlockSpec(memory_space=pltpu.VMEM),
        scratch_shapes=[
            pltpu.VMEM(x.shape, x.dtype),
            pltpu.VMEM(x.shape[1:], x.dtype),
            pltpu.VMEM(x.shape[1:], x.dtype),
            pltpu.SemaphoreType.DMA((n_o, chunks)),
            pltpu.SemaphoreType.DMA((n_o, chunks)),
            pltpu.SemaphoreType.DMA((n_i,)),
            pltpu.SemaphoreType.DMA((n_i,)),
        ],
        compiler_params=pltpu.CompilerParams(
            collective_id=collective_id,
            has_side_effects=True,
            vmem_limit_bytes=min(4 * x.dtype.itemsize * x.size + (8 << 20), 60 << 20),
        ),
    )(x)


def inner_size(devices):
    coords = [tuple(getattr(d, "coords", ())) for d in devices]
    if len(coords) < 2 or not coords[0]:
        return len(coords)
    varying = [c for c in range(len(coords[0])) if len({p[c] for p in coords}) > 1]
    slow = [c for c in varying if coords[1][c] == coords[0][c]]
    if not slow:
        return 1
    run = 0
    while run < len(coords) and coords[run][slow[0]] == coords[0][slow[0]]:
        run += 1
    return run


def per_device(n_sub, mass_inner, sub_inner, spectra, w_in, w_out, partner_rows, pair_counts, pair_labels):
    own_rows = spectra.shape[0]
    peers = partner_rows.shape[2]
    slots = partner_rows.shape[3]
    shard_rows = all_gather(spectra, "sub", n_sub, sub_inner, 2)
    pre = jnp.dot(shard_rows, w_in, preferred_element_type=jnp.float32)
    hidden = jax.nn.silu(pre).astype(jnp.bfloat16)
    embed_part = jnp.dot(hidden, w_out, preferred_element_type=jnp.float32)
    sub_outer = n_sub // sub_inner
    embed = reduce_scatter_2d(
        embed_part.reshape(sub_inner, sub_outer, own_rows, embed_part.shape[1]),
        "sub",
        (sub_inner, 1),
        (sub_outer, sub_inner),
        4,
    )
    norm = jnp.sqrt(jnp.sum(embed * embed, axis=-1, keepdims=True) + 1e-06)
    unit = embed / norm
    unit_b = unit.astype(jnp.bfloat16)
    flat_rows = partner_rows.reshape(peers * slots)
    selector = flat_rows[:, None] == jnp.arange(own_rows, dtype=jnp.int32)[None, :]
    mine = jnp.dot(
        selector.astype(jnp.bfloat16), unit_b, preferred_element_type=jnp.float32
    ).astype(jnp.bfloat16)
    outgoing = mine.reshape(peers, slots, mine.shape[1])
    incoming = exchange(outgoing, "mass", peers, 1)
    theirs = incoming.astype(jnp.float32)
    sim = jnp.sum(outgoing.astype(jnp.float32) * theirs, axis=-1)
    valid = jnp.arange(slots, dtype=jnp.int32)[None, :] < pair_counts.reshape(peers)[:, None]
    labels = pair_labels.reshape(peers, slots).astype(jnp.float32)
    coef = jnp.where(valid, 2.0 * (sim - labels), jnp.float32(0.0))
    weighted = (coef[..., None] * theirs).reshape(peers * slots, theirs.shape[2])
    grad_unit = lax.dot_general(
        selector.astype(jnp.float32),
        weighted,
        (((0,), (0,)), ((), ())),
        precision=lax.Precision.HIGHEST,
    )
    along = jnp.sum(unit * grad_unit, axis=-1, keepdims=True)
    grad_embed = ((grad_unit - unit * along) / norm).astype(jnp.bfloat16)
    grad_rows = all_gather(grad_embed, "sub", n_sub, sub_inner, 6)
    back = lax.dot_general(
        grad_rows, w_out, (((1,), (1,)), ((), ())), preferred_element_type=jnp.float32
    )
    gate = jax.nn.sigmoid(pre)
    grad_pre = lax.optimization_barrier(
        (back * gate * (1.0 + pre * (1.0 - gate))).astype(jnp.bfloat16)
    )
    out_part = lax.dot_general(
        grad_rows, hidden, (((0,), (0,)), ((), ())), preferred_element_type=jnp.float32
    )
    in_part_t = lax.dot_general(
        grad_pre, shard_rows, (((0,), (0,)), ((), ())), preferred_element_type=jnp.float32
    )
    n_mass = peers
    hid = in_part_t.shape[0]
    in_cols = in_part_t.shape[1] // n_mass
    out_rows = out_part.shape[0] // n_mass
    lanes = in_cols
    partial = jnp.concatenate(
        [
            jnp.swapaxes(in_part_t.astype(jnp.bfloat16).reshape(hid, n_mass, in_cols), 0, 1),
            out_part.astype(jnp.bfloat16).reshape(n_mass, out_rows * hid // lanes, lanes),
        ],
        axis=1,
    )
    mass_outer = n_mass // mass_inner
    summed = reduce_scatter_2d(
        partial.reshape((mass_outer, mass_inner) + partial.shape[1:]),
        "mass",
        (mass_outer, mass_inner),
        (mass_inner, 1),
        8,
    )
    grad_in = summed[:hid].T
    grad_out_t = summed[hid:].reshape(out_rows, hid)
    return (grad_in, grad_out_t)


def solution(mesh):
    placed = (
        P(("mass", "sub"), None),
        P(None, "sub"),
        P("sub", None),
        P("mass", "sub", None, None),
        P("mass", "sub", None),
        P("mass", "sub", None, None),
    )
    mass_inner = inner_size(list(mesh.devices[:, 0]))
    sub_inner = inner_size(list(mesh.devices[0, :]))
    return jax.shard_map(
        functools.partial(per_device, mesh.shape["sub"], mass_inner, sub_inner),
        mesh=mesh,
        in_specs=placed,
        out_specs=(P("mass", "sub"), P("mass", "sub")),
        check_vma=False,
    )
```

```python
import functools
import math

import jax
import jax.numpy as jnp
from jax import lax
from jax.experimental import pallas as pl
from jax.experimental.pallas import tpu as pltpu
from jax.sharding import PartitionSpec as P

MESH = pl.DeviceIdType.MESH


def _exchange_kernel(n, stride, axis, gather, x_ref, o_ref, got, send_sems, recv_sems):
    me = lax.axis_index(axis)
    mine = lax.rem(lax.div(me, stride), n)
    base = me - mine * stride

    def member(j):
        return base + j * stride

    barrier = pltpu.get_barrier_semaphore()
    for k in range(1, n):
        pl.semaphore_signal(
            barrier, inc=1, device_id={axis: member(lax.rem(mine + k, n))}, device_id_type=MESH
        )
    pl.semaphore_wait(barrier, n - 1)
    sends = []
    for k in range(1, n):
        peer = lax.rem(mine + k, n)
        copy = pltpu.make_async_remote_copy(
            src_ref=x_ref if gather else x_ref.at[peer],
            dst_ref=got.at[mine],
            send_sem=send_sems.at[k],
            recv_sem=recv_sems.at[k],
            device_id={axis: member(peer)},
            device_id_type=MESH,
        )
        copy.start()
        sends.append(copy)
    o_ref[mine] = x_ref[...] if gather else x_ref[mine]
    for k in range(1, n):
        source = lax.rem(mine + n - k, n)
        pltpu.make_async_remote_copy(
            src_ref=x_ref if gather else x_ref.at[source],
            dst_ref=got.at[source],
            send_sem=send_sems.at[k],
            recv_sem=recv_sems.at[k],
            device_id={axis: member(source)},
            device_id_type=MESH,
        ).wait_recv()
        o_ref[source] = got[source]
    for copy in sends:
        copy.wait_send()


def exchange(x, axis, n, collective_id, gather=False, stride=1):
    shape = (n,) + x.shape if gather else x.shape
    return pl.pallas_call(
        functools.partial(_exchange_kernel, n, stride, axis, gather),
        out_shape=jax.ShapeDtypeStruct(shape, x.dtype),
        in_specs=[pl.BlockSpec(memory_space=pltpu.VMEM)],
        out_specs=pl.BlockSpec(memory_space=pltpu.VMEM),
        scratch_shapes=[
            pltpu.VMEM(shape, x.dtype),
            pltpu.SemaphoreType.DMA((n,)),
            pltpu.SemaphoreType.DMA((n,)),
        ],
        compiler_params=pltpu.CompilerParams(
            collective_id=collective_id,
            has_side_effects=True,
            vmem_limit_bytes=min(3 * x.dtype.itemsize * math.prod(shape) + (8 << 20), 60 << 20),
        ),
    )(x)


def reduce_scatter(x, axis, inner, first_inner, first_id):
    outer = x.shape[0] // inner
    if first_inner:
        blocks = x.reshape((inner, outer) + x.shape[1:])
        phases = [(inner, 1), (outer, inner)]
    else:
        blocks = x.reshape((outer, inner) + x.shape[1:])
        phases = [(outer, inner), (inner, 1)]
    for number, (size, stride) in enumerate(phases):
        if size == 1:
            blocks = blocks[0].astype(jnp.float32)
            continue
        got = exchange(blocks.astype(x.dtype), axis, size, first_id + number, stride=stride)
        blocks = jnp.sum(got.astype(jnp.float32), axis=0)
    return blocks


def _gather_kernel(n_outer, n_inner, axis, x_ref, o_ref, got, send_sems, recv_sems):
    me = lax.axis_index(axis)
    ci = lax.rem(me, n_inner)
    yo = lax.div(me, n_inner)

    def device(c, y):
        return {axis: y * n_inner + c}

    def slot(c, y):
        return c * n_outer + y

    outer_peers = [lax.rem(yo + k, n_outer) for k in range(1, n_outer)]
    inner_peers = [lax.rem(ci + j, n_inner) for j in range(1, n_inner)]
    barrier = pltpu.get_barrier_semaphore()
    for y in outer_peers:
        pl.semaphore_signal(barrier, inc=1, device_id=device(ci, y), device_id_type=MESH)
    for c in inner_peers:
        pl.semaphore_signal(barrier, inc=1, device_id=device(c, yo), device_id_type=MESH)
    pl.semaphore_wait(barrier, len(outer_peers) + len(inner_peers))

    sends = []

    def send(src, c, y, to):
        copy = pltpu.make_async_remote_copy(
            src_ref=src,
            dst_ref=got.at[c, y],
            send_sem=send_sems.at[len(sends)],
            recv_sem=recv_sems.at[slot(c, y)],
            device_id=to,
            device_id_type=MESH,
        )
        copy.start()
        sends.append(copy)

    def receive(c, y):
        pltpu.make_async_remote_copy(
            src_ref=x_ref,
            dst_ref=got.at[c, y],
            send_sem=send_sems.at[0],
            recv_sem=recv_sems.at[slot(c, y)],
            device_id=device(c, y),
            device_id_type=MESH,
        ).wait_recv()

    for y in outer_peers:
        send(x_ref, ci, yo, device(ci, y))
    for c in inner_peers:
        send(x_ref, ci, yo, device(c, yo))
    o_ref[ci, yo] = x_ref[...]
    for k in range(1, n_outer):
        y = lax.rem(yo + n_outer - k, n_outer)
        receive(ci, y)
        for c in inner_peers:
            send(got.at[ci, y], ci, y, device(c, yo))
        o_ref[ci, y] = got[ci, y]
    for j in range(1, n_inner):
        c = lax.rem(ci + n_inner - j, n_inner)
        for k in range(n_outer):
            y = lax.rem(yo + k, n_outer)
            receive(c, y)
            o_ref[c, y] = got[c, y]
    for copy in sends:
        copy.wait_send()


def all_gather(x, axis, n, inner, collective_id):
    outer = n // inner
    shape = (inner, outer) + x.shape
    got = pl.pallas_call(
        functools.partial(_gather_kernel, outer, inner, axis),
        out_shape=jax.ShapeDtypeStruct(shape, x.dtype),
        in_specs=[pl.BlockSpec(memory_space=pltpu.VMEM)],
        out_specs=pl.BlockSpec(memory_space=pltpu.VMEM),
        scratch_shapes=[
            pltpu.VMEM(shape, x.dtype),
            pltpu.SemaphoreType.DMA((n,)),
            pltpu.SemaphoreType.DMA((n,)),
        ],
        compiler_params=pltpu.CompilerParams(
            collective_id=collective_id,
            has_side_effects=True,
            vmem_limit_bytes=min(3 * x.dtype.itemsize * math.prod(shape) + (8 << 20), 60 << 20),
        ),
    )(x)
    return got.reshape((n * x.shape[0],) + x.shape[1:])


def _reduce_kernel(n_o, s_o, n_i, s_i, chunks, axis, p_ref, o_ref, g1, b_ref, g2, s1, r1, s2, r2):
    me = lax.axis_index(axis)
    zi = lax.rem(lax.div(me, s_i), n_i)
    xo = lax.rem(lax.div(me, s_o), n_o)
    zc = n_i // chunks

    def device(x, z):
        return {axis: me + (x - xo) * s_o + (z - zi) * s_i}

    barrier = pltpu.get_barrier_semaphore()
    for k in range(1, n_o):
        pl.semaphore_signal(
            barrier, inc=1, device_id=device(lax.rem(xo + k, n_o), zi), device_id_type=MESH
        )
    for k in range(1, n_i):
        pl.semaphore_signal(
            barrier, inc=1, device_id=device(xo, lax.rem(zi + k, n_i)), device_id_type=MESH
        )
    pl.semaphore_wait(barrier, n_o + n_i - 2)

    def along_x(k, c, to, dst_x):
        blocks = pl.ds(c * zc, zc)
        return pltpu.make_async_remote_copy(
            src_ref=p_ref.at[to, blocks],
            dst_ref=g1.at[dst_x, blocks],
            send_sem=s1.at[k, c],
            recv_sem=r1.at[k, c],
            device_id=device(to, zi),
            device_id_type=MESH,
        )

    def along_z(k, z):
        return pltpu.make_async_remote_copy(
            src_ref=b_ref.at[z],
            dst_ref=g2.at[zi],
            send_sem=s2.at[k],
            recv_sem=r2.at[k],
            device_id=device(xo, z),
            device_id_type=MESH,
        )

    first = []
    for c in range(chunks):
        for k in range(1, n_o):
            copy = along_x(k, c, lax.rem(xo + k, n_o), xo)
            copy.start()
            first.append(copy)
    sources = [lax.rem(xo + n_o - k, n_o) for k in range(1, n_o)]
    for c in range(chunks):
        for k in range(1, n_o):
            pltpu.make_async_remote_copy(
                src_ref=p_ref.at[sources[k - 1], pl.ds(c * zc, zc)],
                dst_ref=g1.at[sources[k - 1], pl.ds(c * zc, zc)],
                send_sem=s1.at[k, c],
                recv_sem=r1.at[k, c],
                device_id=device(sources[k - 1], zi),
                device_id_type=MESH,
            ).wait_recv()
        for z in range(c * zc, (c + 1) * zc):
            total = p_ref[xo, z].astype(jnp.float32)
            for src in sources:
                total = total + g1[src, z].astype(jnp.float32)
            b_ref[z] = total.astype(b_ref.dtype)
            offset = lax.rem(z - zi + n_i, n_i)

            @pl.when(offset == 0)
            def _():
                o_ref[...] = total

            @pl.when(offset != 0)
            def _():
                along_z(offset, z).start()

    for k in range(1, n_i):
        src = lax.rem(zi + n_i - k, n_i)
        pltpu.make_async_remote_copy(
            src_ref=b_ref.at[src],
            dst_ref=g2.at[src],
            send_sem=s2.at[k],
            recv_sem=r2.at[k],
            device_id=device(xo, src),
            device_id_type=MESH,
        ).wait_recv()
        o_ref[...] = o_ref[...] + g2[src].astype(jnp.float32)
    for copy in first:
        copy.wait_send()
    for z in range(n_i):
        offset = lax.rem(z - zi + n_i, n_i)

        @pl.when(offset != 0)
        def _():
            along_z(offset, z).wait_send()


def reduce_scatter_2d(x, axis, first, second, collective_id):
    (n_o, s_o), (n_i, s_i) = first, second
    chunks = next(c for c in (8, 4, 2, 1) if n_i % c == 0)
    return pl.pallas_call(
        functools.partial(_reduce_kernel, n_o, s_o, n_i, s_i, chunks, axis),
        out_shape=jax.ShapeDtypeStruct(x.shape[2:], jnp.float32),
        in_specs=[pl.BlockSpec(memory_space=pltpu.VMEM)],
        out_specs=pl.BlockSpec(memory_space=pltpu.VMEM),
        scratch_shapes=[
            pltpu.VMEM(x.shape, x.dtype),
            pltpu.VMEM(x.shape[1:], x.dtype),
            pltpu.VMEM(x.shape[1:], x.dtype),
            pltpu.SemaphoreType.DMA((n_o, chunks)),
            pltpu.SemaphoreType.DMA((n_o, chunks)),
            pltpu.SemaphoreType.DMA((n_i,)),
            pltpu.SemaphoreType.DMA((n_i,)),
        ],
        compiler_params=pltpu.CompilerParams(
            collective_id=collective_id,
            has_side_effects=True,
            vmem_limit_bytes=min(4 * x.dtype.itemsize * x.size + (8 << 20), 60 << 20),
        ),
    )(x)


def inner_size(devices):
    coords = [tuple(getattr(d, "coords", ())) for d in devices]
    if len(coords) < 2 or not coords[0]:
        return len(coords)
    varying = [c for c in range(len(coords[0])) if len({p[c] for p in coords}) > 1]
    slow = [c for c in varying if coords[1][c] == coords[0][c]]
    if not slow:
        return 1
    run = 0
    while run < len(coords) and coords[run][slow[0]] == coords[0][slow[0]]:
        run += 1
    return run


def per_device(n_sub, mass_inner, sub_inner, spectra, w_in, w_out, partner_rows, pair_counts, pair_labels):
    own_rows = spectra.shape[0]
    peers = partner_rows.shape[2]
    slots = partner_rows.shape[3]
    shard_rows = all_gather(spectra, "sub", n_sub, sub_inner, 2)
    pre = jnp.dot(shard_rows, w_in, preferred_element_type=jnp.float32)
    hidden = jax.nn.silu(pre).astype(jnp.bfloat16)
    embed_part = jnp.dot(hidden, w_out, preferred_element_type=jnp.float32)
    sub_outer = n_sub // sub_inner
    embed = reduce_scatter_2d(
        embed_part.reshape(sub_inner, sub_outer, own_rows, embed_part.shape[1]),
        "sub",
        (sub_inner, 1),
        (sub_outer, sub_inner),
        4,
    )
    norm = jnp.sqrt(jnp.sum(embed * embed, axis=-1, keepdims=True) + 1e-06)
    unit = embed / norm
    unit_b = unit.astype(jnp.bfloat16)
    flat_rows = partner_rows.reshape(peers * slots)
    selector = flat_rows[:, None] == jnp.arange(own_rows, dtype=jnp.int32)[None, :]
    mine = jnp.dot(
        selector.astype(jnp.bfloat16), unit_b, preferred_element_type=jnp.float32
    ).astype(jnp.bfloat16)
    outgoing = mine.reshape(peers, slots, mine.shape[1])
    incoming = exchange(outgoing, "mass", peers, 1)
    theirs = incoming.astype(jnp.float32)
    sim = jnp.sum(outgoing.astype(jnp.float32) * theirs, axis=-1)
    valid = jnp.arange(slots, dtype=jnp.int32)[None, :] < pair_counts.reshape(peers)[:, None]
    labels = pair_labels.reshape(peers, slots).astype(jnp.float32)
    coef = jnp.where(valid, 2.0 * (sim - labels), jnp.float32(0.0))
    weighted = (coef[..., None] * theirs).reshape(peers * slots, theirs.shape[2])
    grad_unit = lax.dot_general(
        selector.astype(jnp.float32),
        weighted,
        (((0,), (0,)), ((), ())),
        precision=lax.Precision.HIGHEST,
    )
    along = jnp.sum(unit * grad_unit, axis=-1, keepdims=True)
    grad_embed = ((grad_unit - unit * along) / norm).astype(jnp.bfloat16)
    grad_rows = all_gather(grad_embed, "sub", n_sub, sub_inner, 6)
    back = lax.dot_general(
        grad_rows, w_out, (((1,), (1,)), ((), ())), preferred_element_type=jnp.float32
    )
    gate = jax.nn.sigmoid(pre)
    grad_pre = lax.optimization_barrier(
        (back * gate * (1.0 + pre * (1.0 - gate))).astype(jnp.bfloat16)
    )
    out_part = lax.dot_general(
        grad_rows, hidden, (((0,), (0,)), ((), ())), preferred_element_type=jnp.float32
    )
    in_part_t = lax.dot_general(
        grad_pre, shard_rows, (((0,), (0,)), ((), ())), preferred_element_type=jnp.float32
    )
    n_mass = peers
    hid = in_part_t.shape[0]
    in_cols = in_part_t.shape[1] // n_mass
    out_rows = out_part.shape[0] // n_mass
    lanes = in_cols
    partial = jnp.concatenate(
        [
            jnp.swapaxes(in_part_t.astype(jnp.bfloat16).reshape(hid, n_mass, in_cols), 0, 1),
            out_part.astype(jnp.bfloat16).reshape(n_mass, out_rows * hid // lanes, lanes),
        ],
        axis=1,
    )
    mass_outer = n_mass // mass_inner
    summed = reduce_scatter_2d(
        partial.reshape((mass_outer, mass_inner) + partial.shape[1:]),
        "mass",
        (mass_outer, mass_inner),
        (mass_inner, 1),
        8,
    )
    grad_in = summed[:hid].T
    grad_out_t = summed[hid:].reshape(out_rows, hid)
    return (grad_in, grad_out_t)


def solution(mesh):
    placed = (
        P(("mass", "sub"), None),
        P(None, "sub"),
        P("sub", None),
        P("mass", "sub", None, None),
        P("mass", "sub", None),
        P("mass", "sub", None, None),
    )
    mass_inner = inner_size(list(mesh.devices[:, 0]))
    sub_inner = inner_size(list(mesh.devices[0, :]))
    return jax.shard_map(
        functools.partial(per_device, mesh.shape["sub"], mass_inner, sub_inner),
        mesh=mesh,
        in_specs=placed,
        out_specs=(P("mass", "sub"), P("mass", "sub")),
        check_vma=False,
    )
```

```python
import functools
import math

import jax
import jax.numpy as jnp
from jax import lax
from jax.experimental import pallas as pl
from jax.experimental.pallas import tpu as pltpu
from jax.sharding import PartitionSpec as P

MESH = pl.DeviceIdType.MESH


def _exchange_kernel(n, stride, axis, gather, x_ref, o_ref, got, send_sems, recv_sems):
    me = lax.axis_index(axis)
    mine = lax.rem(lax.div(me, stride), n)
    base = me - mine * stride

    def member(j):
        return base + j * stride

    barrier = pltpu.get_barrier_semaphore()
    for k in range(1, n):
        pl.semaphore_signal(
            barrier, inc=1, device_id={axis: member(lax.rem(mine + k, n))}, device_id_type=MESH
        )
    pl.semaphore_wait(barrier, n - 1)
    sends = []
    for k in range(1, n):
        peer = lax.rem(mine + k, n)
        copy = pltpu.make_async_remote_copy(
            src_ref=x_ref if gather else x_ref.at[peer],
            dst_ref=got.at[mine],
            send_sem=send_sems.at[k],
            recv_sem=recv_sems.at[k],
            device_id={axis: member(peer)},
            device_id_type=MESH,
        )
        copy.start()
        sends.append(copy)
    o_ref[mine] = x_ref[...] if gather else x_ref[mine]
    for k in range(1, n):
        sends[k - 1].wait_send()
        source = lax.rem(mine + n - k, n)
        pltpu.make_async_remote_copy(
            src_ref=x_ref if gather else x_ref.at[source],
            dst_ref=got.at[source],
            send_sem=send_sems.at[k],
            recv_sem=recv_sems.at[k],
            device_id={axis: member(source)},
            device_id_type=MESH,
        ).wait_recv()
        o_ref[source] = got[source]


def exchange(x, axis, n, collective_id, gather=False, stride=1):
    shape = (n,) + x.shape if gather else x.shape
    return pl.pallas_call(
        functools.partial(_exchange_kernel, n, stride, axis, gather),
        out_shape=jax.ShapeDtypeStruct(shape, x.dtype),
        in_specs=[pl.BlockSpec(memory_space=pltpu.VMEM)],
        out_specs=pl.BlockSpec(memory_space=pltpu.VMEM),
        scratch_shapes=[
            pltpu.VMEM(shape, x.dtype),
            pltpu.SemaphoreType.DMA((n,)),
            pltpu.SemaphoreType.DMA((n,)),
        ],
        compiler_params=pltpu.CompilerParams(
            collective_id=collective_id,
            has_side_effects=True,
            vmem_limit_bytes=min(3 * x.dtype.itemsize * math.prod(shape) + (8 << 20), 60 << 20),
        ),
    )(x)


def reduce_scatter(x, axis, inner, first_inner, first_id):
    outer = x.shape[0] // inner
    if first_inner:
        blocks = x.reshape((inner, outer) + x.shape[1:])
        phases = [(inner, 1), (outer, inner)]
    else:
        blocks = x.reshape((outer, inner) + x.shape[1:])
        phases = [(outer, inner), (inner, 1)]
    for number, (size, stride) in enumerate(phases):
        if size == 1:
            blocks = blocks[0].astype(jnp.float32)
            continue
        got = exchange(blocks.astype(x.dtype), axis, size, first_id + number, stride=stride)
        blocks = jnp.sum(got.astype(jnp.float32), axis=0)
    return blocks


def _gather_kernel(n_outer, n_inner, parts, axis, x_ref, o_ref, got, send_sems, recv_sems):
    me = lax.axis_index(axis)
    ci = lax.rem(me, n_inner)
    yo = lax.div(me, n_inner)
    rows = x_ref.shape[0] // parts

    def device(c, y):
        return {axis: y * n_inner + c}

    def slot(c, y, p):
        return (c * n_outer + y) * parts + p

    def piece(p):
        return pl.ds(p * rows, rows)

    outer_peers = [lax.rem(yo + k, n_outer) for k in range(1, n_outer)]
    inner_peers = [lax.rem(ci + j, n_inner) for j in range(1, n_inner)]
    barrier = pltpu.get_barrier_semaphore()
    for y in outer_peers:
        pl.semaphore_signal(barrier, inc=1, device_id=device(ci, y), device_id_type=MESH)
    for c in inner_peers:
        pl.semaphore_signal(barrier, inc=1, device_id=device(c, yo), device_id_type=MESH)
    pl.semaphore_wait(barrier, len(outer_peers) + len(inner_peers))

    sends = []

    def send(src, c, y, p, to):
        copy = pltpu.make_async_remote_copy(
            src_ref=src,
            dst_ref=got.at[c, y, piece(p)],
            send_sem=send_sems.at[len(sends)],
            recv_sem=recv_sems.at[slot(c, y, p)],
            device_id=to,
            device_id_type=MESH,
        )
        copy.start()
        sends.append(copy)

    def receive(c, y, p):
        pltpu.make_async_remote_copy(
            src_ref=x_ref.at[piece(p)],
            dst_ref=got.at[c, y, piece(p)],
            send_sem=send_sems.at[0],
            recv_sem=recv_sems.at[slot(c, y, p)],
            device_id=device(c, y),
            device_id_type=MESH,
        ).wait_recv()

    for p in range(parts):
        for y in outer_peers:
            send(x_ref.at[piece(p)], ci, yo, p, device(ci, y))
        for c in inner_peers:
            send(x_ref.at[piece(p)], ci, yo, p, device(c, yo))
    o_ref[ci, yo] = x_ref[...]
    for p in range(parts):
        for k in range(1, n_outer):
            y = lax.rem(yo + n_outer - k, n_outer)
            receive(ci, y, p)
            for c in inner_peers:
                send(got.at[ci, y, piece(p)], ci, y, p, device(c, yo))
            o_ref[ci, y, piece(p)] = got[ci, y, piece(p)]
    for j in range(1, n_inner):
        c = lax.rem(ci + n_inner - j, n_inner)
        for p in range(parts):
            for k in range(n_outer):
                y = lax.rem(yo + k, n_outer)
                receive(c, y, p)
                o_ref[c, y, piece(p)] = got[c, y, piece(p)]
    for copy in sends:
        copy.wait_send()


def all_gather(x, axis, n, inner, collective_id):
    outer = n // inner
    shape = (inner, outer) + x.shape
    parts = 2 if x.shape[0] % 32 == 0 else 1
    got = pl.pallas_call(
        functools.partial(_gather_kernel, outer, inner, parts, axis),
        out_shape=jax.ShapeDtypeStruct(shape, x.dtype),
        in_specs=[pl.BlockSpec(memory_space=pltpu.VMEM)],
        out_specs=pl.BlockSpec(memory_space=pltpu.VMEM),
        scratch_shapes=[
            pltpu.VMEM(shape, x.dtype),
            pltpu.SemaphoreType.DMA((n * parts,)),
            pltpu.SemaphoreType.DMA((n * parts,)),
        ],
        compiler_params=pltpu.CompilerParams(
            collective_id=collective_id,
            has_side_effects=True,
            vmem_limit_bytes=min(3 * x.dtype.itemsize * math.prod(shape) + (8 << 20), 60 << 20),
        ),
    )(x)
    return got.reshape((n * x.shape[0],) + x.shape[1:])


def _reduce_kernel(n_o, s_o, n_i, s_i, chunks, axis, p_ref, o_ref, g1, b_ref, g2, s1, r1, s2, r2):
    me = lax.axis_index(axis)
    zi = lax.rem(lax.div(me, s_i), n_i)
    xo = lax.rem(lax.div(me, s_o), n_o)
    zc = n_i // chunks

    def device(x, z):
        return {axis: me + (x - xo) * s_o + (z - zi) * s_i}

    barrier = pltpu.get_barrier_semaphore()
    for k in range(1, n_o):
        pl.semaphore_signal(
            barrier, inc=1, device_id=device(lax.rem(xo + k, n_o), zi), device_id_type=MESH
        )
    for k in range(1, n_i):
        pl.semaphore_signal(
            barrier, inc=1, device_id=device(xo, lax.rem(zi + k, n_i)), device_id_type=MESH
        )
    pl.semaphore_wait(barrier, n_o + n_i - 2)

    def along_x(k, c, to, dst_x):
        blocks = pl.ds(c * zc, zc)
        return pltpu.make_async_remote_copy(
            src_ref=p_ref.at[to, blocks],
            dst_ref=g1.at[dst_x, blocks],
            send_sem=s1.at[k, c],
            recv_sem=r1.at[k, c],
            device_id=device(to, zi),
            device_id_type=MESH,
        )

    def along_z(k, z):
        return pltpu.make_async_remote_copy(
            src_ref=b_ref.at[z],
            dst_ref=g2.at[zi],
            send_sem=s2.at[k],
            recv_sem=r2.at[k],
            device_id=device(xo, z),
            device_id_type=MESH,
        )

    first = []
    for c in range(chunks):
        for k in range(1, n_o):
            copy = along_x(k, c, lax.rem(xo + k, n_o), xo)
            copy.start()
            first.append(copy)
    sources = [lax.rem(xo + n_o - k, n_o) for k in range(1, n_o)]
    for c in range(chunks):
        for k in range(1, n_o):
            pltpu.make_async_remote_copy(
                src_ref=p_ref.at[sources[k - 1], pl.ds(c * zc, zc)],
                dst_ref=g1.at[sources[k - 1], pl.ds(c * zc, zc)],
                send_sem=s1.at[k, c],
                recv_sem=r1.at[k, c],
                device_id=device(sources[k - 1], zi),
                device_id_type=MESH,
            ).wait_recv()
        for z in range(c * zc, (c + 1) * zc):
            total = p_ref[xo, z].astype(jnp.float32)
            for src in sources:
                total = total + g1[src, z].astype(jnp.float32)
            b_ref[z] = total.astype(b_ref.dtype)
            offset = lax.rem(z - zi + n_i, n_i)

            @pl.when(offset == 0)
            def _():
                o_ref[...] = total

            @pl.when(offset != 0)
            def _():
                along_z(offset, z).start()

    for k in range(1, n_i):
        src = lax.rem(zi + n_i - k, n_i)
        pltpu.make_async_remote_copy(
            src_ref=b_ref.at[src],
            dst_ref=g2.at[src],
            send_sem=s2.at[k],
            recv_sem=r2.at[k],
            device_id=device(xo, src),
            device_id_type=MESH,
        ).wait_recv()
        o_ref[...] = o_ref[...] + g2[src].astype(jnp.float32)
    for copy in first:
        copy.wait_send()
    for z in range(n_i):
        offset = lax.rem(z - zi + n_i, n_i)

        @pl.when(offset != 0)
        def _():
            along_z(offset, z).wait_send()


def reduce_scatter_2d(x, axis, first, second, collective_id):
    (n_o, s_o), (n_i, s_i) = first, second
    chunks = next(c for c in (8, 4, 2, 1) if n_i % c == 0)
    return pl.pallas_call(
        functools.partial(_reduce_kernel, n_o, s_o, n_i, s_i, chunks, axis),
        out_shape=jax.ShapeDtypeStruct(x.shape[2:], jnp.float32),
        in_specs=[pl.BlockSpec(memory_space=pltpu.VMEM)],
        out_specs=pl.BlockSpec(memory_space=pltpu.VMEM),
        scratch_shapes=[
            pltpu.VMEM(x.shape, x.dtype),
            pltpu.VMEM(x.shape[1:], x.dtype),
            pltpu.VMEM(x.shape[1:], x.dtype),
            pltpu.SemaphoreType.DMA((n_o, chunks)),
            pltpu.SemaphoreType.DMA((n_o, chunks)),
            pltpu.SemaphoreType.DMA((n_i,)),
            pltpu.SemaphoreType.DMA((n_i,)),
        ],
        compiler_params=pltpu.CompilerParams(
            collective_id=collective_id,
            has_side_effects=True,
            vmem_limit_bytes=min(4 * x.dtype.itemsize * x.size + (8 << 20), 60 << 20),
        ),
    )(x)


def inner_size(devices):
    coords = [tuple(getattr(d, "coords", ())) for d in devices]
    if len(coords) < 2 or not coords[0]:
        return len(coords)
    varying = [c for c in range(len(coords[0])) if len({p[c] for p in coords}) > 1]
    slow = [c for c in varying if coords[1][c] == coords[0][c]]
    if not slow:
        return 1
    run = 0
    while run < len(coords) and coords[run][slow[0]] == coords[0][slow[0]]:
        run += 1
    return run


def per_device(n_sub, mass_inner, sub_inner, spectra, w_in, w_out, partner_rows, pair_counts, pair_labels):
    own_rows = spectra.shape[0]
    peers = partner_rows.shape[2]
    slots = partner_rows.shape[3]
    shard_rows = all_gather(spectra, "sub", n_sub, sub_inner, 2)
    pre = jnp.dot(shard_rows, w_in, preferred_element_type=jnp.float32)
    hidden = jax.nn.silu(pre).astype(jnp.bfloat16)
    embed_part = jnp.dot(hidden, w_out, preferred_element_type=jnp.float32)
    sub_outer = n_sub // sub_inner
    embed = reduce_scatter_2d(
        embed_part.reshape(sub_inner, sub_outer, own_rows, embed_part.shape[1]),
        "sub",
        (sub_inner, 1),
        (sub_outer, sub_inner),
        4,
    )
    norm = jnp.sqrt(jnp.sum(embed * embed, axis=-1, keepdims=True) + 1e-06)
    unit = embed / norm
    unit_b = unit.astype(jnp.bfloat16)
    flat_rows = partner_rows.reshape(peers * slots)
    selector = flat_rows[:, None] == jnp.arange(own_rows, dtype=jnp.int32)[None, :]
    mine = jnp.dot(
        selector.astype(jnp.bfloat16), unit_b, preferred_element_type=jnp.float32
    ).astype(jnp.bfloat16)
    outgoing = mine.reshape(peers, slots, mine.shape[1])
    incoming = exchange(outgoing, "mass", peers, 1)
    theirs = incoming.astype(jnp.float32)
    sim = jnp.sum(outgoing.astype(jnp.float32) * theirs, axis=-1)
    valid = jnp.arange(slots, dtype=jnp.int32)[None, :] < pair_counts.reshape(peers)[:, None]
    labels = pair_labels.reshape(peers, slots).astype(jnp.float32)
    coef = jnp.where(valid, 2.0 * (sim - labels), jnp.float32(0.0))
    weighted = (coef[..., None] * theirs).reshape(peers * slots, theirs.shape[2])
    grad_unit = lax.dot_general(
        selector.astype(jnp.float32),
        weighted,
        (((0,), (0,)), ((), ())),
        precision=lax.Precision.HIGHEST,
    )
    along = jnp.sum(unit * grad_unit, axis=-1, keepdims=True)
    grad_embed = ((grad_unit - unit * along) / norm).astype(jnp.bfloat16)
    grad_rows = all_gather(grad_embed, "sub", n_sub, sub_inner, 6)
    back = lax.dot_general(
        grad_rows, w_out, (((1,), (1,)), ((), ())), preferred_element_type=jnp.float32
    )
    gate = jax.nn.sigmoid(pre)
    grad_pre = lax.optimization_barrier(
        (back * gate * (1.0 + pre * (1.0 - gate))).astype(jnp.bfloat16)
    )
    out_part = lax.dot_general(
        grad_rows, hidden, (((0,), (0,)), ((), ())), preferred_element_type=jnp.float32
    )
    in_part_t = lax.dot_general(
        grad_pre, shard_rows, (((0,), (0,)), ((), ())), preferred_element_type=jnp.float32
    )
    n_mass = peers
    hid = in_part_t.shape[0]
    in_cols = in_part_t.shape[1] // n_mass
    out_rows = out_part.shape[0] // n_mass
    lanes = in_cols
    partial = jnp.concatenate(
        [
            jnp.swapaxes(in_part_t.astype(jnp.bfloat16).reshape(hid, n_mass, in_cols), 0, 1),
            out_part.astype(jnp.bfloat16).reshape(n_mass, out_rows * hid // lanes, lanes),
        ],
        axis=1,
    )
    mass_outer = n_mass // mass_inner
    summed = reduce_scatter_2d(
        partial.reshape((mass_outer, mass_inner) + partial.shape[1:]),
        "mass",
        (mass_outer, mass_inner),
        (mass_inner, 1),
        8,
    )
    grad_in = summed[:hid].T
    grad_out_t = summed[hid:].reshape(out_rows, hid)
    return (grad_in, grad_out_t)


def solution(mesh):
    placed = (
        P(("mass", "sub"), None),
        P(None, "sub"),
        P("sub", None),
        P("mass", "sub", None, None),
        P("mass", "sub", None),
        P("mass", "sub", None, None),
    )
    mass_inner = inner_size(list(mesh.devices[:, 0]))
    sub_inner = inner_size(list(mesh.devices[0, :]))
    return jax.shard_map(
        functools.partial(per_device, mesh.shape["sub"], mass_inner, sub_inner),
        mesh=mesh,
        in_specs=placed,
        out_specs=(P("mass", "sub"), P("mass", "sub")),
        check_vma=False,
    )
```

```python
import functools
import math

import jax
import jax.numpy as jnp
from jax import lax
from jax.experimental import pallas as pl
from jax.experimental.pallas import tpu as pltpu
from jax.sharding import PartitionSpec as P

MESH = pl.DeviceIdType.MESH


def _exchange_kernel(n, stride, axis, gather, x_ref, o_ref, got, send_sems, recv_sems):
    me = lax.axis_index(axis)
    mine = lax.rem(lax.div(me, stride), n)
    base = me - mine * stride

    def member(j):
        return base + j * stride

    barrier = pltpu.get_barrier_semaphore()
    for k in range(1, n):
        pl.semaphore_signal(
            barrier, inc=1, device_id={axis: member(lax.rem(mine + k, n))}, device_id_type=MESH
        )
    pl.semaphore_wait(barrier, n - 1)
    sends = []
    for k in range(1, n):
        peer = lax.rem(mine + k, n)
        copy = pltpu.make_async_remote_copy(
            src_ref=x_ref if gather else x_ref.at[peer],
            dst_ref=got.at[mine],
            send_sem=send_sems.at[k],
            recv_sem=recv_sems.at[k],
            device_id={axis: member(peer)},
            device_id_type=MESH,
        )
        copy.start()
        sends.append(copy)
    o_ref[mine] = x_ref[...] if gather else x_ref[mine]
    for k in range(1, n):
        sends[k - 1].wait_send()
        source = lax.rem(mine + n - k, n)
        pltpu.make_async_remote_copy(
            src_ref=x_ref if gather else x_ref.at[source],
            dst_ref=got.at[source],
            send_sem=send_sems.at[k],
            recv_sem=recv_sems.at[k],
            device_id={axis: member(source)},
            device_id_type=MESH,
        ).wait_recv()
        o_ref[source] = got[source]


def exchange(x, axis, n, collective_id, gather=False, stride=1):
    shape = (n,) + x.shape if gather else x.shape
    return pl.pallas_call(
        functools.partial(_exchange_kernel, n, stride, axis, gather),
        out_shape=jax.ShapeDtypeStruct(shape, x.dtype),
        in_specs=[pl.BlockSpec(memory_space=pltpu.VMEM)],
        out_specs=pl.BlockSpec(memory_space=pltpu.VMEM),
        scratch_shapes=[
            pltpu.VMEM(shape, x.dtype),
            pltpu.SemaphoreType.DMA((n,)),
            pltpu.SemaphoreType.DMA((n,)),
        ],
        compiler_params=pltpu.CompilerParams(
            collective_id=collective_id,
            has_side_effects=True,
            vmem_limit_bytes=min(3 * x.dtype.itemsize * math.prod(shape) + (8 << 20), 60 << 20),
        ),
    )(x)


def reduce_scatter(x, axis, inner, first_inner, first_id):
    outer = x.shape[0] // inner
    if first_inner:
        blocks = x.reshape((inner, outer) + x.shape[1:])
        phases = [(inner, 1), (outer, inner)]
    else:
        blocks = x.reshape((outer, inner) + x.shape[1:])
        phases = [(outer, inner), (inner, 1)]
    for number, (size, stride) in enumerate(phases):
        if size == 1:
            blocks = blocks[0].astype(jnp.float32)
            continue
        got = exchange(blocks.astype(x.dtype), axis, size, first_id + number, stride=stride)
        blocks = jnp.sum(got.astype(jnp.float32), axis=0)
    return blocks


def _gather_kernel(n_outer, n_inner, parts, axis, x_ref, o_ref, got, send_sems, recv_sems):
    me = lax.axis_index(axis)
    ci = lax.rem(me, n_inner)
    yo = lax.div(me, n_inner)
    rows = x_ref.shape[0] // parts

    def device(c, y):
        return {axis: y * n_inner + c}

    def slot(c, y, p):
        return (c * n_outer + y) * parts + p

    def piece(p):
        return pl.ds(p * rows, rows)

    outer_peers = [lax.rem(yo + k, n_outer) for k in range(1, n_outer)]
    inner_peers = [lax.rem(ci + j, n_inner) for j in range(1, n_inner)]
    barrier = pltpu.get_barrier_semaphore()
    for y in outer_peers:
        pl.semaphore_signal(barrier, inc=1, device_id=device(ci, y), device_id_type=MESH)
    for c in inner_peers:
        pl.semaphore_signal(barrier, inc=1, device_id=device(c, yo), device_id_type=MESH)
    pl.semaphore_wait(barrier, len(outer_peers) + len(inner_peers))

    sends = []

    def send(src, c, y, p, to):
        copy = pltpu.make_async_remote_copy(
            src_ref=src,
            dst_ref=got.at[c, y, piece(p)],
            send_sem=send_sems.at[len(sends)],
            recv_sem=recv_sems.at[slot(c, y, p)],
            device_id=to,
            device_id_type=MESH,
        )
        copy.start()
        sends.append(copy)

    def receive(c, y, p):
        pltpu.make_async_remote_copy(
            src_ref=x_ref.at[piece(p)],
            dst_ref=got.at[c, y, piece(p)],
            send_sem=send_sems.at[0],
            recv_sem=recv_sems.at[slot(c, y, p)],
            device_id=device(c, y),
            device_id_type=MESH,
        ).wait_recv()

    for p in range(parts):
        for y in outer_peers:
            send(x_ref.at[piece(p)], ci, yo, p, device(ci, y))
        for c in inner_peers:
            send(x_ref.at[piece(p)], ci, yo, p, device(c, yo))
    o_ref[ci, yo] = x_ref[...]
    for p in range(parts):
        for k in range(1, n_outer):
            y = lax.rem(yo + n_outer - k, n_outer)
            receive(ci, y, p)
            for c in inner_peers:
                send(got.at[ci, y, piece(p)], ci, y, p, device(c, yo))
            o_ref[ci, y, piece(p)] = got[ci, y, piece(p)]
    for j in range(1, n_inner):
        c = lax.rem(ci + n_inner - j, n_inner)
        for p in range(parts):
            for k in range(n_outer):
                y = lax.rem(yo + k, n_outer)
                receive(c, y, p)
                o_ref[c, y, piece(p)] = got[c, y, piece(p)]
    for copy in sends:
        copy.wait_send()


def all_gather(x, axis, n, inner, collective_id):
    outer = n // inner
    shape = (inner, outer) + x.shape
    parts = next(p for p in (4, 2, 1) if x.shape[0] % (16 * p) == 0)
    got = pl.pallas_call(
        functools.partial(_gather_kernel, outer, inner, parts, axis),
        out_shape=jax.ShapeDtypeStruct(shape, x.dtype),
        in_specs=[pl.BlockSpec(memory_space=pltpu.VMEM)],
        out_specs=pl.BlockSpec(memory_space=pltpu.VMEM),
        scratch_shapes=[
            pltpu.VMEM(shape, x.dtype),
            pltpu.SemaphoreType.DMA((n * parts,)),
            pltpu.SemaphoreType.DMA((n * parts,)),
        ],
        compiler_params=pltpu.CompilerParams(
            collective_id=collective_id,
            has_side_effects=True,
            vmem_limit_bytes=min(3 * x.dtype.itemsize * math.prod(shape) + (8 << 20), 60 << 20),
        ),
    )(x)
    return got.reshape((n * x.shape[0],) + x.shape[1:])


def _reduce_kernel(n_o, s_o, n_i, s_i, chunks, axis, p_ref, o_ref, g1, b_ref, g2, s1, r1, s2, r2):
    me = lax.axis_index(axis)
    zi = lax.rem(lax.div(me, s_i), n_i)
    xo = lax.rem(lax.div(me, s_o), n_o)
    zc = n_i // chunks

    def device(x, z):
        return {axis: me + (x - xo) * s_o + (z - zi) * s_i}

    barrier = pltpu.get_barrier_semaphore()
    for k in range(1, n_o):
        pl.semaphore_signal(
            barrier, inc=1, device_id=device(lax.rem(xo + k, n_o), zi), device_id_type=MESH
        )
    for k in range(1, n_i):
        pl.semaphore_signal(
            barrier, inc=1, device_id=device(xo, lax.rem(zi + k, n_i)), device_id_type=MESH
        )
    pl.semaphore_wait(barrier, n_o + n_i - 2)

    def along_x(k, c, to, dst_x):
        blocks = pl.ds(c * zc, zc)
        return pltpu.make_async_remote_copy(
            src_ref=p_ref.at[to, blocks],
            dst_ref=g1.at[dst_x, blocks],
            send_sem=s1.at[k, c],
            recv_sem=r1.at[k, c],
            device_id=device(to, zi),
            device_id_type=MESH,
        )

    def along_z(k, z):
        return pltpu.make_async_remote_copy(
            src_ref=b_ref.at[z],
            dst_ref=g2.at[zi],
            send_sem=s2.at[k],
            recv_sem=r2.at[k],
            device_id=device(xo, z),
            device_id_type=MESH,
        )

    first = []
    for c in range(chunks):
        for k in range(1, n_o):
            copy = along_x(k, c, lax.rem(xo + k, n_o), xo)
            copy.start()
            first.append(copy)
    sources = [lax.rem(xo + n_o - k, n_o) for k in range(1, n_o)]
    for c in range(chunks):
        for k in range(1, n_o):
            pltpu.make_async_remote_copy(
                src_ref=p_ref.at[sources[k - 1], pl.ds(c * zc, zc)],
                dst_ref=g1.at[sources[k - 1], pl.ds(c * zc, zc)],
                send_sem=s1.at[k, c],
                recv_sem=r1.at[k, c],
                device_id=device(sources[k - 1], zi),
                device_id_type=MESH,
            ).wait_recv()
        for z in range(c * zc, (c + 1) * zc):
            total = p_ref[xo, z].astype(jnp.float32)
            for src in sources:
                total = total + g1[src, z].astype(jnp.float32)
            b_ref[z] = total.astype(b_ref.dtype)
            offset = lax.rem(z - zi + n_i, n_i)

            @pl.when(offset == 0)
            def _():
                o_ref[...] = total

            @pl.when(offset != 0)
            def _():
                along_z(offset, z).start()

    for k in range(1, n_i):
        src = lax.rem(zi + n_i - k, n_i)
        pltpu.make_async_remote_copy(
            src_ref=b_ref.at[src],
            dst_ref=g2.at[src],
            send_sem=s2.at[k],
            recv_sem=r2.at[k],
            device_id=device(xo, src),
            device_id_type=MESH,
        ).wait_recv()
        o_ref[...] = o_ref[...] + g2[src].astype(jnp.float32)
    for copy in first:
        copy.wait_send()
    for z in range(n_i):
        offset = lax.rem(z - zi + n_i, n_i)

        @pl.when(offset != 0)
        def _():
            along_z(offset, z).wait_send()


def reduce_scatter_2d(x, axis, first, second, collective_id):
    (n_o, s_o), (n_i, s_i) = first, second
    chunks = next(c for c in (8, 4, 2, 1) if n_i % c == 0)
    return pl.pallas_call(
        functools.partial(_reduce_kernel, n_o, s_o, n_i, s_i, chunks, axis),
        out_shape=jax.ShapeDtypeStruct(x.shape[2:], jnp.float32),
        in_specs=[pl.BlockSpec(memory_space=pltpu.VMEM)],
        out_specs=pl.BlockSpec(memory_space=pltpu.VMEM),
        scratch_shapes=[
            pltpu.VMEM(x.shape, x.dtype),
            pltpu.VMEM(x.shape[1:], x.dtype),
            pltpu.VMEM(x.shape[1:], x.dtype),
            pltpu.SemaphoreType.DMA((n_o, chunks)),
            pltpu.SemaphoreType.DMA((n_o, chunks)),
            pltpu.SemaphoreType.DMA((n_i,)),
            pltpu.SemaphoreType.DMA((n_i,)),
        ],
        compiler_params=pltpu.CompilerParams(
            collective_id=collective_id,
            has_side_effects=True,
            vmem_limit_bytes=min(4 * x.dtype.itemsize * x.size + (8 << 20), 60 << 20),
        ),
    )(x)


def inner_size(devices):
    coords = [tuple(getattr(d, "coords", ())) for d in devices]
    if len(coords) < 2 or not coords[0]:
        return len(coords)
    varying = [c for c in range(len(coords[0])) if len({p[c] for p in coords}) > 1]
    slow = [c for c in varying if coords[1][c] == coords[0][c]]
    if not slow:
        return 1
    run = 0
    while run < len(coords) and coords[run][slow[0]] == coords[0][slow[0]]:
        run += 1
    return run


def per_device(n_sub, mass_inner, sub_inner, spectra, w_in, w_out, partner_rows, pair_counts, pair_labels):
    own_rows = spectra.shape[0]
    peers = partner_rows.shape[2]
    slots = partner_rows.shape[3]
    shard_rows = all_gather(spectra, "sub", n_sub, sub_inner, 2)
    pre = jnp.dot(shard_rows, w_in, preferred_element_type=jnp.float32)
    hidden = jax.nn.silu(pre).astype(jnp.bfloat16)
    embed_part = jnp.dot(hidden, w_out, preferred_element_type=jnp.float32)
    sub_outer = n_sub // sub_inner
    embed = reduce_scatter_2d(
        embed_part.reshape(sub_inner, sub_outer, own_rows, embed_part.shape[1]),
        "sub",
        (sub_inner, 1),
        (sub_outer, sub_inner),
        4,
    )
    norm = jnp.sqrt(jnp.sum(embed * embed, axis=-1, keepdims=True) + 1e-06)
    unit = embed / norm
    unit_b = unit.astype(jnp.bfloat16)
    flat_rows = partner_rows.reshape(peers * slots)
    selector = flat_rows[:, None] == jnp.arange(own_rows, dtype=jnp.int32)[None, :]
    mine = jnp.dot(
        selector.astype(jnp.bfloat16), unit_b, preferred_element_type=jnp.float32
    ).astype(jnp.bfloat16)
    outgoing = mine.reshape(peers, slots, mine.shape[1])
    incoming = exchange(outgoing, "mass", peers, 1)
    theirs = incoming.astype(jnp.float32)
    sim = jnp.sum(outgoing.astype(jnp.float32) * theirs, axis=-1)
    valid = jnp.arange(slots, dtype=jnp.int32)[None, :] < pair_counts.reshape(peers)[:, None]
    labels = pair_labels.reshape(peers, slots).astype(jnp.float32)
    coef = jnp.where(valid, 2.0 * (sim - labels), jnp.float32(0.0))
    weighted = (coef[..., None] * theirs).reshape(peers * slots, theirs.shape[2])
    grad_unit = lax.dot_general(
        selector.astype(jnp.float32),
        weighted,
        (((0,), (0,)), ((), ())),
        precision=lax.Precision.HIGHEST,
    )
    along = jnp.sum(unit * grad_unit, axis=-1, keepdims=True)
    grad_embed = ((grad_unit - unit * along) / norm).astype(jnp.bfloat16)
    grad_rows = all_gather(grad_embed, "sub", n_sub, sub_inner, 6)
    back = lax.dot_general(
        grad_rows, w_out, (((1,), (1,)), ((), ())), preferred_element_type=jnp.float32
    )
    gate = jax.nn.sigmoid(pre)
    grad_pre = lax.optimization_barrier(
        (back * gate * (1.0 + pre * (1.0 - gate))).astype(jnp.bfloat16)
    )
    out_part = lax.dot_general(
        grad_rows, hidden, (((0,), (0,)), ((), ())), preferred_element_type=jnp.float32
    )
    in_part_t = lax.dot_general(
        grad_pre, shard_rows, (((0,), (0,)), ((), ())), preferred_element_type=jnp.float32
    )
    n_mass = peers
    hid = in_part_t.shape[0]
    in_cols = in_part_t.shape[1] // n_mass
    out_rows = out_part.shape[0] // n_mass
    lanes = in_cols
    partial = jnp.concatenate(
        [
            jnp.swapaxes(in_part_t.astype(jnp.bfloat16).reshape(hid, n_mass, in_cols), 0, 1),
            out_part.astype(jnp.bfloat16).reshape(n_mass, out_rows * hid // lanes, lanes),
        ],
        axis=1,
    )
    mass_outer = n_mass // mass_inner
    summed = reduce_scatter_2d(
        partial.reshape((mass_outer, mass_inner) + partial.shape[1:]),
        "mass",
        (mass_outer, mass_inner),
        (mass_inner, 1),
        8,
    )
    grad_in = summed[:hid].T
    grad_out_t = summed[hid:].reshape(out_rows, hid)
    return (grad_in, grad_out_t)


def solution(mesh):
    placed = (
        P(("mass", "sub"), None),
        P(None, "sub"),
        P("sub", None),
        P("mass", "sub", None, None),
        P("mass", "sub", None),
        P("mass", "sub", None, None),
    )
    mass_inner = inner_size(list(mesh.devices[:, 0]))
    sub_inner = inner_size(list(mesh.devices[0, :]))
    return jax.shard_map(
        functools.partial(per_device, mesh.shape["sub"], mass_inner, sub_inner),
        mesh=mesh,
        in_specs=placed,
        out_specs=(P("mass", "sub"), P("mass", "sub")),
        check_vma=False,
    )
```

```python
import functools
import math

import jax
import jax.numpy as jnp
from jax import lax
from jax.experimental import pallas as pl
from jax.experimental.pallas import tpu as pltpu
from jax.sharding import PartitionSpec as P

MESH = pl.DeviceIdType.MESH


def _exchange_kernel(n, stride, axis, gather, x_ref, o_ref, got, send_sems, recv_sems):
    me = lax.axis_index(axis)
    mine = lax.rem(lax.div(me, stride), n)
    base = me - mine * stride

    def member(j):
        return base + j * stride

    barrier = pltpu.get_barrier_semaphore()
    for k in range(1, n):
        pl.semaphore_signal(
            barrier, inc=1, device_id={axis: member(lax.rem(mine + k, n))}, device_id_type=MESH
        )
    pl.semaphore_wait(barrier, n - 1)
    sends = []
    for k in range(1, n):
        peer = lax.rem(mine + k, n)
        copy = pltpu.make_async_remote_copy(
            src_ref=x_ref if gather else x_ref.at[peer],
            dst_ref=got.at[mine],
            send_sem=send_sems.at[k],
            recv_sem=recv_sems.at[k],
            device_id={axis: member(peer)},
            device_id_type=MESH,
        )
        copy.start()
        sends.append(copy)
    o_ref[mine] = x_ref[...] if gather else x_ref[mine]
    for k in range(1, n):
        sends[k - 1].wait_send()
        source = lax.rem(mine + n - k, n)
        pltpu.make_async_remote_copy(
            src_ref=x_ref if gather else x_ref.at[source],
            dst_ref=got.at[source],
            send_sem=send_sems.at[k],
            recv_sem=recv_sems.at[k],
            device_id={axis: member(source)},
            device_id_type=MESH,
        ).wait_recv()
        o_ref[source] = got[source]


def exchange(x, axis, n, collective_id, gather=False, stride=1):
    shape = (n,) + x.shape if gather else x.shape
    return pl.pallas_call(
        functools.partial(_exchange_kernel, n, stride, axis, gather),
        out_shape=jax.ShapeDtypeStruct(shape, x.dtype),
        in_specs=[pl.BlockSpec(memory_space=pltpu.VMEM)],
        out_specs=pl.BlockSpec(memory_space=pltpu.VMEM),
        scratch_shapes=[
            pltpu.VMEM(shape, x.dtype),
            pltpu.SemaphoreType.DMA((n,)),
            pltpu.SemaphoreType.DMA((n,)),
        ],
        compiler_params=pltpu.CompilerParams(
            collective_id=collective_id,
            has_side_effects=True,
            vmem_limit_bytes=min(3 * x.dtype.itemsize * math.prod(shape) + (8 << 20), 60 << 20),
        ),
    )(x)


def reduce_scatter(x, axis, inner, first_inner, first_id):
    outer = x.shape[0] // inner
    if first_inner:
        blocks = x.reshape((inner, outer) + x.shape[1:])
        phases = [(inner, 1), (outer, inner)]
    else:
        blocks = x.reshape((outer, inner) + x.shape[1:])
        phases = [(outer, inner), (inner, 1)]
    for number, (size, stride) in enumerate(phases):
        if size == 1:
            blocks = blocks[0].astype(jnp.float32)
            continue
        got = exchange(blocks.astype(x.dtype), axis, size, first_id + number, stride=stride)
        blocks = jnp.sum(got.astype(jnp.float32), axis=0)
    return blocks


def _gather_kernel(n_outer, n_inner, parts, axis, x_ref, o_ref, got, send_sems, recv_sems):
    me = lax.axis_index(axis)
    ci = lax.rem(me, n_inner)
    yo = lax.div(me, n_inner)
    rows = x_ref.shape[0] // parts

    def device(c, y):
        return {axis: y * n_inner + c}

    def slot(c, y, p):
        return (c * n_outer + y) * parts + p

    def piece(p):
        return pl.ds(p * rows, rows)

    outer_peers = [lax.rem(yo + k, n_outer) for k in range(1, n_outer)]
    inner_peers = [lax.rem(ci + j, n_inner) for j in range(1, n_inner)]
    barrier = pltpu.get_barrier_semaphore()
    for y in outer_peers:
        pl.semaphore_signal(barrier, inc=1, device_id=device(ci, y), device_id_type=MESH)
    for c in inner_peers:
        pl.semaphore_signal(barrier, inc=1, device_id=device(c, yo), device_id_type=MESH)
    pl.semaphore_wait(barrier, len(outer_peers) + len(inner_peers))

    sends = []

    def send(src, c, y, p, to):
        copy = pltpu.make_async_remote_copy(
            src_ref=src,
            dst_ref=got.at[c, y, piece(p)],
            send_sem=send_sems.at[len(sends)],
            recv_sem=recv_sems.at[slot(c, y, p)],
            device_id=to,
            device_id_type=MESH,
        )
        copy.start()
        sends.append(copy)

    def receive(c, y, p):
        pltpu.make_async_remote_copy(
            src_ref=x_ref.at[piece(p)],
            dst_ref=got.at[c, y, piece(p)],
            send_sem=send_sems.at[0],
            recv_sem=recv_sems.at[slot(c, y, p)],
            device_id=device(c, y),
            device_id_type=MESH,
        ).wait_recv()

    for p in range(parts):
        for y in outer_peers:
            send(x_ref.at[piece(p)], ci, yo, p, device(ci, y))
        for c in inner_peers:
            send(x_ref.at[piece(p)], ci, yo, p, device(c, yo))
    o_ref[ci, yo] = x_ref[...]
    for p in range(parts):
        for k in range(1, n_outer):
            y = lax.rem(yo + n_outer - k, n_outer)
            receive(ci, y, p)
            for c in inner_peers:
                send(got.at[ci, y, piece(p)], ci, y, p, device(c, yo))
            o_ref[ci, y, piece(p)] = got[ci, y, piece(p)]
    for j in range(1, n_inner):
        c = lax.rem(ci + n_inner - j, n_inner)
        for p in range(parts):
            for k in range(n_outer):
                y = lax.rem(yo + k, n_outer)
                receive(c, y, p)
                o_ref[c, y, piece(p)] = got[c, y, piece(p)]
    for copy in sends:
        copy.wait_send()


def all_gather(x, axis, n, inner, collective_id):
    outer = n // inner
    shape = (inner, outer) + x.shape
    parts = next(p for p in (8, 4, 2, 1) if x.shape[0] % (16 * p) == 0)
    got = pl.pallas_call(
        functools.partial(_gather_kernel, outer, inner, parts, axis),
        out_shape=jax.ShapeDtypeStruct(shape, x.dtype),
        in_specs=[pl.BlockSpec(memory_space=pltpu.VMEM)],
        out_specs=pl.BlockSpec(memory_space=pltpu.VMEM),
        scratch_shapes=[
            pltpu.VMEM(shape, x.dtype),
            pltpu.SemaphoreType.DMA((n * parts,)),
            pltpu.SemaphoreType.DMA((n * parts,)),
        ],
        compiler_params=pltpu.CompilerParams(
            collective_id=collective_id,
            has_side_effects=True,
            vmem_limit_bytes=min(3 * x.dtype.itemsize * math.prod(shape) + (8 << 20), 60 << 20),
        ),
    )(x)
    return got.reshape((n * x.shape[0],) + x.shape[1:])


def _reduce_kernel(n_o, s_o, n_i, s_i, chunks, axis, p_ref, o_ref, g1, b_ref, g2, s1, r1, s2, r2):
    me = lax.axis_index(axis)
    zi = lax.rem(lax.div(me, s_i), n_i)
    xo = lax.rem(lax.div(me, s_o), n_o)
    zc = n_i // chunks

    def device(x, z):
        return {axis: me + (x - xo) * s_o + (z - zi) * s_i}

    barrier = pltpu.get_barrier_semaphore()
    for k in range(1, n_o):
        pl.semaphore_signal(
            barrier, inc=1, device_id=device(lax.rem(xo + k, n_o), zi), device_id_type=MESH
        )
    for k in range(1, n_i):
        pl.semaphore_signal(
            barrier, inc=1, device_id=device(xo, lax.rem(zi + k, n_i)), device_id_type=MESH
        )
    pl.semaphore_wait(barrier, n_o + n_i - 2)

    def along_x(k, c, to, dst_x):
        blocks = pl.ds(c * zc, zc)
        return pltpu.make_async_remote_copy(
            src_ref=p_ref.at[to, blocks],
            dst_ref=g1.at[dst_x, blocks],
            send_sem=s1.at[k, c],
            recv_sem=r1.at[k, c],
            device_id=device(to, zi),
            device_id_type=MESH,
        )

    def along_z(k, z):
        return pltpu.make_async_remote_copy(
            src_ref=b_ref.at[z],
            dst_ref=g2.at[zi],
            send_sem=s2.at[k],
            recv_sem=r2.at[k],
            device_id=device(xo, z),
            device_id_type=MESH,
        )

    first = []
    for c in range(chunks):
        for k in range(1, n_o):
            copy = along_x(k, c, lax.rem(xo + k, n_o), xo)
            copy.start()
            first.append(copy)
    sources = [lax.rem(xo + n_o - k, n_o) for k in range(1, n_o)]
    for c in range(chunks):
        for k in range(1, n_o):
            pltpu.make_async_remote_copy(
                src_ref=p_ref.at[sources[k - 1], pl.ds(c * zc, zc)],
                dst_ref=g1.at[sources[k - 1], pl.ds(c * zc, zc)],
                send_sem=s1.at[k, c],
                recv_sem=r1.at[k, c],
                device_id=device(sources[k - 1], zi),
                device_id_type=MESH,
            ).wait_recv()
        for z in range(c * zc, (c + 1) * zc):
            total = p_ref[xo, z].astype(jnp.float32)
            for src in sources:
                total = total + g1[src, z].astype(jnp.float32)
            b_ref[z] = total.astype(b_ref.dtype)
            offset = lax.rem(z - zi + n_i, n_i)

            @pl.when(offset == 0)
            def _():
                o_ref[...] = total

            @pl.when(offset != 0)
            def _():
                along_z(offset, z).start()

    for k in range(1, n_i):
        src = lax.rem(zi + n_i - k, n_i)
        pltpu.make_async_remote_copy(
            src_ref=b_ref.at[src],
            dst_ref=g2.at[src],
            send_sem=s2.at[k],
            recv_sem=r2.at[k],
            device_id=device(xo, src),
            device_id_type=MESH,
        ).wait_recv()
        o_ref[...] = o_ref[...] + g2[src].astype(jnp.float32)
    for copy in first:
        copy.wait_send()
    for z in range(n_i):
        offset = lax.rem(z - zi + n_i, n_i)

        @pl.when(offset != 0)
        def _():
            along_z(offset, z).wait_send()


def reduce_scatter_2d(x, axis, first, second, collective_id):
    (n_o, s_o), (n_i, s_i) = first, second
    chunks = next(c for c in (8, 4, 2, 1) if n_i % c == 0)
    return pl.pallas_call(
        functools.partial(_reduce_kernel, n_o, s_o, n_i, s_i, chunks, axis),
        out_shape=jax.ShapeDtypeStruct(x.shape[2:], jnp.float32),
        in_specs=[pl.BlockSpec(memory_space=pltpu.VMEM)],
        out_specs=pl.BlockSpec(memory_space=pltpu.VMEM),
        scratch_shapes=[
            pltpu.VMEM(x.shape, x.dtype),
            pltpu.VMEM(x.shape[1:], x.dtype),
            pltpu.VMEM(x.shape[1:], x.dtype),
            pltpu.SemaphoreType.DMA((n_o, chunks)),
            pltpu.SemaphoreType.DMA((n_o, chunks)),
            pltpu.SemaphoreType.DMA((n_i,)),
            pltpu.SemaphoreType.DMA((n_i,)),
        ],
        compiler_params=pltpu.CompilerParams(
            collective_id=collective_id,
            has_side_effects=True,
            vmem_limit_bytes=min(4 * x.dtype.itemsize * x.size + (8 << 20), 60 << 20),
        ),
    )(x)


def inner_size(devices):
    coords = [tuple(getattr(d, "coords", ())) for d in devices]
    if len(coords) < 2 or not coords[0]:
        return len(coords)
    varying = [c for c in range(len(coords[0])) if len({p[c] for p in coords}) > 1]
    slow = [c for c in varying if coords[1][c] == coords[0][c]]
    if not slow:
        return 1
    run = 0
    while run < len(coords) and coords[run][slow[0]] == coords[0][slow[0]]:
        run += 1
    return run


def per_device(n_sub, mass_inner, sub_inner, spectra, w_in, w_out, partner_rows, pair_counts, pair_labels):
    own_rows = spectra.shape[0]
    peers = partner_rows.shape[2]
    slots = partner_rows.shape[3]
    shard_rows = all_gather(spectra, "sub", n_sub, sub_inner, 2)
    pre = jnp.dot(shard_rows, w_in, preferred_element_type=jnp.float32)
    hidden = jax.nn.silu(pre).astype(jnp.bfloat16)
    embed_part = jnp.dot(hidden, w_out, preferred_element_type=jnp.float32)
    sub_outer = n_sub // sub_inner
    embed = reduce_scatter_2d(
        embed_part.reshape(sub_inner, sub_outer, own_rows, embed_part.shape[1]),
        "sub",
        (sub_inner, 1),
        (sub_outer, sub_inner),
        4,
    )
    norm = jnp.sqrt(jnp.sum(embed * embed, axis=-1, keepdims=True) + 1e-06)
    unit = embed / norm
    unit_b = unit.astype(jnp.bfloat16)
    flat_rows = partner_rows.reshape(peers * slots)
    selector = flat_rows[:, None] == jnp.arange(own_rows, dtype=jnp.int32)[None, :]
    mine = jnp.dot(
        selector.astype(jnp.bfloat16), unit_b, preferred_element_type=jnp.float32
    ).astype(jnp.bfloat16)
    outgoing = mine.reshape(peers, slots, mine.shape[1])
    incoming = exchange(outgoing, "mass", peers, 1)
    theirs = incoming.astype(jnp.float32)
    sim = jnp.sum(outgoing.astype(jnp.float32) * theirs, axis=-1)
    valid = jnp.arange(slots, dtype=jnp.int32)[None, :] < pair_counts.reshape(peers)[:, None]
    labels = pair_labels.reshape(peers, slots).astype(jnp.float32)
    coef = jnp.where(valid, 2.0 * (sim - labels), jnp.float32(0.0))
    weighted = (coef[..., None] * theirs).reshape(peers * slots, theirs.shape[2])
    grad_unit = lax.dot_general(
        selector.astype(jnp.float32),
        weighted,
        (((0,), (0,)), ((), ())),
        precision=lax.Precision.HIGHEST,
    )
    along = jnp.sum(unit * grad_unit, axis=-1, keepdims=True)
    grad_embed = ((grad_unit - unit * along) / norm).astype(jnp.bfloat16)
    grad_rows = all_gather(grad_embed, "sub", n_sub, sub_inner, 6)
    back = lax.dot_general(
        grad_rows, w_out, (((1,), (1,)), ((), ())), preferred_element_type=jnp.float32
    )
    gate = jax.nn.sigmoid(pre)
    grad_pre = lax.optimization_barrier(
        (back * gate * (1.0 + pre * (1.0 - gate))).astype(jnp.bfloat16)
    )
    out_part = lax.dot_general(
        grad_rows, hidden, (((0,), (0,)), ((), ())), preferred_element_type=jnp.float32
    )
    in_part_t = lax.dot_general(
        grad_pre, shard_rows, (((0,), (0,)), ((), ())), preferred_element_type=jnp.float32
    )
    n_mass = peers
    hid = in_part_t.shape[0]
    in_cols = in_part_t.shape[1] // n_mass
    out_rows = out_part.shape[0] // n_mass
    lanes = in_cols
    partial = jnp.concatenate(
        [
            jnp.swapaxes(in_part_t.astype(jnp.bfloat16).reshape(hid, n_mass, in_cols), 0, 1),
            out_part.astype(jnp.bfloat16).reshape(n_mass, out_rows * hid // lanes, lanes),
        ],
        axis=1,
    )
    mass_outer = n_mass // mass_inner
    summed = reduce_scatter_2d(
        partial.reshape((mass_outer, mass_inner) + partial.shape[1:]),
        "mass",
        (mass_outer, mass_inner),
        (mass_inner, 1),
        8,
    )
    grad_in = summed[:hid].T
    grad_out_t = summed[hid:].reshape(out_rows, hid)
    return (grad_in, grad_out_t)


def solution(mesh):
    placed = (
        P(("mass", "sub"), None),
        P(None, "sub"),
        P("sub", None),
        P("mass", "sub", None, None),
        P("mass", "sub", None),
        P("mass", "sub", None, None),
    )
    mass_inner = inner_size(list(mesh.devices[:, 0]))
    sub_inner = inner_size(list(mesh.devices[0, :]))
    return jax.shard_map(
        functools.partial(per_device, mesh.shape["sub"], mass_inner, sub_inner),
        mesh=mesh,
        in_specs=placed,
        out_specs=(P("mass", "sub"), P("mass", "sub")),
        check_vma=False,
    )
```

```python
import functools
import math

import jax
import jax.numpy as jnp
from jax import lax
from jax.experimental import pallas as pl
from jax.experimental.pallas import tpu as pltpu
from jax.sharding import PartitionSpec as P

MESH = pl.DeviceIdType.MESH


def _exchange_kernel(n, stride, axis, gather, x_ref, o_ref, got, send_sems, recv_sems):
    me = lax.axis_index(axis)
    mine = lax.rem(lax.div(me, stride), n)
    base = me - mine * stride

    def member(j):
        return base + j * stride

    barrier = pltpu.get_barrier_semaphore()
    for k in range(1, n):
        pl.semaphore_signal(
            barrier, inc=1, device_id={axis: member(lax.rem(mine + k, n))}, device_id_type=MESH
        )
    pl.semaphore_wait(barrier, n - 1)
    sends = []
    for k in range(1, n):
        peer = lax.rem(mine + k, n)
        copy = pltpu.make_async_remote_copy(
            src_ref=x_ref if gather else x_ref.at[peer],
            dst_ref=got.at[mine],
            send_sem=send_sems.at[k],
            recv_sem=recv_sems.at[k],
            device_id={axis: member(peer)},
            device_id_type=MESH,
        )
        copy.start()
        sends.append(copy)
    o_ref[mine] = x_ref[...] if gather else x_ref[mine]
    for k in range(1, n):
        sends[k - 1].wait_send()
        source = lax.rem(mine + n - k, n)
        pltpu.make_async_remote_copy(
            src_ref=x_ref if gather else x_ref.at[source],
            dst_ref=got.at[source],
            send_sem=send_sems.at[k],
            recv_sem=recv_sems.at[k],
            device_id={axis: member(source)},
            device_id_type=MESH,
        ).wait_recv()
        o_ref[source] = got[source]


def exchange(x, axis, n, collective_id, gather=False, stride=1):
    shape = (n,) + x.shape if gather else x.shape
    return pl.pallas_call(
        functools.partial(_exchange_kernel, n, stride, axis, gather),
        out_shape=jax.ShapeDtypeStruct(shape, x.dtype),
        in_specs=[pl.BlockSpec(memory_space=pltpu.VMEM)],
        out_specs=pl.BlockSpec(memory_space=pltpu.VMEM),
        scratch_shapes=[
            pltpu.VMEM(shape, x.dtype),
            pltpu.SemaphoreType.DMA((n,)),
            pltpu.SemaphoreType.DMA((n,)),
        ],
        compiler_params=pltpu.CompilerParams(
            collective_id=collective_id,
            has_side_effects=True,
            vmem_limit_bytes=min(3 * x.dtype.itemsize * math.prod(shape) + (8 << 20), 60 << 20),
        ),
    )(x)


def reduce_scatter(x, axis, inner, first_inner, first_id):
    outer = x.shape[0] // inner
    if first_inner:
        blocks = x.reshape((inner, outer) + x.shape[1:])
        phases = [(inner, 1), (outer, inner)]
    else:
        blocks = x.reshape((outer, inner) + x.shape[1:])
        phases = [(outer, inner), (inner, 1)]
    for number, (size, stride) in enumerate(phases):
        if size == 1:
            blocks = blocks[0].astype(jnp.float32)
            continue
        got = exchange(blocks.astype(x.dtype), axis, size, first_id + number, stride=stride)
        blocks = jnp.sum(got.astype(jnp.float32), axis=0)
    return blocks


def _gather_kernel(n_outer, n_inner, parts, axis, x_ref, o_ref, got, send_sems, recv_sems):
    me = lax.axis_index(axis)
    ci = lax.rem(me, n_inner)
    yo = lax.div(me, n_inner)
    rows = x_ref.shape[0] // parts

    def device(c, y):
        return {axis: y * n_inner + c}

    def slot(c, y, p):
        return (c * n_outer + y) * parts + p

    def piece(p):
        return pl.ds(p * rows, rows)

    outer_peers = [lax.rem(yo + k, n_outer) for k in range(1, n_outer)]
    inner_peers = [lax.rem(ci + j, n_inner) for j in range(1, n_inner)]
    barrier = pltpu.get_barrier_semaphore()
    for y in outer_peers:
        pl.semaphore_signal(barrier, inc=1, device_id=device(ci, y), device_id_type=MESH)
    for c in inner_peers:
        pl.semaphore_signal(barrier, inc=1, device_id=device(c, yo), device_id_type=MESH)
    pl.semaphore_wait(barrier, len(outer_peers) + len(inner_peers))

    sends = []

    def send(src, c, y, p, to):
        copy = pltpu.make_async_remote_copy(
            src_ref=src,
            dst_ref=got.at[c, y, piece(p)],
            send_sem=send_sems.at[len(sends)],
            recv_sem=recv_sems.at[slot(c, y, p)],
            device_id=to,
            device_id_type=MESH,
        )
        copy.start()
        sends.append(copy)

    def receive(c, y, p):
        pltpu.make_async_remote_copy(
            src_ref=x_ref.at[piece(p)],
            dst_ref=got.at[c, y, piece(p)],
            send_sem=send_sems.at[0],
            recv_sem=recv_sems.at[slot(c, y, p)],
            device_id=device(c, y),
            device_id_type=MESH,
        ).wait_recv()

    for p in range(parts):
        for y in outer_peers:
            send(x_ref.at[piece(p)], ci, yo, p, device(ci, y))
        for c in inner_peers:
            send(x_ref.at[piece(p)], ci, yo, p, device(c, yo))
    o_ref[ci, yo] = x_ref[...]
    for p in range(parts):
        for k in range(1, n_outer):
            y = lax.rem(yo + n_outer - k, n_outer)
            receive(ci, y, p)
            for c in inner_peers:
                send(got.at[ci, y, piece(p)], ci, y, p, device(c, yo))
            o_ref[ci, y, piece(p)] = got[ci, y, piece(p)]
    for j in range(1, n_inner):
        c = lax.rem(ci + n_inner - j, n_inner)
        for p in range(parts):
            for k in range(n_outer):
                y = lax.rem(yo + k, n_outer)
                receive(c, y, p)
                o_ref[c, y, piece(p)] = got[c, y, piece(p)]
    for copy in sends:
        copy.wait_send()


def all_gather(x, axis, n, inner, collective_id):
    outer = n // inner
    shape = (inner, outer) + x.shape
    parts = next(p for p in (4, 2, 1) if x.shape[0] % (16 * p) == 0)
    got = pl.pallas_call(
        functools.partial(_gather_kernel, outer, inner, parts, axis),
        out_shape=jax.ShapeDtypeStruct(shape, x.dtype),
        in_specs=[pl.BlockSpec(memory_space=pltpu.VMEM)],
        out_specs=pl.BlockSpec(memory_space=pltpu.VMEM),
        scratch_shapes=[
            pltpu.VMEM(shape, x.dtype),
            pltpu.SemaphoreType.DMA((n * parts,)),
            pltpu.SemaphoreType.DMA((n * parts,)),
        ],
        compiler_params=pltpu.CompilerParams(
            collective_id=collective_id,
            has_side_effects=True,
            vmem_limit_bytes=min(3 * x.dtype.itemsize * math.prod(shape) + (8 << 20), 60 << 20),
        ),
    )(x)
    return got.reshape((n * x.shape[0],) + x.shape[1:])


def _reduce_kernel(n_o, s_o, n_i, s_i, chunks, halves, axis, p_ref, o_ref, g1, b_ref, g2, s1, r1, s2, r2):
    me = lax.axis_index(axis)
    zi = lax.rem(lax.div(me, s_i), n_i)
    xo = lax.rem(lax.div(me, s_o), n_o)
    zc = n_i // chunks
    rh = p_ref.shape[2] // halves

    def device(x, z):
        return {axis: me + (x - xo) * s_o + (z - zi) * s_i}

    def half(h):
        return pl.ds(h * rh, rh)

    barrier = pltpu.get_barrier_semaphore()
    for k in range(1, n_o):
        pl.semaphore_signal(
            barrier, inc=1, device_id=device(lax.rem(xo + k, n_o), zi), device_id_type=MESH
        )
    for k in range(1, n_i):
        pl.semaphore_signal(
            barrier, inc=1, device_id=device(xo, lax.rem(zi + k, n_i)), device_id_type=MESH
        )
    pl.semaphore_wait(barrier, n_o + n_i - 2)

    def along_x(k, c, h, to, dst_x):
        blocks = pl.ds(c * zc, zc)
        return pltpu.make_async_remote_copy(
            src_ref=p_ref.at[to, blocks, half(h)],
            dst_ref=g1.at[dst_x, blocks, half(h)],
            send_sem=s1.at[k, c * halves + h],
            recv_sem=r1.at[k, c * halves + h],
            device_id=device(to, zi),
            device_id_type=MESH,
        )

    def along_z(k, z, h):
        return pltpu.make_async_remote_copy(
            src_ref=b_ref.at[z, half(h)],
            dst_ref=g2.at[zi, half(h)],
            send_sem=s2.at[k, h],
            recv_sem=r2.at[k, h],
            device_id=device(xo, z),
            device_id_type=MESH,
        )

    first = []
    for c in range(chunks):
        for h in range(halves):
            for k in range(1, n_o):
                copy = along_x(k, c, h, lax.rem(xo + k, n_o), xo)
                copy.start()
                first.append(copy)
    sources = [lax.rem(xo + n_o - k, n_o) for k in range(1, n_o)]
    for c in range(chunks):
        for h in range(halves):
            for k in range(1, n_o):
                along_x(k, c, h, sources[k - 1], sources[k - 1]).wait_recv()
            for z in range(c * zc, (c + 1) * zc):
                total = p_ref[xo, z, half(h)].astype(jnp.float32)
                for src in sources:
                    total = total + g1[src, z, half(h)].astype(jnp.float32)
                b_ref[z, half(h)] = total.astype(b_ref.dtype)
                offset = lax.rem(z - zi + n_i, n_i)

                @pl.when(offset == 0)
                def _():
                    o_ref[half(h)] = total

                @pl.when(offset != 0)
                def _():
                    along_z(offset, z, h).start()

    for k in range(1, n_i):
        src = lax.rem(zi + n_i - k, n_i)
        for h in range(halves):
            pltpu.make_async_remote_copy(
                src_ref=b_ref.at[src, half(h)],
                dst_ref=g2.at[src, half(h)],
                send_sem=s2.at[k, h],
                recv_sem=r2.at[k, h],
                device_id=device(xo, src),
                device_id_type=MESH,
            ).wait_recv()
            o_ref[half(h)] = o_ref[half(h)] + g2[src, half(h)].astype(jnp.float32)
    for copy in first:
        copy.wait_send()
    for z in range(n_i):
        offset = lax.rem(z - zi + n_i, n_i)
        for h in range(halves):

            @pl.when(offset != 0)
            def _():
                along_z(offset, z, h).wait_send()


def reduce_scatter_2d(x, axis, first, second, collective_id):
    (n_o, s_o), (n_i, s_i) = first, second
    chunks = next(c for c in (8, 4, 2, 1) if n_i % c == 0)
    halves = 2 if x.shape[2] % 32 == 0 else 1
    return pl.pallas_call(
        functools.partial(_reduce_kernel, n_o, s_o, n_i, s_i, chunks, halves, axis),
        out_shape=jax.ShapeDtypeStruct(x.shape[2:], jnp.float32),
        in_specs=[pl.BlockSpec(memory_space=pltpu.VMEM)],
        out_specs=pl.BlockSpec(memory_space=pltpu.VMEM),
        scratch_shapes=[
            pltpu.VMEM(x.shape, x.dtype),
            pltpu.VMEM(x.shape[1:], x.dtype),
            pltpu.VMEM(x.shape[1:], x.dtype),
            pltpu.SemaphoreType.DMA((n_o, chunks * halves)),
            pltpu.SemaphoreType.DMA((n_o, chunks * halves)),
            pltpu.SemaphoreType.DMA((n_i, halves)),
            pltpu.SemaphoreType.DMA((n_i, halves)),
        ],
        compiler_params=pltpu.CompilerParams(
            collective_id=collective_id,
            has_side_effects=True,
            vmem_limit_bytes=min(4 * x.dtype.itemsize * x.size + (8 << 20), 60 << 20),
        ),
    )(x)


def inner_size(devices):
    coords = [tuple(getattr(d, "coords", ())) for d in devices]
    if len(coords) < 2 or not coords[0]:
        return len(coords)
    varying = [c for c in range(len(coords[0])) if len({p[c] for p in coords}) > 1]
    slow = [c for c in varying if coords[1][c] == coords[0][c]]
    if not slow:
        return 1
    run = 0
    while run < len(coords) and coords[run][slow[0]] == coords[0][slow[0]]:
        run += 1
    return run


def per_device(n_sub, mass_inner, sub_inner, spectra, w_in, w_out, partner_rows, pair_counts, pair_labels):
    own_rows = spectra.shape[0]
    peers = partner_rows.shape[2]
    slots = partner_rows.shape[3]
    shard_rows = all_gather(spectra, "sub", n_sub, sub_inner, 2)
    pre = jnp.dot(shard_rows, w_in, preferred_element_type=jnp.float32)
    hidden = jax.nn.silu(pre).astype(jnp.bfloat16)
    embed_part = jnp.dot(hidden, w_out, preferred_element_type=jnp.float32)
    sub_outer = n_sub // sub_inner
    embed = reduce_scatter_2d(
        embed_part.reshape(sub_inner, sub_outer, own_rows, embed_part.shape[1]),
        "sub",
        (sub_inner, 1),
        (sub_outer, sub_inner),
        4,
    )
    norm = jnp.sqrt(jnp.sum(embed * embed, axis=-1, keepdims=True) + 1e-06)
    unit = embed / norm
    unit_b = unit.astype(jnp.bfloat16)
    flat_rows = partner_rows.reshape(peers * slots)
    selector = flat_rows[:, None] == jnp.arange(own_rows, dtype=jnp.int32)[None, :]
    mine = jnp.dot(
        selector.astype(jnp.bfloat16), unit_b, preferred_element_type=jnp.float32
    ).astype(jnp.bfloat16)
    outgoing = mine.reshape(peers, slots, mine.shape[1])
    incoming = exchange(outgoing, "mass", peers, 1)
    theirs = incoming.astype(jnp.float32)
    sim = jnp.sum(outgoing.astype(jnp.float32) * theirs, axis=-1)
    valid = jnp.arange(slots, dtype=jnp.int32)[None, :] < pair_counts.reshape(peers)[:, None]
    labels = pair_labels.reshape(peers, slots).astype(jnp.float32)
    coef = jnp.where(valid, 2.0 * (sim - labels), jnp.float32(0.0))
    weighted = (coef[..., None] * theirs).reshape(peers * slots, theirs.shape[2])
    grad_unit = lax.dot_general(
        selector.astype(jnp.float32),
        weighted,
        (((0,), (0,)), ((), ())),
        precision=lax.Precision.HIGHEST,
    )
    along = jnp.sum(unit * grad_unit, axis=-1, keepdims=True)
    grad_embed = ((grad_unit - unit * along) / norm).astype(jnp.bfloat16)
    grad_rows = all_gather(grad_embed, "sub", n_sub, sub_inner, 6)
    back = lax.dot_general(
        grad_rows, w_out, (((1,), (1,)), ((), ())), preferred_element_type=jnp.float32
    )
    gate = jax.nn.sigmoid(pre)
    grad_pre = lax.optimization_barrier(
        (back * gate * (1.0 + pre * (1.0 - gate))).astype(jnp.bfloat16)
    )
    out_part = lax.dot_general(
        grad_rows, hidden, (((0,), (0,)), ((), ())), preferred_element_type=jnp.float32
    )
    in_part_t = lax.dot_general(
        grad_pre, shard_rows, (((0,), (0,)), ((), ())), preferred_element_type=jnp.float32
    )
    n_mass = peers
    hid = in_part_t.shape[0]
    in_cols = in_part_t.shape[1] // n_mass
    out_rows = out_part.shape[0] // n_mass
    lanes = in_cols
    partial = jnp.concatenate(
        [
            jnp.swapaxes(in_part_t.astype(jnp.bfloat16).reshape(hid, n_mass, in_cols), 0, 1),
            out_part.astype(jnp.bfloat16).reshape(n_mass, out_rows * hid // lanes, lanes),
        ],
        axis=1,
    )
    mass_outer = n_mass // mass_inner
    summed = reduce_scatter_2d(
        partial.reshape((mass_outer, mass_inner) + partial.shape[1:]),
        "mass",
        (mass_outer, mass_inner),
        (mass_inner, 1),
        8,
    )
    grad_in = summed[:hid].T
    grad_out_t = summed[hid:].reshape(out_rows, hid)
    return (grad_in, grad_out_t)


def solution(mesh):
    placed = (
        P(("mass", "sub"), None),
        P(None, "sub"),
        P("sub", None),
        P("mass", "sub", None, None),
        P("mass", "sub", None),
        P("mass", "sub", None, None),
    )
    mass_inner = inner_size(list(mesh.devices[:, 0]))
    sub_inner = inner_size(list(mesh.devices[0, :]))
    return jax.shard_map(
        functools.partial(per_device, mesh.shape["sub"], mass_inner, sub_inner),
        mesh=mesh,
        in_specs=placed,
        out_specs=(P("mass", "sub"), P("mass", "sub")),
        check_vma=False,
    )
```

```python
import functools
import math

import jax
import jax.numpy as jnp
from jax import lax
from jax.experimental import pallas as pl
from jax.experimental.pallas import tpu as pltpu
from jax.sharding import PartitionSpec as P

MESH = pl.DeviceIdType.MESH


def _exchange_kernel(n, stride, axis, gather, x_ref, o_ref, got, send_sems, recv_sems):
    me = lax.axis_index(axis)
    mine = lax.rem(lax.div(me, stride), n)
    base = me - mine * stride

    def member(j):
        return base + j * stride

    barrier = pltpu.get_barrier_semaphore()
    for k in range(1, n):
        pl.semaphore_signal(
            barrier, inc=1, device_id={axis: member(lax.rem(mine + k, n))}, device_id_type=MESH
        )
    pl.semaphore_wait(barrier, n - 1)
    sends = []
    for k in range(1, n):
        peer = lax.rem(mine + k, n)
        copy = pltpu.make_async_remote_copy(
            src_ref=x_ref if gather else x_ref.at[peer],
            dst_ref=got.at[mine],
            send_sem=send_sems.at[k],
            recv_sem=recv_sems.at[k],
            device_id={axis: member(peer)},
            device_id_type=MESH,
        )
        copy.start()
        sends.append(copy)
    o_ref[mine] = x_ref[...] if gather else x_ref[mine]
    for k in range(1, n):
        sends[k - 1].wait_send()
        source = lax.rem(mine + n - k, n)
        pltpu.make_async_remote_copy(
            src_ref=x_ref if gather else x_ref.at[source],
            dst_ref=got.at[source],
            send_sem=send_sems.at[k],
            recv_sem=recv_sems.at[k],
            device_id={axis: member(source)},
            device_id_type=MESH,
        ).wait_recv()
        o_ref[source] = got[source]


def exchange(x, axis, n, collective_id, gather=False, stride=1):
    shape = (n,) + x.shape if gather else x.shape
    return pl.pallas_call(
        functools.partial(_exchange_kernel, n, stride, axis, gather),
        out_shape=jax.ShapeDtypeStruct(shape, x.dtype),
        in_specs=[pl.BlockSpec(memory_space=pltpu.VMEM)],
        out_specs=pl.BlockSpec(memory_space=pltpu.VMEM),
        scratch_shapes=[
            pltpu.VMEM(shape, x.dtype),
            pltpu.SemaphoreType.DMA((n,)),
            pltpu.SemaphoreType.DMA((n,)),
        ],
        compiler_params=pltpu.CompilerParams(
            collective_id=collective_id,
            has_side_effects=True,
            vmem_limit_bytes=min(3 * x.dtype.itemsize * math.prod(shape) + (8 << 20), 60 << 20),
        ),
    )(x)


def reduce_scatter(x, axis, inner, first_inner, first_id):
    outer = x.shape[0] // inner
    if first_inner:
        blocks = x.reshape((inner, outer) + x.shape[1:])
        phases = [(inner, 1), (outer, inner)]
    else:
        blocks = x.reshape((outer, inner) + x.shape[1:])
        phases = [(outer, inner), (inner, 1)]
    for number, (size, stride) in enumerate(phases):
        if size == 1:
            blocks = blocks[0].astype(jnp.float32)
            continue
        got = exchange(blocks.astype(x.dtype), axis, size, first_id + number, stride=stride)
        blocks = jnp.sum(got.astype(jnp.float32), axis=0)
    return blocks


def _gather_kernel(n_outer, n_inner, parts, axis, x_ref, o_ref, got, send_sems, recv_sems):
    me = lax.axis_index(axis)
    ci = lax.rem(me, n_inner)
    yo = lax.div(me, n_inner)
    rows = x_ref.shape[0] // parts

    def device(c, y):
        return {axis: y * n_inner + c}

    def slot(c, y, p):
        return (c * n_outer + y) * parts + p

    def piece(p):
        return pl.ds(p * rows, rows)

    outer_peers = [lax.rem(yo + k, n_outer) for k in range(1, n_outer)]
    inner_peers = [lax.rem(ci + j, n_inner) for j in range(1, n_inner)]
    barrier = pltpu.get_barrier_semaphore()
    for y in outer_peers:
        pl.semaphore_signal(barrier, inc=1, device_id=device(ci, y), device_id_type=MESH)
    for c in inner_peers:
        pl.semaphore_signal(barrier, inc=1, device_id=device(c, yo), device_id_type=MESH)
    pl.semaphore_wait(barrier, len(outer_peers) + len(inner_peers))

    sends = []

    def send(src, c, y, p, to):
        copy = pltpu.make_async_remote_copy(
            src_ref=src,
            dst_ref=got.at[c, y, piece(p)],
            send_sem=send_sems.at[len(sends)],
            recv_sem=recv_sems.at[slot(c, y, p)],
            device_id=to,
            device_id_type=MESH,
        )
        copy.start()
        sends.append(copy)

    def receive(c, y, p):
        pltpu.make_async_remote_copy(
            src_ref=x_ref.at[piece(p)],
            dst_ref=got.at[c, y, piece(p)],
            send_sem=send_sems.at[0],
            recv_sem=recv_sems.at[slot(c, y, p)],
            device_id=device(c, y),
            device_id_type=MESH,
        ).wait_recv()

    for p in range(parts):
        for y in outer_peers:
            send(x_ref.at[piece(p)], ci, yo, p, device(ci, y))
        for c in inner_peers:
            send(x_ref.at[piece(p)], ci, yo, p, device(c, yo))
    o_ref[ci, yo] = x_ref[...]
    for p in range(parts):
        for k in range(1, n_outer):
            y = lax.rem(yo + n_outer - k, n_outer)
            receive(ci, y, p)
            for c in inner_peers:
                send(got.at[ci, y, piece(p)], ci, y, p, device(c, yo))
            o_ref[ci, y, piece(p)] = got[ci, y, piece(p)]
    for j in range(1, n_inner):
        c = lax.rem(ci + n_inner - j, n_inner)
        for p in range(parts):
            for k in range(n_outer):
                y = lax.rem(yo + k, n_outer)
                receive(c, y, p)
                o_ref[c, y, piece(p)] = got[c, y, piece(p)]
    for copy in sends:
        copy.wait_send()


def all_gather(x, axis, n, inner, collective_id):
    outer = n // inner
    shape = (inner, outer) + x.shape
    parts = next(p for p in (4, 2, 1) if x.shape[0] % (16 * p) == 0)
    got = pl.pallas_call(
        functools.partial(_gather_kernel, outer, inner, parts, axis),
        out_shape=jax.ShapeDtypeStruct(shape, x.dtype),
        in_specs=[pl.BlockSpec(memory_space=pltpu.VMEM)],
        out_specs=pl.BlockSpec(memory_space=pltpu.VMEM),
        scratch_shapes=[
            pltpu.VMEM(shape, x.dtype),
            pltpu.SemaphoreType.DMA((n * parts,)),
            pltpu.SemaphoreType.DMA((n * parts,)),
        ],
        compiler_params=pltpu.CompilerParams(
            collective_id=collective_id,
            has_side_effects=True,
            vmem_limit_bytes=min(3 * x.dtype.itemsize * math.prod(shape) + (8 << 20), 60 << 20),
        ),
    )(x)
    return got.reshape((n * x.shape[0],) + x.shape[1:])


def _reduce_kernel(n_o, s_o, n_i, s_i, chunks, halves, axis, p_ref, o_ref, g1, b_ref, g2, s1, r1, s2, r2):
    me = lax.axis_index(axis)
    zi = lax.rem(lax.div(me, s_i), n_i)
    xo = lax.rem(lax.div(me, s_o), n_o)
    zc = n_i // chunks
    rh = p_ref.shape[2] // halves

    def device(x, z):
        return {axis: me + (x - xo) * s_o + (z - zi) * s_i}

    def half(h):
        return pl.ds(h * rh, rh)

    barrier = pltpu.get_barrier_semaphore()
    for k in range(1, n_o):
        pl.semaphore_signal(
            barrier, inc=1, device_id=device(lax.rem(xo + k, n_o), zi), device_id_type=MESH
        )
    for k in range(1, n_i):
        pl.semaphore_signal(
            barrier, inc=1, device_id=device(xo, lax.rem(zi + k, n_i)), device_id_type=MESH
        )
    pl.semaphore_wait(barrier, n_o + n_i - 2)

    def along_x(k, c, h, to, dst_x):
        blocks = pl.ds(c * zc, zc)
        return pltpu.make_async_remote_copy(
            src_ref=p_ref.at[to, blocks, half(h)],
            dst_ref=g1.at[dst_x, blocks, half(h)],
            send_sem=s1.at[k, c * halves + h],
            recv_sem=r1.at[k, c * halves + h],
            device_id=device(to, zi),
            device_id_type=MESH,
        )

    def along_z(k, z, h):
        return pltpu.make_async_remote_copy(
            src_ref=b_ref.at[z, half(h)],
            dst_ref=g2.at[zi, half(h)],
            send_sem=s2.at[k, h],
            recv_sem=r2.at[k, h],
            device_id=device(xo, z),
            device_id_type=MESH,
        )

    first = []
    for c in range(chunks):
        for h in range(halves):
            for k in range(1, n_o):
                copy = along_x(k, c, h, lax.rem(xo + k, n_o), xo)
                copy.start()
                first.append(copy)
    sources = [lax.rem(xo + n_o - k, n_o) for k in range(1, n_o)]
    for c in range(chunks):
        for h in range(halves):
            for k in range(1, n_o):
                along_x(k, c, h, sources[k - 1], sources[k - 1]).wait_recv()
            for z in range(c * zc, (c + 1) * zc):
                total = p_ref[xo, z, half(h)].astype(jnp.float32)
                for src in sources:
                    total = total + g1[src, z, half(h)].astype(jnp.float32)
                b_ref[z, half(h)] = total.astype(b_ref.dtype)
                offset = lax.rem(z - zi + n_i, n_i)

                @pl.when(offset == 0)
                def _():
                    o_ref[half(h)] = total

                @pl.when(offset != 0)
                def _():
                    along_z(offset, z, h).start()

    for k in range(1, n_i):
        src = lax.rem(zi + n_i - k, n_i)
        for h in range(halves):
            pltpu.make_async_remote_copy(
                src_ref=b_ref.at[src, half(h)],
                dst_ref=g2.at[src, half(h)],
                send_sem=s2.at[k, h],
                recv_sem=r2.at[k, h],
                device_id=device(xo, src),
                device_id_type=MESH,
            ).wait_recv()
            o_ref[half(h)] = o_ref[half(h)] + g2[src, half(h)].astype(jnp.float32)
    for copy in first:
        copy.wait_send()
    for z in range(n_i):
        offset = lax.rem(z - zi + n_i, n_i)
        for h in range(halves):

            @pl.when(offset != 0)
            def _():
                along_z(offset, z, h).wait_send()


def reduce_scatter_2d(x, axis, first, second, collective_id):
    (n_o, s_o), (n_i, s_i) = first, second
    chunks = next(c for c in (8, 4, 2, 1) if n_i % c == 0)
    halves = next(p for p in (3, 2, 1) if x.shape[2] % (16 * p) == 0)
    return pl.pallas_call(
        functools.partial(_reduce_kernel, n_o, s_o, n_i, s_i, chunks, halves, axis),
        out_shape=jax.ShapeDtypeStruct(x.shape[2:], jnp.float32),
        in_specs=[pl.BlockSpec(memory_space=pltpu.VMEM)],
        out_specs=pl.BlockSpec(memory_space=pltpu.VMEM),
        scratch_shapes=[
            pltpu.VMEM(x.shape, x.dtype),
            pltpu.VMEM(x.shape[1:], x.dtype),
            pltpu.VMEM(x.shape[1:], x.dtype),
            pltpu.SemaphoreType.DMA((n_o, chunks * halves)),
            pltpu.SemaphoreType.DMA((n_o, chunks * halves)),
            pltpu.SemaphoreType.DMA((n_i, halves)),
            pltpu.SemaphoreType.DMA((n_i, halves)),
        ],
        compiler_params=pltpu.CompilerParams(
            collective_id=collective_id,
            has_side_effects=True,
            vmem_limit_bytes=min(4 * x.dtype.itemsize * x.size + (8 << 20), 60 << 20),
        ),
    )(x)


def inner_size(devices):
    coords = [tuple(getattr(d, "coords", ())) for d in devices]
    if len(coords) < 2 or not coords[0]:
        return len(coords)
    varying = [c for c in range(len(coords[0])) if len({p[c] for p in coords}) > 1]
    slow = [c for c in varying if coords[1][c] == coords[0][c]]
    if not slow:
        return 1
    run = 0
    while run < len(coords) and coords[run][slow[0]] == coords[0][slow[0]]:
        run += 1
    return run


def per_device(n_sub, mass_inner, sub_inner, spectra, w_in, w_out, partner_rows, pair_counts, pair_labels):
    own_rows = spectra.shape[0]
    peers = partner_rows.shape[2]
    slots = partner_rows.shape[3]
    shard_rows = all_gather(spectra, "sub", n_sub, sub_inner, 2)
    pre = jnp.dot(shard_rows, w_in, preferred_element_type=jnp.float32)
    hidden = jax.nn.silu(pre).astype(jnp.bfloat16)
    embed_part = jnp.dot(hidden, w_out, preferred_element_type=jnp.float32)
    sub_outer = n_sub // sub_inner
    embed = reduce_scatter_2d(
        embed_part.reshape(sub_inner, sub_outer, own_rows, embed_part.shape[1]),
        "sub",
        (sub_inner, 1),
        (sub_outer, sub_inner),
        4,
    )
    norm = jnp.sqrt(jnp.sum(embed * embed, axis=-1, keepdims=True) + 1e-06)
    unit = embed / norm
    unit_b = unit.astype(jnp.bfloat16)
    flat_rows = partner_rows.reshape(peers * slots)
    selector = flat_rows[:, None] == jnp.arange(own_rows, dtype=jnp.int32)[None, :]
    mine = jnp.dot(
        selector.astype(jnp.bfloat16), unit_b, preferred_element_type=jnp.float32
    ).astype(jnp.bfloat16)
    outgoing = mine.reshape(peers, slots, mine.shape[1])
    incoming = exchange(outgoing, "mass", peers, 1)
    theirs = incoming.astype(jnp.float32)
    sim = jnp.sum(outgoing.astype(jnp.float32) * theirs, axis=-1)
    valid = jnp.arange(slots, dtype=jnp.int32)[None, :] < pair_counts.reshape(peers)[:, None]
    labels = pair_labels.reshape(peers, slots).astype(jnp.float32)
    coef = jnp.where(valid, 2.0 * (sim - labels), jnp.float32(0.0))
    weighted = (coef[..., None] * theirs).reshape(peers * slots, theirs.shape[2])
    grad_unit = lax.dot_general(
        selector.astype(jnp.float32),
        weighted,
        (((0,), (0,)), ((), ())),
        precision=lax.Precision.HIGHEST,
    )
    along = jnp.sum(unit * grad_unit, axis=-1, keepdims=True)
    grad_embed = ((grad_unit - unit * along) / norm).astype(jnp.bfloat16)
    grad_rows = all_gather(grad_embed, "sub", n_sub, sub_inner, 6)
    back = lax.dot_general(
        grad_rows, w_out, (((1,), (1,)), ((), ())), preferred_element_type=jnp.float32
    )
    gate = jax.nn.sigmoid(pre)
    grad_pre = lax.optimization_barrier(
        (back * gate * (1.0 + pre * (1.0 - gate))).astype(jnp.bfloat16)
    )
    out_part = lax.dot_general(
        grad_rows, hidden, (((0,), (0,)), ((), ())), preferred_element_type=jnp.float32
    )
    in_part_t = lax.dot_general(
        grad_pre, shard_rows, (((0,), (0,)), ((), ())), preferred_element_type=jnp.float32
    )
    n_mass = peers
    hid = in_part_t.shape[0]
    in_cols = in_part_t.shape[1] // n_mass
    out_rows = out_part.shape[0] // n_mass
    lanes = in_cols
    partial = jnp.concatenate(
        [
            jnp.swapaxes(in_part_t.astype(jnp.bfloat16).reshape(hid, n_mass, in_cols), 0, 1),
            out_part.astype(jnp.bfloat16).reshape(n_mass, out_rows * hid // lanes, lanes),
        ],
        axis=1,
    )
    mass_outer = n_mass // mass_inner
    summed = reduce_scatter_2d(
        partial.reshape((mass_outer, mass_inner) + partial.shape[1:]),
        "mass",
        (mass_outer, mass_inner),
        (mass_inner, 1),
        8,
    )
    grad_in = summed[:hid].T
    grad_out_t = summed[hid:].reshape(out_rows, hid)
    return (grad_in, grad_out_t)


def solution(mesh):
    placed = (
        P(("mass", "sub"), None),
        P(None, "sub"),
        P("sub", None),
        P("mass", "sub", None, None),
        P("mass", "sub", None),
        P("mass", "sub", None, None),
    )
    mass_inner = inner_size(list(mesh.devices[:, 0]))
    sub_inner = inner_size(list(mesh.devices[0, :]))
    return jax.shard_map(
        functools.partial(per_device, mesh.shape["sub"], mass_inner, sub_inner),
        mesh=mesh,
        in_specs=placed,
        out_specs=(P("mass", "sub"), P("mass", "sub")),
        check_vma=False,
    )
```

```python
import functools
import math

import jax
import jax.numpy as jnp
from jax import lax
from jax.experimental import pallas as pl
from jax.experimental.pallas import tpu as pltpu
from jax.sharding import PartitionSpec as P

MESH = pl.DeviceIdType.MESH


def _exchange_kernel(n, stride, axis, gather, x_ref, o_ref, got, send_sems, recv_sems):
    me = lax.axis_index(axis)
    mine = lax.rem(lax.div(me, stride), n)
    base = me - mine * stride

    def member(j):
        return base + j * stride

    barrier = pltpu.get_barrier_semaphore()
    for k in range(1, n):
        pl.semaphore_signal(
            barrier, inc=1, device_id={axis: member(lax.rem(mine + k, n))}, device_id_type=MESH
        )
    pl.semaphore_wait(barrier, n - 1)
    sends = []
    for k in range(1, n):
        peer = lax.rem(mine + k, n)
        copy = pltpu.make_async_remote_copy(
            src_ref=x_ref if gather else x_ref.at[peer],
            dst_ref=got.at[mine],
            send_sem=send_sems.at[k],
            recv_sem=recv_sems.at[k],
            device_id={axis: member(peer)},
            device_id_type=MESH,
        )
        copy.start()
        sends.append(copy)
    o_ref[mine] = x_ref[...] if gather else x_ref[mine]
    for k in range(1, n):
        sends[k - 1].wait_send()
        source = lax.rem(mine + n - k, n)
        pltpu.make_async_remote_copy(
            src_ref=x_ref if gather else x_ref.at[source],
            dst_ref=got.at[source],
            send_sem=send_sems.at[k],
            recv_sem=recv_sems.at[k],
            device_id={axis: member(source)},
            device_id_type=MESH,
        ).wait_recv()
        o_ref[source] = got[source]


def exchange(x, axis, n, collective_id, gather=False, stride=1):
    shape = (n,) + x.shape if gather else x.shape
    return pl.pallas_call(
        functools.partial(_exchange_kernel, n, stride, axis, gather),
        out_shape=jax.ShapeDtypeStruct(shape, x.dtype),
        in_specs=[pl.BlockSpec(memory_space=pltpu.VMEM)],
        out_specs=pl.BlockSpec(memory_space=pltpu.VMEM),
        scratch_shapes=[
            pltpu.VMEM(shape, x.dtype),
            pltpu.SemaphoreType.DMA((n,)),
            pltpu.SemaphoreType.DMA((n,)),
        ],
        compiler_params=pltpu.CompilerParams(
            collective_id=collective_id,
            has_side_effects=True,
            vmem_limit_bytes=min(3 * x.dtype.itemsize * math.prod(shape) + (8 << 20), 60 << 20),
        ),
    )(x)


def reduce_scatter(x, axis, inner, first_inner, first_id):
    outer = x.shape[0] // inner
    if first_inner:
        blocks = x.reshape((inner, outer) + x.shape[1:])
        phases = [(inner, 1), (outer, inner)]
    else:
        blocks = x.reshape((outer, inner) + x.shape[1:])
        phases = [(outer, inner), (inner, 1)]
    for number, (size, stride) in enumerate(phases):
        if size == 1:
            blocks = blocks[0].astype(jnp.float32)
            continue
        got = exchange(blocks.astype(x.dtype), axis, size, first_id + number, stride=stride)
        blocks = jnp.sum(got.astype(jnp.float32), axis=0)
    return blocks


def _gather_kernel(n_outer, n_inner, parts, axis, x_ref, o_ref, got, send_sems, recv_sems):
    me = lax.axis_index(axis)
    ci = lax.rem(me, n_inner)
    yo = lax.div(me, n_inner)
    rows = x_ref.shape[0] // parts

    def device(c, y):
        return {axis: y * n_inner + c}

    def slot(c, y, p):
        return (c * n_outer + y) * parts + p

    def piece(p):
        return pl.ds(p * rows, rows)

    outer_peers = [lax.rem(yo + k, n_outer) for k in range(1, n_outer)]
    inner_peers = [lax.rem(ci + j, n_inner) for j in range(1, n_inner)]
    barrier = pltpu.get_barrier_semaphore()
    for y in outer_peers:
        pl.semaphore_signal(barrier, inc=1, device_id=device(ci, y), device_id_type=MESH)
    for c in inner_peers:
        pl.semaphore_signal(barrier, inc=1, device_id=device(c, yo), device_id_type=MESH)
    pl.semaphore_wait(barrier, len(outer_peers) + len(inner_peers))

    sends = []

    def send(src, c, y, p, to):
        copy = pltpu.make_async_remote_copy(
            src_ref=src,
            dst_ref=got.at[c, y, piece(p)],
            send_sem=send_sems.at[len(sends)],
            recv_sem=recv_sems.at[slot(c, y, p)],
            device_id=to,
            device_id_type=MESH,
        )
        copy.start()
        sends.append(copy)

    def receive(c, y, p):
        pltpu.make_async_remote_copy(
            src_ref=x_ref.at[piece(p)],
            dst_ref=got.at[c, y, piece(p)],
            send_sem=send_sems.at[0],
            recv_sem=recv_sems.at[slot(c, y, p)],
            device_id=device(c, y),
            device_id_type=MESH,
        ).wait_recv()

    for p in range(parts):
        for y in outer_peers:
            send(x_ref.at[piece(p)], ci, yo, p, device(ci, y))
        for c in inner_peers:
            send(x_ref.at[piece(p)], ci, yo, p, device(c, yo))
    o_ref[ci, yo] = x_ref[...]
    for p in range(parts):
        for k in range(1, n_outer):
            y = lax.rem(yo + n_outer - k, n_outer)
            receive(ci, y, p)
            for c in inner_peers:
                send(got.at[ci, y, piece(p)], ci, y, p, device(c, yo))
            o_ref[ci, y, piece(p)] = got[ci, y, piece(p)]
    for j in range(1, n_inner):
        c = lax.rem(ci + n_inner - j, n_inner)
        for p in range(parts):
            for k in range(n_outer):
                y = lax.rem(yo + k, n_outer)
                receive(c, y, p)
                o_ref[c, y, piece(p)] = got[c, y, piece(p)]
    for copy in sends:
        copy.wait_send()


def all_gather(x, axis, n, inner, collective_id):
    outer = n // inner
    shape = (inner, outer) + x.shape
    parts = next(p for p in (4, 2, 1) if x.shape[0] % (16 * p) == 0)
    got = pl.pallas_call(
        functools.partial(_gather_kernel, outer, inner, parts, axis),
        out_shape=jax.ShapeDtypeStruct(shape, x.dtype),
        in_specs=[pl.BlockSpec(memory_space=pltpu.VMEM)],
        out_specs=pl.BlockSpec(memory_space=pltpu.VMEM),
        scratch_shapes=[
            pltpu.VMEM(shape, x.dtype),
            pltpu.SemaphoreType.DMA((n * parts,)),
            pltpu.SemaphoreType.DMA((n * parts,)),
        ],
        compiler_params=pltpu.CompilerParams(
            collective_id=collective_id,
            has_side_effects=True,
            vmem_limit_bytes=min(3 * x.dtype.itemsize * math.prod(shape) + (8 << 20), 60 << 20),
        ),
    )(x)
    return got.reshape((n * x.shape[0],) + x.shape[1:])


def _reduce_kernel(n_o, s_o, n_i, s_i, chunks, halves, axis, p_ref, o_ref, g1, b_ref, g2, s1, r1, s2, r2):
    me = lax.axis_index(axis)
    zi = lax.rem(lax.div(me, s_i), n_i)
    xo = lax.rem(lax.div(me, s_o), n_o)
    zc = n_i // chunks
    rh = p_ref.shape[2] // halves

    def device(x, z):
        return {axis: me + (x - xo) * s_o + (z - zi) * s_i}

    def half(h):
        return pl.ds(h * rh, rh)

    barrier = pltpu.get_barrier_semaphore()
    for k in range(1, n_o):
        pl.semaphore_signal(
            barrier, inc=1, device_id=device(lax.rem(xo + k, n_o), zi), device_id_type=MESH
        )
    for k in range(1, n_i):
        pl.semaphore_signal(
            barrier, inc=1, device_id=device(xo, lax.rem(zi + k, n_i)), device_id_type=MESH
        )
    pl.semaphore_wait(barrier, n_o + n_i - 2)

    def along_x(k, c, h, to, dst_x):
        blocks = pl.ds(c * zc, zc)
        return pltpu.make_async_remote_copy(
            src_ref=p_ref.at[to, blocks, half(h)],
            dst_ref=g1.at[dst_x, blocks, half(h)],
            send_sem=s1.at[k, c * halves + h],
            recv_sem=r1.at[k, c * halves + h],
            device_id=device(to, zi),
            device_id_type=MESH,
        )

    def along_z(k, z, h):
        return pltpu.make_async_remote_copy(
            src_ref=b_ref.at[z, half(h)],
            dst_ref=g2.at[zi, half(h)],
            send_sem=s2.at[k, h],
            recv_sem=r2.at[k, h],
            device_id=device(xo, z),
            device_id_type=MESH,
        )

    first = []
    for c in range(chunks):
        for h in range(halves):
            for k in range(1, n_o):
                copy = along_x(k, c, h, lax.rem(xo + k, n_o), xo)
                copy.start()
                first.append(copy)
    sources = [lax.rem(xo + n_o - k, n_o) for k in range(1, n_o)]
    for c in range(chunks):
        for h in range(halves):
            for k in range(1, n_o):
                along_x(k, c, h, sources[k - 1], sources[k - 1]).wait_recv()
            for z in range(c * zc, (c + 1) * zc):
                total = p_ref[xo, z, half(h)].astype(jnp.float32)
                for src in sources:
                    total = total + g1[src, z, half(h)].astype(jnp.float32)
                b_ref[z, half(h)] = total.astype(b_ref.dtype)
                offset = lax.rem(z - zi + n_i, n_i)

                @pl.when(offset == 0)
                def _():
                    o_ref[half(h)] = total

                @pl.when(offset != 0)
                def _():
                    along_z(offset, z, h).start()

    for k in range(1, n_i):
        src = lax.rem(zi + n_i - k, n_i)
        for h in range(halves):
            pltpu.make_async_remote_copy(
                src_ref=b_ref.at[src, half(h)],
                dst_ref=g2.at[src, half(h)],
                send_sem=s2.at[k, h],
                recv_sem=r2.at[k, h],
                device_id=device(xo, src),
                device_id_type=MESH,
            ).wait_recv()
            o_ref[half(h)] = o_ref[half(h)] + g2[src, half(h)].astype(jnp.float32)
    for copy in first:
        copy.wait_send()
    for z in range(n_i):
        offset = lax.rem(z - zi + n_i, n_i)
        for h in range(halves):

            @pl.when(offset != 0)
            def _():
                along_z(offset, z, h).wait_send()


def reduce_scatter_2d(x, axis, first, second, collective_id):
    (n_o, s_o), (n_i, s_i) = first, second
    chunks = next(c for c in (8, 4, 2, 1) if n_i % c == 0)
    halves = next(p for p in (4, 2, 1) if x.shape[2] % (16 * p) == 0)
    return pl.pallas_call(
        functools.partial(_reduce_kernel, n_o, s_o, n_i, s_i, chunks, halves, axis),
        out_shape=jax.ShapeDtypeStruct(x.shape[2:], jnp.float32),
        in_specs=[pl.BlockSpec(memory_space=pltpu.VMEM)],
        out_specs=pl.BlockSpec(memory_space=pltpu.VMEM),
        scratch_shapes=[
            pltpu.VMEM(x.shape, x.dtype),
            pltpu.VMEM(x.shape[1:], x.dtype),
            pltpu.VMEM(x.shape[1:], x.dtype),
            pltpu.SemaphoreType.DMA((n_o, chunks * halves)),
            pltpu.SemaphoreType.DMA((n_o, chunks * halves)),
            pltpu.SemaphoreType.DMA((n_i, halves)),
            pltpu.SemaphoreType.DMA((n_i, halves)),
        ],
        compiler_params=pltpu.CompilerParams(
            collective_id=collective_id,
            has_side_effects=True,
            vmem_limit_bytes=min(4 * x.dtype.itemsize * x.size + (8 << 20), 60 << 20),
        ),
    )(x)


def inner_size(devices):
    coords = [tuple(getattr(d, "coords", ())) for d in devices]
    if len(coords) < 2 or not coords[0]:
        return len(coords)
    varying = [c for c in range(len(coords[0])) if len({p[c] for p in coords}) > 1]
    slow = [c for c in varying if coords[1][c] == coords[0][c]]
    if not slow:
        return 1
    run = 0
    while run < len(coords) and coords[run][slow[0]] == coords[0][slow[0]]:
        run += 1
    return run


def per_device(n_sub, mass_inner, sub_inner, spectra, w_in, w_out, partner_rows, pair_counts, pair_labels):
    own_rows = spectra.shape[0]
    peers = partner_rows.shape[2]
    slots = partner_rows.shape[3]
    shard_rows = all_gather(spectra, "sub", n_sub, sub_inner, 2)
    pre = jnp.dot(shard_rows, w_in, preferred_element_type=jnp.float32)
    hidden = jax.nn.silu(pre).astype(jnp.bfloat16)
    embed_part = jnp.dot(hidden, w_out, preferred_element_type=jnp.float32)
    sub_outer = n_sub // sub_inner
    embed = reduce_scatter_2d(
        embed_part.reshape(sub_inner, sub_outer, own_rows, embed_part.shape[1]),
        "sub",
        (sub_inner, 1),
        (sub_outer, sub_inner),
        4,
    )
    norm = jnp.sqrt(jnp.sum(embed * embed, axis=-1, keepdims=True) + 1e-06)
    unit = embed / norm
    unit_b = unit.astype(jnp.bfloat16)
    flat_rows = partner_rows.reshape(peers * slots)
    selector = flat_rows[:, None] == jnp.arange(own_rows, dtype=jnp.int32)[None, :]
    mine = jnp.dot(
        selector.astype(jnp.bfloat16), unit_b, preferred_element_type=jnp.float32
    ).astype(jnp.bfloat16)
    outgoing = mine.reshape(peers, slots, mine.shape[1])
    incoming = exchange(outgoing, "mass", peers, 1)
    theirs = incoming.astype(jnp.float32)
    sim = jnp.sum(outgoing.astype(jnp.float32) * theirs, axis=-1)
    valid = jnp.arange(slots, dtype=jnp.int32)[None, :] < pair_counts.reshape(peers)[:, None]
    labels = pair_labels.reshape(peers, slots).astype(jnp.float32)
    coef = jnp.where(valid, 2.0 * (sim - labels), jnp.float32(0.0))
    weighted = (coef[..., None] * theirs).reshape(peers * slots, theirs.shape[2])
    grad_unit = lax.dot_general(
        selector.astype(jnp.float32),
        weighted,
        (((0,), (0,)), ((), ())),
        precision=lax.Precision.HIGHEST,
    )
    along = jnp.sum(unit * grad_unit, axis=-1, keepdims=True)
    grad_embed = ((grad_unit - unit * along) / norm).astype(jnp.bfloat16)
    grad_rows = all_gather(grad_embed, "sub", n_sub, sub_inner, 6)
    back = lax.dot_general(
        grad_rows, w_out, (((1,), (1,)), ((), ())), preferred_element_type=jnp.float32
    )
    gate = jax.nn.sigmoid(pre)
    grad_pre = lax.optimization_barrier(
        (back * gate * (1.0 + pre * (1.0 - gate))).astype(jnp.bfloat16)
    )
    out_part = lax.dot_general(
        grad_rows, hidden, (((0,), (0,)), ((), ())), preferred_element_type=jnp.float32
    )
    in_part_t = lax.dot_general(
        grad_pre, shard_rows, (((0,), (0,)), ((), ())), preferred_element_type=jnp.float32
    )
    n_mass = peers
    hid = in_part_t.shape[0]
    in_cols = in_part_t.shape[1] // n_mass
    out_rows = out_part.shape[0] // n_mass
    lanes = in_cols
    partial = jnp.concatenate(
        [
            jnp.swapaxes(in_part_t.astype(jnp.bfloat16).reshape(hid, n_mass, in_cols), 0, 1),
            out_part.astype(jnp.bfloat16).reshape(n_mass, out_rows * hid // lanes, lanes),
        ],
        axis=1,
    )
    mass_outer = n_mass // mass_inner
    summed = reduce_scatter_2d(
        partial.reshape((mass_outer, mass_inner) + partial.shape[1:]),
        "mass",
        (mass_outer, mass_inner),
        (mass_inner, 1),
        8,
    )
    grad_in = summed[:hid].T
    grad_out_t = summed[hid:].reshape(out_rows, hid)
    return (grad_in, grad_out_t)


def solution(mesh):
    placed = (
        P(("mass", "sub"), None),
        P(None, "sub"),
        P("sub", None),
        P("mass", "sub", None, None),
        P("mass", "sub", None),
        P("mass", "sub", None, None),
    )
    mass_inner = inner_size(list(mesh.devices[:, 0]))
    sub_inner = inner_size(list(mesh.devices[0, :]))
    return jax.shard_map(
        functools.partial(per_device, mesh.shape["sub"], mass_inner, sub_inner),
        mesh=mesh,
        in_specs=placed,
        out_specs=(P("mass", "sub"), P("mass", "sub")),
        check_vma=False,
    )
```

```python
import functools
import math

import jax
import jax.numpy as jnp
from jax import lax
from jax.experimental import pallas as pl
from jax.experimental.pallas import tpu as pltpu
from jax.sharding import PartitionSpec as P

MESH = pl.DeviceIdType.MESH


def _exchange_kernel(n, stride, axis, gather, x_ref, o_ref, got, send_sems, recv_sems):
    me = lax.axis_index(axis)
    mine = lax.rem(lax.div(me, stride), n)
    base = me - mine * stride

    def member(j):
        return base + j * stride

    barrier = pltpu.get_barrier_semaphore()
    for k in range(1, n):
        pl.semaphore_signal(
            barrier, inc=1, device_id={axis: member(lax.rem(mine + k, n))}, device_id_type=MESH
        )
    pl.semaphore_wait(barrier, n - 1)
    sends = []
    for k in range(1, n):
        peer = lax.rem(mine + k, n)
        copy = pltpu.make_async_remote_copy(
            src_ref=x_ref if gather else x_ref.at[peer],
            dst_ref=got.at[mine],
            send_sem=send_sems.at[k],
            recv_sem=recv_sems.at[k],
            device_id={axis: member(peer)},
            device_id_type=MESH,
        )
        copy.start()
        sends.append(copy)
    o_ref[mine] = x_ref[...] if gather else x_ref[mine]
    for k in range(1, n):
        sends[k - 1].wait_send()
        source = lax.rem(mine + n - k, n)
        pltpu.make_async_remote_copy(
            src_ref=x_ref if gather else x_ref.at[source],
            dst_ref=got.at[source],
            send_sem=send_sems.at[k],
            recv_sem=recv_sems.at[k],
            device_id={axis: member(source)},
            device_id_type=MESH,
        ).wait_recv()
        o_ref[source] = got[source]


def exchange(x, axis, n, collective_id, gather=False, stride=1):
    shape = (n,) + x.shape if gather else x.shape
    return pl.pallas_call(
        functools.partial(_exchange_kernel, n, stride, axis, gather),
        out_shape=jax.ShapeDtypeStruct(shape, x.dtype),
        in_specs=[pl.BlockSpec(memory_space=pltpu.VMEM)],
        out_specs=pl.BlockSpec(memory_space=pltpu.VMEM),
        scratch_shapes=[
            pltpu.VMEM(shape, x.dtype),
            pltpu.SemaphoreType.DMA((n,)),
            pltpu.SemaphoreType.DMA((n,)),
        ],
        compiler_params=pltpu.CompilerParams(
            collective_id=collective_id,
            has_side_effects=True,
            vmem_limit_bytes=min(3 * x.dtype.itemsize * math.prod(shape) + (8 << 20), 60 << 20),
        ),
    )(x)


def reduce_scatter(x, axis, inner, first_inner, first_id):
    outer = x.shape[0] // inner
    if first_inner:
        blocks = x.reshape((inner, outer) + x.shape[1:])
        phases = [(inner, 1), (outer, inner)]
    else:
        blocks = x.reshape((outer, inner) + x.shape[1:])
        phases = [(outer, inner), (inner, 1)]
    for number, (size, stride) in enumerate(phases):
        if size == 1:
            blocks = blocks[0].astype(jnp.float32)
            continue
        got = exchange(blocks.astype(x.dtype), axis, size, first_id + number, stride=stride)
        blocks = jnp.sum(got.astype(jnp.float32), axis=0)
    return blocks


def _gather_kernel(n_outer, n_inner, parts, axis, x_ref, o_ref, got, send_sems, recv_sems):
    me = lax.axis_index(axis)
    ci = lax.rem(me, n_inner)
    yo = lax.div(me, n_inner)
    rows = x_ref.shape[0] // parts

    def device(c, y):
        return {axis: y * n_inner + c}

    def slot(c, y, p):
        return (c * n_outer + y) * parts + p

    def piece(p):
        return pl.ds(p * rows, rows)

    outer_peers = [lax.rem(yo + k, n_outer) for k in range(1, n_outer)]
    inner_peers = [lax.rem(ci + j, n_inner) for j in range(1, n_inner)]
    barrier = pltpu.get_barrier_semaphore()
    for y in outer_peers:
        pl.semaphore_signal(barrier, inc=1, device_id=device(ci, y), device_id_type=MESH)
    for c in inner_peers:
        pl.semaphore_signal(barrier, inc=1, device_id=device(c, yo), device_id_type=MESH)
    pl.semaphore_wait(barrier, len(outer_peers) + len(inner_peers))

    sends = []

    def send(src, c, y, p, to):
        copy = pltpu.make_async_remote_copy(
            src_ref=src,
            dst_ref=got.at[c, y, piece(p)],
            send_sem=send_sems.at[len(sends)],
            recv_sem=recv_sems.at[slot(c, y, p)],
            device_id=to,
            device_id_type=MESH,
        )
        copy.start()
        sends.append(copy)

    def receive(c, y, p):
        pltpu.make_async_remote_copy(
            src_ref=x_ref.at[piece(p)],
            dst_ref=got.at[c, y, piece(p)],
            send_sem=send_sems.at[0],
            recv_sem=recv_sems.at[slot(c, y, p)],
            device_id=device(c, y),
            device_id_type=MESH,
        ).wait_recv()

    for p in range(parts):
        for y in outer_peers:
            send(x_ref.at[piece(p)], ci, yo, p, device(ci, y))
        for c in inner_peers:
            send(x_ref.at[piece(p)], ci, yo, p, device(c, yo))
    o_ref[ci, yo] = x_ref[...]
    for p in range(parts):
        for k in range(1, n_outer):
            y = lax.rem(yo + n_outer - k, n_outer)
            receive(ci, y, p)
            for c in inner_peers:
                send(got.at[ci, y, piece(p)], ci, y, p, device(c, yo))
            o_ref[ci, y, piece(p)] = got[ci, y, piece(p)]
    for j in range(1, n_inner):
        c = lax.rem(ci + n_inner - j, n_inner)
        for p in range(parts):
            for k in range(n_outer):
                y = lax.rem(yo + k, n_outer)
                receive(c, y, p)
                o_ref[c, y, piece(p)] = got[c, y, piece(p)]
    for copy in sends:
        copy.wait_send()


def all_gather(x, axis, n, inner, collective_id):
    outer = n // inner
    shape = (inner, outer) + x.shape
    parts = next(p for p in (4, 2, 1) if x.shape[0] % (16 * p) == 0)
    got = pl.pallas_call(
        functools.partial(_gather_kernel, outer, inner, parts, axis),
        out_shape=jax.ShapeDtypeStruct(shape, x.dtype),
        in_specs=[pl.BlockSpec(memory_space=pltpu.VMEM)],
        out_specs=pl.BlockSpec(memory_space=pltpu.VMEM),
        scratch_shapes=[
            pltpu.VMEM(shape, x.dtype),
            pltpu.SemaphoreType.DMA((n * parts,)),
            pltpu.SemaphoreType.DMA((n * parts,)),
        ],
        compiler_params=pltpu.CompilerParams(
            collective_id=collective_id,
            has_side_effects=True,
            vmem_limit_bytes=min(3 * x.dtype.itemsize * math.prod(shape) + (8 << 20), 60 << 20),
        ),
    )(x)
    return got.reshape((n * x.shape[0],) + x.shape[1:])


def _reduce_kernel(n_o, s_o, n_i, s_i, chunks, halves, axis, p_ref, o_ref, g1, b_ref, g2, s1, r1, s2, r2):
    me = lax.axis_index(axis)
    zi = lax.rem(lax.div(me, s_i), n_i)
    xo = lax.rem(lax.div(me, s_o), n_o)
    zc = n_i // chunks
    rh = p_ref.shape[2] // halves

    def device(x, z):
        return {axis: me + (x - xo) * s_o + (z - zi) * s_i}

    def half(h):
        return pl.ds(h * rh, rh)

    barrier = pltpu.get_barrier_semaphore()
    for k in range(1, n_o):
        pl.semaphore_signal(
            barrier, inc=1, device_id=device(lax.rem(xo + k, n_o), zi), device_id_type=MESH
        )
    for k in range(1, n_i):
        pl.semaphore_signal(
            barrier, inc=1, device_id=device(xo, lax.rem(zi + k, n_i)), device_id_type=MESH
        )
    pl.semaphore_wait(barrier, n_o + n_i - 2)

    def along_x(k, c, h, to, dst_x):
        blocks = pl.ds(c * zc, zc)
        return pltpu.make_async_remote_copy(
            src_ref=p_ref.at[to, blocks, half(h)],
            dst_ref=g1.at[dst_x, blocks, half(h)],
            send_sem=s1.at[k, c * halves + h],
            recv_sem=r1.at[k, c * halves + h],
            device_id=device(to, zi),
            device_id_type=MESH,
        )

    def along_z(k, z, h):
        return pltpu.make_async_remote_copy(
            src_ref=b_ref.at[z, half(h)],
            dst_ref=g2.at[zi, half(h)],
            send_sem=s2.at[k, h],
            recv_sem=r2.at[k, h],
            device_id=device(xo, z),
            device_id_type=MESH,
        )

    first = []
    for c in range(chunks):
        for h in range(halves):
            for k in range(1, n_o):
                copy = along_x(k, c, h, lax.rem(xo + k, n_o), xo)
                copy.start()
                first.append(copy)
    sources = [lax.rem(xo + n_o - k, n_o) for k in range(1, n_o)]
    for c in range(chunks):
        for h in range(halves):
            for k in range(1, n_o):
                along_x(k, c, h, sources[k - 1], sources[k - 1]).wait_recv()
            for z in range(c * zc, (c + 1) * zc):
                total = p_ref[xo, z, half(h)].astype(jnp.float32)
                for src in sources:
                    total = total + g1[src, z, half(h)].astype(jnp.float32)
                b_ref[z, half(h)] = total.astype(b_ref.dtype)
                offset = lax.rem(z - zi + n_i, n_i)

                @pl.when(offset == 0)
                def _():
                    o_ref[half(h)] = total

                @pl.when(offset != 0)
                def _():
                    along_z(offset, z, h).start()

    for k in range(1, n_i):
        src = lax.rem(zi + n_i - k, n_i)
        for h in range(halves):
            pltpu.make_async_remote_copy(
                src_ref=b_ref.at[src, half(h)],
                dst_ref=g2.at[src, half(h)],
                send_sem=s2.at[k, h],
                recv_sem=r2.at[k, h],
                device_id=device(xo, src),
                device_id_type=MESH,
            ).wait_recv()
            o_ref[half(h)] = o_ref[half(h)] + g2[src, half(h)].astype(jnp.float32)
    for copy in first:
        copy.wait_send()
    for z in range(n_i):
        offset = lax.rem(z - zi + n_i, n_i)
        for h in range(halves):

            @pl.when(offset != 0)
            def _():
                along_z(offset, z, h).wait_send()


def reduce_scatter_2d(x, axis, first, second, collective_id):
    (n_o, s_o), (n_i, s_i) = first, second
    chunks = next(c for c in (8, 4, 2, 1) if n_i % c == 0)
    halves = 2 if x.shape[2] % 32 == 0 and x.shape[2] >= 256 else 1
    return pl.pallas_call(
        functools.partial(_reduce_kernel, n_o, s_o, n_i, s_i, chunks, halves, axis),
        out_shape=jax.ShapeDtypeStruct(x.shape[2:], jnp.float32),
        in_specs=[pl.BlockSpec(memory_space=pltpu.VMEM)],
        out_specs=pl.BlockSpec(memory_space=pltpu.VMEM),
        scratch_shapes=[
            pltpu.VMEM(x.shape, x.dtype),
            pltpu.VMEM(x.shape[1:], x.dtype),
            pltpu.VMEM(x.shape[1:], x.dtype),
            pltpu.SemaphoreType.DMA((n_o, chunks * halves)),
            pltpu.SemaphoreType.DMA((n_o, chunks * halves)),
            pltpu.SemaphoreType.DMA((n_i, halves)),
            pltpu.SemaphoreType.DMA((n_i, halves)),
        ],
        compiler_params=pltpu.CompilerParams(
            collective_id=collective_id,
            has_side_effects=True,
            vmem_limit_bytes=min(4 * x.dtype.itemsize * x.size + (8 << 20), 60 << 20),
        ),
    )(x)


def inner_size(devices):
    coords = [tuple(getattr(d, "coords", ())) for d in devices]
    if len(coords) < 2 or not coords[0]:
        return len(coords)
    varying = [c for c in range(len(coords[0])) if len({p[c] for p in coords}) > 1]
    slow = [c for c in varying if coords[1][c] == coords[0][c]]
    if not slow:
        return 1
    run = 0
    while run < len(coords) and coords[run][slow[0]] == coords[0][slow[0]]:
        run += 1
    return run


def per_device(n_sub, mass_inner, sub_inner, spectra, w_in, w_out, partner_rows, pair_counts, pair_labels):
    own_rows = spectra.shape[0]
    peers = partner_rows.shape[2]
    slots = partner_rows.shape[3]
    shard_rows = all_gather(spectra, "sub", n_sub, sub_inner, 2)
    pre = jnp.dot(shard_rows, w_in, preferred_element_type=jnp.float32)
    hidden = jax.nn.silu(pre).astype(jnp.bfloat16)
    embed_part = jnp.dot(hidden, w_out, preferred_element_type=jnp.float32)
    sub_outer = n_sub // sub_inner
    embed = reduce_scatter_2d(
        embed_part.reshape(sub_inner, sub_outer, own_rows, embed_part.shape[1]),
        "sub",
        (sub_inner, 1),
        (sub_outer, sub_inner),
        4,
    )
    norm = jnp.sqrt(jnp.sum(embed * embed, axis=-1, keepdims=True) + 1e-06)
    unit = embed / norm
    unit_b = unit.astype(jnp.bfloat16)
    flat_rows = partner_rows.reshape(peers * slots)
    selector = flat_rows[:, None] == jnp.arange(own_rows, dtype=jnp.int32)[None, :]
    mine = jnp.dot(
        selector.astype(jnp.bfloat16), unit_b, preferred_element_type=jnp.float32
    ).astype(jnp.bfloat16)
    outgoing = mine.reshape(peers, slots, mine.shape[1])
    incoming = exchange(outgoing, "mass", peers, 1)
    theirs = incoming.astype(jnp.float32)
    sim = jnp.sum(outgoing.astype(jnp.float32) * theirs, axis=-1)
    valid = jnp.arange(slots, dtype=jnp.int32)[None, :] < pair_counts.reshape(peers)[:, None]
    labels = pair_labels.reshape(peers, slots).astype(jnp.float32)
    coef = jnp.where(valid, 2.0 * (sim - labels), jnp.float32(0.0))
    weighted = (coef[..., None] * theirs).reshape(peers * slots, theirs.shape[2])
    grad_unit = lax.dot_general(
        selector.astype(jnp.float32),
        weighted,
        (((0,), (0,)), ((), ())),
        precision=lax.Precision.HIGHEST,
    )
    along = jnp.sum(unit * grad_unit, axis=-1, keepdims=True)
    grad_embed = ((grad_unit - unit * along) / norm).astype(jnp.bfloat16)
    grad_rows = all_gather(grad_embed, "sub", n_sub, sub_inner, 6)
    back = lax.dot_general(
        grad_rows, w_out, (((1,), (1,)), ((), ())), preferred_element_type=jnp.float32
    )
    gate = jax.nn.sigmoid(pre)
    grad_pre = lax.optimization_barrier(
        (back * gate * (1.0 + pre * (1.0 - gate))).astype(jnp.bfloat16)
    )
    out_part = lax.dot_general(
        grad_rows, hidden, (((0,), (0,)), ((), ())), preferred_element_type=jnp.float32
    )
    in_part_t = lax.dot_general(
        grad_pre, shard_rows, (((0,), (0,)), ((), ())), preferred_element_type=jnp.float32
    )
    n_mass = peers
    hid = in_part_t.shape[0]
    in_cols = in_part_t.shape[1] // n_mass
    out_rows = out_part.shape[0] // n_mass
    lanes = in_cols
    partial = jnp.concatenate(
        [
            jnp.swapaxes(in_part_t.astype(jnp.bfloat16).reshape(hid, n_mass, in_cols), 0, 1),
            out_part.astype(jnp.bfloat16).reshape(n_mass, out_rows * hid // lanes, lanes),
        ],
        axis=1,
    )
    mass_outer = n_mass // mass_inner
    summed = reduce_scatter_2d(
        partial.reshape((mass_outer, mass_inner) + partial.shape[1:]),
        "mass",
        (mass_outer, mass_inner),
        (mass_inner, 1),
        8,
    )
    grad_in = summed[:hid].T
    grad_out_t = summed[hid:].reshape(out_rows, hid)
    return (grad_in, grad_out_t)


def solution(mesh):
    placed = (
        P(("mass", "sub"), None),
        P(None, "sub"),
        P("sub", None),
        P("mass", "sub", None, None),
        P("mass", "sub", None),
        P("mass", "sub", None, None),
    )
    mass_inner = inner_size(list(mesh.devices[:, 0]))
    sub_inner = inner_size(list(mesh.devices[0, :]))
    return jax.shard_map(
        functools.partial(per_device, mesh.shape["sub"], mass_inner, sub_inner),
        mesh=mesh,
        in_specs=placed,
        out_specs=(P("mass", "sub"), P("mass", "sub")),
        check_vma=False,
    )
```

```python
import functools
import math

import jax
import jax.numpy as jnp
from jax import lax
from jax.experimental import pallas as pl
from jax.experimental.pallas import tpu as pltpu
from jax.sharding import PartitionSpec as P

MESH = pl.DeviceIdType.MESH


def _exchange_kernel(n, stride, axis, gather, x_ref, o_ref, got, send_sems, recv_sems):
    me = lax.axis_index(axis)
    mine = lax.rem(lax.div(me, stride), n)
    base = me - mine * stride

    def member(j):
        return base + j * stride

    barrier = pltpu.get_barrier_semaphore()
    for k in range(1, n):
        pl.semaphore_signal(
            barrier, inc=1, device_id={axis: member(lax.rem(mine + k, n))}, device_id_type=MESH
        )
    pl.semaphore_wait(barrier, n - 1)
    sends = []
    for k in range(1, n):
        peer = lax.rem(mine + k, n)
        copy = pltpu.make_async_remote_copy(
            src_ref=x_ref if gather else x_ref.at[peer],
            dst_ref=got.at[mine],
            send_sem=send_sems.at[k],
            recv_sem=recv_sems.at[k],
            device_id={axis: member(peer)},
            device_id_type=MESH,
        )
        copy.start()
        sends.append(copy)
    o_ref[mine] = x_ref[...] if gather else x_ref[mine]
    for k in range(1, n):
        sends[k - 1].wait_send()
        source = lax.rem(mine + n - k, n)
        pltpu.make_async_remote_copy(
            src_ref=x_ref if gather else x_ref.at[source],
            dst_ref=got.at[source],
            send_sem=send_sems.at[k],
            recv_sem=recv_sems.at[k],
            device_id={axis: member(source)},
            device_id_type=MESH,
        ).wait_recv()
        o_ref[source] = got[source]


def exchange(x, axis, n, collective_id, gather=False, stride=1):
    shape = (n,) + x.shape if gather else x.shape
    return pl.pallas_call(
        functools.partial(_exchange_kernel, n, stride, axis, gather),
        out_shape=jax.ShapeDtypeStruct(shape, x.dtype),
        in_specs=[pl.BlockSpec(memory_space=pltpu.VMEM)],
        out_specs=pl.BlockSpec(memory_space=pltpu.VMEM),
        scratch_shapes=[
            pltpu.VMEM(shape, x.dtype),
            pltpu.SemaphoreType.DMA((n,)),
            pltpu.SemaphoreType.DMA((n,)),
        ],
        compiler_params=pltpu.CompilerParams(
            collective_id=collective_id,
            has_side_effects=True,
            vmem_limit_bytes=min(3 * x.dtype.itemsize * math.prod(shape) + (8 << 20), 60 << 20),
        ),
    )(x)


def reduce_scatter(x, axis, inner, first_inner, first_id):
    outer = x.shape[0] // inner
    if first_inner:
        blocks = x.reshape((inner, outer) + x.shape[1:])
        phases = [(inner, 1), (outer, inner)]
    else:
        blocks = x.reshape((outer, inner) + x.shape[1:])
        phases = [(outer, inner), (inner, 1)]
    for number, (size, stride) in enumerate(phases):
        if size == 1:
            blocks = blocks[0].astype(jnp.float32)
            continue
        got = exchange(blocks.astype(x.dtype), axis, size, first_id + number, stride=stride)
        blocks = jnp.sum(got.astype(jnp.float32), axis=0)
    return blocks


def _gather_kernel(n_outer, n_inner, parts, axis, x_ref, o_ref, got, send_sems, recv_sems):
    me = lax.axis_index(axis)
    ci = lax.rem(me, n_inner)
    yo = lax.div(me, n_inner)
    rows = x_ref.shape[0] // parts

    def device(c, y):
        return {axis: y * n_inner + c}

    def slot(c, y, p):
        return (c * n_outer + y) * parts + p

    def piece(p):
        return pl.ds(p * rows, rows)

    outer_peers = [lax.rem(yo + k, n_outer) for k in range(1, n_outer)]
    inner_peers = [lax.rem(ci + j, n_inner) for j in range(1, n_inner)]
    barrier = pltpu.get_barrier_semaphore()
    for y in outer_peers:
        pl.semaphore_signal(barrier, inc=1, device_id=device(ci, y), device_id_type=MESH)
    for c in inner_peers:
        pl.semaphore_signal(barrier, inc=1, device_id=device(c, yo), device_id_type=MESH)
    pl.semaphore_wait(barrier, len(outer_peers) + len(inner_peers))

    sends = []

    def send(src, c, y, p, to):
        copy = pltpu.make_async_remote_copy(
            src_ref=src,
            dst_ref=got.at[c, y, piece(p)],
            send_sem=send_sems.at[len(sends)],
            recv_sem=recv_sems.at[slot(c, y, p)],
            device_id=to,
            device_id_type=MESH,
        )
        copy.start()
        sends.append(copy)

    def receive(c, y, p):
        pltpu.make_async_remote_copy(
            src_ref=x_ref.at[piece(p)],
            dst_ref=got.at[c, y, piece(p)],
            send_sem=send_sems.at[0],
            recv_sem=recv_sems.at[slot(c, y, p)],
            device_id=device(c, y),
            device_id_type=MESH,
        ).wait_recv()

    for p in range(parts):
        for y in outer_peers:
            send(x_ref.at[piece(p)], ci, yo, p, device(ci, y))
        for c in inner_peers:
            send(x_ref.at[piece(p)], ci, yo, p, device(c, yo))
    o_ref[ci, yo] = x_ref[...]
    for p in range(parts):
        for k in range(1, n_outer):
            y = lax.rem(yo + n_outer - k, n_outer)
            receive(ci, y, p)
            for c in inner_peers:
                send(got.at[ci, y, piece(p)], ci, y, p, device(c, yo))
            o_ref[ci, y, piece(p)] = got[ci, y, piece(p)]
    for j in range(1, n_inner):
        c = lax.rem(ci + n_inner - j, n_inner)
        for p in range(parts):
            for k in range(n_outer):
                y = lax.rem(yo + k, n_outer)
                receive(c, y, p)
                o_ref[c, y, piece(p)] = got[c, y, piece(p)]
    for copy in sends:
        copy.wait_send()


def all_gather(x, axis, n, inner, collective_id):
    outer = n // inner
    shape = (inner, outer) + x.shape
    parts = next(p for p in (2, 1) if x.shape[0] % (16 * p) == 0)
    got = pl.pallas_call(
        functools.partial(_gather_kernel, outer, inner, parts, axis),
        out_shape=jax.ShapeDtypeStruct(shape, x.dtype),
        in_specs=[pl.BlockSpec(memory_space=pltpu.VMEM)],
        out_specs=pl.BlockSpec(memory_space=pltpu.VMEM),
        scratch_shapes=[
            pltpu.VMEM(shape, x.dtype),
            pltpu.SemaphoreType.DMA((n * parts,)),
            pltpu.SemaphoreType.DMA((n * parts,)),
        ],
        compiler_params=pltpu.CompilerParams(
            collective_id=collective_id,
            has_side_effects=True,
            vmem_limit_bytes=min(3 * x.dtype.itemsize * math.prod(shape) + (8 << 20), 60 << 20),
        ),
    )(x)
    return got.reshape((n * x.shape[0],) + x.shape[1:])


def _reduce_kernel(n_o, s_o, n_i, s_i, chunks, halves, axis, p_ref, o_ref, g1, b_ref, g2, s1, r1, s2, r2):
    me = lax.axis_index(axis)
    zi = lax.rem(lax.div(me, s_i), n_i)
    xo = lax.rem(lax.div(me, s_o), n_o)
    zc = n_i // chunks
    rh = p_ref.shape[2] // halves

    def device(x, z):
        return {axis: me + (x - xo) * s_o + (z - zi) * s_i}

    def half(h):
        return pl.ds(h * rh, rh)

    barrier = pltpu.get_barrier_semaphore()
    for k in range(1, n_o):
        pl.semaphore_signal(
            barrier, inc=1, device_id=device(lax.rem(xo + k, n_o), zi), device_id_type=MESH
        )
    for k in range(1, n_i):
        pl.semaphore_signal(
            barrier, inc=1, device_id=device(xo, lax.rem(zi + k, n_i)), device_id_type=MESH
        )
    pl.semaphore_wait(barrier, n_o + n_i - 2)

    def along_x(k, c, h, to, dst_x):
        blocks = pl.ds(c * zc, zc)
        return pltpu.make_async_remote_copy(
            src_ref=p_ref.at[to, blocks, half(h)],
            dst_ref=g1.at[dst_x, blocks, half(h)],
            send_sem=s1.at[k, c * halves + h],
            recv_sem=r1.at[k, c * halves + h],
            device_id=device(to, zi),
            device_id_type=MESH,
        )

    def along_z(k, z, h):
        return pltpu.make_async_remote_copy(
            src_ref=b_ref.at[z, half(h)],
            dst_ref=g2.at[zi, half(h)],
            send_sem=s2.at[k, h],
            recv_sem=r2.at[k, h],
            device_id=device(xo, z),
            device_id_type=MESH,
        )

    first = []
    for c in range(chunks):
        for h in range(halves):
            for k in range(1, n_o):
                copy = along_x(k, c, h, lax.rem(xo + k, n_o), xo)
                copy.start()
                first.append(copy)
    sources = [lax.rem(xo + n_o - k, n_o) for k in range(1, n_o)]
    for c in range(chunks):
        for h in range(halves):
            for k in range(1, n_o):
                along_x(k, c, h, sources[k - 1], sources[k - 1]).wait_recv()
            for z in range(c * zc, (c + 1) * zc):
                total = p_ref[xo, z, half(h)].astype(jnp.float32)
                for src in sources:
                    total = total + g1[src, z, half(h)].astype(jnp.float32)
                b_ref[z, half(h)] = total.astype(b_ref.dtype)
                offset = lax.rem(z - zi + n_i, n_i)

                @pl.when(offset == 0)
                def _():
                    o_ref[half(h)] = total

                @pl.when(offset != 0)
                def _():
                    along_z(offset, z, h).start()

    for k in range(1, n_i):
        src = lax.rem(zi + n_i - k, n_i)
        for h in range(halves):
            pltpu.make_async_remote_copy(
                src_ref=b_ref.at[src, half(h)],
                dst_ref=g2.at[src, half(h)],
                send_sem=s2.at[k, h],
                recv_sem=r2.at[k, h],
                device_id=device(xo, src),
                device_id_type=MESH,
            ).wait_recv()
            o_ref[half(h)] = o_ref[half(h)] + g2[src, half(h)].astype(jnp.float32)
    for copy in first:
        copy.wait_send()
    for z in range(n_i):
        offset = lax.rem(z - zi + n_i, n_i)
        for h in range(halves):

            @pl.when(offset != 0)
            def _():
                along_z(offset, z, h).wait_send()


def reduce_scatter_2d(x, axis, first, second, collective_id):
    (n_o, s_o), (n_i, s_i) = first, second
    chunks = next(c for c in (8, 4, 2, 1) if n_i % c == 0)
    halves = 2 if x.shape[2] % 32 == 0 else 1
    return pl.pallas_call(
        functools.partial(_reduce_kernel, n_o, s_o, n_i, s_i, chunks, halves, axis),
        out_shape=jax.ShapeDtypeStruct(x.shape[2:], jnp.float32),
        in_specs=[pl.BlockSpec(memory_space=pltpu.VMEM)],
        out_specs=pl.BlockSpec(memory_space=pltpu.VMEM),
        scratch_shapes=[
            pltpu.VMEM(x.shape, x.dtype),
            pltpu.VMEM(x.shape[1:], x.dtype),
            pltpu.VMEM(x.shape[1:], x.dtype),
            pltpu.SemaphoreType.DMA((n_o, chunks * halves)),
            pltpu.SemaphoreType.DMA((n_o, chunks * halves)),
            pltpu.SemaphoreType.DMA((n_i, halves)),
            pltpu.SemaphoreType.DMA((n_i, halves)),
        ],
        compiler_params=pltpu.CompilerParams(
            collective_id=collective_id,
            has_side_effects=True,
            vmem_limit_bytes=min(4 * x.dtype.itemsize * x.size + (8 << 20), 60 << 20),
        ),
    )(x)


def inner_size(devices):
    coords = [tuple(getattr(d, "coords", ())) for d in devices]
    if len(coords) < 2 or not coords[0]:
        return len(coords)
    varying = [c for c in range(len(coords[0])) if len({p[c] for p in coords}) > 1]
    slow = [c for c in varying if coords[1][c] == coords[0][c]]
    if not slow:
        return 1
    run = 0
    while run < len(coords) and coords[run][slow[0]] == coords[0][slow[0]]:
        run += 1
    return run


def per_device(n_sub, mass_inner, sub_inner, spectra, w_in, w_out, partner_rows, pair_counts, pair_labels):
    own_rows = spectra.shape[0]
    peers = partner_rows.shape[2]
    slots = partner_rows.shape[3]
    shard_rows = all_gather(spectra, "sub", n_sub, sub_inner, 2)
    pre = jnp.dot(shard_rows, w_in, preferred_element_type=jnp.float32)
    hidden = jax.nn.silu(pre).astype(jnp.bfloat16)
    embed_part = jnp.dot(hidden, w_out, preferred_element_type=jnp.float32)
    sub_outer = n_sub // sub_inner
    embed = reduce_scatter_2d(
        embed_part.reshape(sub_inner, sub_outer, own_rows, embed_part.shape[1]),
        "sub",
        (sub_inner, 1),
        (sub_outer, sub_inner),
        4,
    )
    norm = jnp.sqrt(jnp.sum(embed * embed, axis=-1, keepdims=True) + 1e-06)
    unit = embed / norm
    unit_b = unit.astype(jnp.bfloat16)
    flat_rows = partner_rows.reshape(peers * slots)
    selector = flat_rows[:, None] == jnp.arange(own_rows, dtype=jnp.int32)[None, :]
    mine = jnp.dot(
        selector.astype(jnp.bfloat16), unit_b, preferred_element_type=jnp.float32
    ).astype(jnp.bfloat16)
    outgoing = mine.reshape(peers, slots, mine.shape[1])
    incoming = exchange(outgoing, "mass", peers, 1)
    theirs = incoming.astype(jnp.float32)
    sim = jnp.sum(outgoing.astype(jnp.float32) * theirs, axis=-1)
    valid = jnp.arange(slots, dtype=jnp.int32)[None, :] < pair_counts.reshape(peers)[:, None]
    labels = pair_labels.reshape(peers, slots).astype(jnp.float32)
    coef = jnp.where(valid, 2.0 * (sim - labels), jnp.float32(0.0))
    weighted = (coef[..., None] * theirs).reshape(peers * slots, theirs.shape[2])
    grad_unit = lax.dot_general(
        selector.astype(jnp.float32),
        weighted,
        (((0,), (0,)), ((), ())),
        precision=lax.Precision.HIGHEST,
    )
    along = jnp.sum(unit * grad_unit, axis=-1, keepdims=True)
    grad_embed = ((grad_unit - unit * along) / norm).astype(jnp.bfloat16)
    grad_rows = all_gather(grad_embed, "sub", n_sub, sub_inner, 6)
    back = lax.dot_general(
        grad_rows, w_out, (((1,), (1,)), ((), ())), preferred_element_type=jnp.float32
    )
    gate = jax.nn.sigmoid(pre)
    grad_pre = lax.optimization_barrier(
        (back * gate * (1.0 + pre * (1.0 - gate))).astype(jnp.bfloat16)
    )
    out_part = lax.dot_general(
        grad_rows, hidden, (((0,), (0,)), ((), ())), preferred_element_type=jnp.float32
    )
    in_part_t = lax.dot_general(
        grad_pre, shard_rows, (((0,), (0,)), ((), ())), preferred_element_type=jnp.float32
    )
    n_mass = peers
    hid = in_part_t.shape[0]
    in_cols = in_part_t.shape[1] // n_mass
    out_rows = out_part.shape[0] // n_mass
    lanes = in_cols
    partial = jnp.concatenate(
        [
            jnp.swapaxes(in_part_t.astype(jnp.bfloat16).reshape(hid, n_mass, in_cols), 0, 1),
            out_part.astype(jnp.bfloat16).reshape(n_mass, out_rows * hid // lanes, lanes),
        ],
        axis=1,
    )
    mass_outer = n_mass // mass_inner
    summed = reduce_scatter_2d(
        partial.reshape((mass_outer, mass_inner) + partial.shape[1:]),
        "mass",
        (mass_outer, mass_inner),
        (mass_inner, 1),
        8,
    )
    grad_in = summed[:hid].T
    grad_out_t = summed[hid:].reshape(out_rows, hid)
    return (grad_in, grad_out_t)


def solution(mesh):
    placed = (
        P(("mass", "sub"), None),
        P(None, "sub"),
        P("sub", None),
        P("mass", "sub", None, None),
        P("mass", "sub", None),
        P("mass", "sub", None, None),
    )
    mass_inner = inner_size(list(mesh.devices[:, 0]))
    sub_inner = inner_size(list(mesh.devices[0, :]))
    return jax.shard_map(
        functools.partial(per_device, mesh.shape["sub"], mass_inner, sub_inner),
        mesh=mesh,
        in_specs=placed,
        out_specs=(P("mass", "sub"), P("mass", "sub")),
        check_vma=False,
    )
```
